256 devices in a mesh: row: 32 (over y, z), col: 8 (over x, core).
Axes of the slice: x: 4, y: 4, z: 8, core: 2. Of those that a mesh axis runs over, the one named last changes fastest.
Arguments:
- embedding: bfloat16 [8, 32, 48, 256], P('col', 'row'), may hold values from -0.3984375 to 0.3984375
- preference: float32 [12288], P('row'), may hold values from -2.5 to -0.5
Outputs:
- responsibility: float32 [12288, 12288], P('row', 'col')
- availability: float32 [12288, 12288], P('row', 'col')
The draws below stay inside these ranges and needn't reach their ends.
All inputs are finite; a program needn't handle non-finite values.
Results may differ from the reference program's by a relative error of at most 0.0003.
Values may be sent and summed in bfloat16 or wider, within the bound.
A program may use at most 64 MiB of HBM per device.

```python
import jax
import jax.numpy as jnp
from jax import lax

E = 256
MOL_DEV = 48
ITERS = 2
N = 12288
N_ROW = 32
N_COL = 8


def block_levels(key, extent, shards, smallest, top_value):
    gain, own = 1.0, jax.random.fold_in(key, 6)
    for dim, shards_of in shards:
        steps = jnp.exp(jax.random.uniform(jax.random.fold_in(own, dim), (shards_of,), jnp.float32, smallest / len(shards), top_value / len(shards)))
        gain = gain * jnp.repeat(steps, extent[dim] // shards_of).reshape([-1 if axis == dim else 1 for axis in range(len(extent))])
    return gain


def noise(key, dims, scale, reach, cuts=(), kind=jnp.bfloat16):
    gain = block_levels(key, dims, cuts, -0.22, 0.18) if cuts else 1.0
    values = jax.random.normal(key, dims, jnp.float32) * scale * gain
    return jnp.minimum(jnp.maximum(values, -reach), reach).astype(kind)


def setup_inputs(seed: int = 0) -> dict:
    keys = jax.random.split(jax.random.key(seed), 3)
    embedding = noise(keys[0], (N_COL, N_ROW, MOL_DEV, E), 0.0625, 0.3984375, ((0, 8), (1, 32)))
    preference = jnp.clip(-2.5 + 2.0 * jax.random.uniform(keys[1], (N,), jnp.float32) ** block_levels(keys[1], (N,), ((0, 32),), -0.2, 0.2), -2.5, -0.5)
    return dict(embedding=embedding, preference=preference)


DAMPING = 0.5


def similarity(row_emb, col_emb, row_start, col_start, pref_rows):
    cross = lax.dot_general(row_emb, col_emb, (((1,), (1,)), ((), ())), preferred_element_type=jnp.float32)
    row_vals = row_emb.astype(jnp.float32)
    col_vals = col_emb.astype(jnp.float32)
    row_sq = jnp.sum(row_vals * row_vals, axis=1)
    col_sq = jnp.sum(col_vals * col_vals, axis=1)
    dist = (2.0 * cross - row_sq[:, None]) - col_sq[None, :]
    row_ids = row_start + jnp.arange(row_emb.shape[0], dtype=jnp.int32)
    col_ids = col_start + jnp.arange(col_emb.shape[0], dtype=jnp.int32)
    diagonal = row_ids[:, None] == col_ids[None, :]
    return jnp.where(diagonal, pref_rows[:, None], dist), diagonal


def top_two(summed):
    first = jnp.max(summed, axis=1)
    hits = summed == first[:, None]
    repeats = jnp.sum(hits.astype(jnp.int32), axis=1)
    others = jnp.max(jnp.where(hits, -jnp.inf, summed), axis=1)
    second = jnp.where(repeats > 1, first, others)
    return first, second


def row_update(sim, avail, resp, first, second):
    summed = avail + sim
    fresh = sim - jnp.where(summed == first[:, None], second[:, None], first[:, None])
    return DAMPING * resp + (1.0 - DAMPING) * fresh


def reference(embedding, preference):
    width = embedding.shape[3]
    flat = embedding.reshape(-1, width)
    total = flat.shape[0]
    block = MOL_DEV * N_COL
    groups = total // block
    row_groups = flat.reshape(groups, block, width)
    pref_groups = preference.reshape(groups, block)
    starts = jnp.arange(groups, dtype=jnp.int32) * block

    def build(items):
        rows, prefs, start = items
        sim_rows, unused = similarity(rows, flat, start, jnp.int32(0), prefs)
        return sim_rows

    sim = lax.map(build, (row_groups, pref_groups, starts))
    ids = jnp.arange(total, dtype=jnp.int32)
    diagonal = ids[:, None] == ids[None, :]
    resp = jnp.zeros((groups, block, total), jnp.float32)
    avail = jnp.zeros((groups, block, total), jnp.float32)

    def update(items):
        sim_rows, avail_rows, resp_rows = items
        first, second = top_two(avail_rows + sim_rows)
        return row_update(sim_rows, avail_rows, resp_rows, first, second)

    for step in range(ITERS):
        resp = lax.map(update, (sim, avail, resp))
        whole = resp.reshape(total, total)
        positive = jnp.where(diagonal, whole, jnp.maximum(whole, 0.0))
        colsum = jnp.sum(positive, axis=0)
        renew = colsum[None, :] - positive
        renew = jnp.where(diagonal, renew, jnp.minimum(renew, 0.0))
        avail = (DAMPING * avail.reshape(total, total) + (1.0 - DAMPING) * renew).reshape(groups, block, total)
    return resp.reshape(total, total), avail.reshape(total, total)
```

```python
import functools

import jax
import jax.numpy as jnp
from jax import lax
from jax.experimental import pallas as pl
from jax.experimental.pallas import tpu as pltpu
from jax.sharding import PartitionSpec as P

ITERS = 2


DAMPING = 0.5

MESH = pl.DeviceIdType.MESH
VMEM = pl.BlockSpec(memory_space=pltpu.VMEM)


def params(cid):
    return pltpu.CompilerParams(collective_id=cid, has_side_effects=True)


def embed_kernel(n_row, n_col, chunk_ref, colb_ref, rowb_ref, send_c, send_r, recv_c, recv_r):
    r = lax.axis_index("row")
    c = lax.axis_index("col")
    g = c * n_row + r
    target_row = g // n_col
    my_slot = g % n_col
    peers = [(lax.rem(r + d, n_row), c) for d in range(1, n_row)]
    targets = [(target_row, j) for j in range(n_col)]
    sources = []
    for s in range(n_col):
        gs = r * n_col + s
        sources.append((gs % n_row, gs // n_row))

    def differs(dev):
        return jnp.logical_or(dev[0] != r, dev[1] != c)

    barrier = pltpu.get_barrier_semaphore()
    for dev in peers:
        pl.semaphore_signal(barrier, inc=1, device_id=dev, device_id_type=MESH)
    for dev in targets + sources:
        @pl.when(differs(dev))
        def _():
            pl.semaphore_signal(barrier, inc=1, device_id=dev, device_id_type=MESH)
    self_in = (target_row == r).astype(jnp.int32)
    pl.semaphore_wait(barrier, (n_row - 1) + 2 * (n_col - self_in))

    local_c = pltpu.make_async_copy(chunk_ref, colb_ref.at[r], recv_c.at[r])
    local_c.start()
    copies = []
    for i, dev in enumerate(peers):
        cp = pltpu.make_async_remote_copy(
            src_ref=chunk_ref, dst_ref=colb_ref.at[r], send_sem=send_c.at[i],
            recv_sem=recv_c.at[r], device_id=dev, device_id_type=MESH)
        cp.start()
        copies.append(cp)
    row_copies = []
    for j, dev in enumerate(targets):
        cp = pltpu.make_async_remote_copy(
            src_ref=chunk_ref, dst_ref=rowb_ref.at[my_slot], send_sem=send_r.at[j],
            recv_sem=recv_r.at[my_slot], device_id=dev, device_id_type=MESH)
        row_copies.append(cp)

        @pl.when(differs(dev))
        def _():
            cp.start()

        @pl.when(jnp.logical_not(differs(dev)))
        def _():
            pltpu.make_async_copy(chunk_ref, rowb_ref.at[my_slot], recv_r.at[my_slot]).start()

    for cp in copies:
        cp.wait_send()
    for j, dev in enumerate(targets):
        @pl.when(differs(dev))
        def _():
            row_copies[j].wait_send()
    for s in range(n_row):
        pltpu.make_async_copy(chunk_ref, colb_ref.at[s], recv_c.at[s]).wait()
    for s in range(n_col):
        pltpu.make_async_copy(chunk_ref, rowb_ref.at[s], recv_r.at[s]).wait()


def distribute(chunk, n_row, n_col):
    mol, width = chunk.shape
    return pl.pallas_call(
        functools.partial(embed_kernel, n_row, n_col),
        out_shape=(jax.ShapeDtypeStruct((n_row, mol, width), chunk.dtype),
                   jax.ShapeDtypeStruct((n_col, mol, width), chunk.dtype)),
        in_specs=[VMEM],
        out_specs=(VMEM, VMEM),
        scratch_shapes=[
            pltpu.SemaphoreType.DMA((n_row - 1,)),
            pltpu.SemaphoreType.DMA((n_col,)),
            pltpu.SemaphoreType.DMA((n_row,)),
            pltpu.SemaphoreType.DMA((n_col,)),
        ],
        compiler_params=params(0),
    )(chunk)


def gather_kernel(axis, n, src_ref, out_ref, send_sem, recv_sem):
    me = lax.axis_index(axis)
    peers = [lax.rem(me + d, n) for d in range(1, n)]
    barrier = pltpu.get_barrier_semaphore()
    for p in peers:
        pl.semaphore_signal(barrier, inc=1, device_id={axis: p}, device_id_type=MESH)
    pl.semaphore_wait(barrier, n - 1)
    pltpu.make_async_copy(src_ref, out_ref.at[me], recv_sem.at[me]).start()
    copies = []
    for i, p in enumerate(peers):
        cp = pltpu.make_async_remote_copy(
            src_ref=src_ref, dst_ref=out_ref.at[me], send_sem=send_sem.at[i],
            recv_sem=recv_sem.at[me], device_id={axis: p}, device_id_type=MESH)
        cp.start()
        copies.append(cp)
    for cp in copies:
        cp.wait_send()
    for s in range(n):
        pltpu.make_async_copy(src_ref, out_ref.at[s], recv_sem.at[s]).wait()


def gather(x, axis, n, cid):
    return pl.pallas_call(
        functools.partial(gather_kernel, axis, n),
        out_shape=jax.ShapeDtypeStruct((n,) + x.shape, x.dtype),
        in_specs=[VMEM],
        out_specs=VMEM,
        scratch_shapes=[
            pltpu.SemaphoreType.DMA((n - 1,)),
            pltpu.SemaphoreType.DMA((n,)),
        ],
        compiler_params=params(cid),
    )(x)


def similarity(row_emb, col_emb, row_start, col_start, pref_rows):
    cross = lax.dot_general(
        row_emb, col_emb, (((1,), (1,)), ((), ())), preferred_element_type=jnp.float32
    )
    row_vals = row_emb.astype(jnp.float32)
    col_vals = col_emb.astype(jnp.float32)
    row_sq = jnp.sum(row_vals * row_vals, axis=1)
    col_sq = jnp.sum(col_vals * col_vals, axis=1)
    dist = 2.0 * cross - row_sq[:, None] - col_sq[None, :]
    row_ids = row_start + jnp.arange(row_emb.shape[0], dtype=jnp.int32)
    col_ids = col_start + jnp.arange(col_emb.shape[0], dtype=jnp.int32)
    diagonal = row_ids[:, None] == col_ids[None, :]
    return (jnp.where(diagonal, pref_rows[:, None], dist), diagonal)


def top_two(summed):
    first = jnp.max(summed, axis=1)
    hits = summed == first[:, None]
    repeats = jnp.sum(hits.astype(jnp.int32), axis=1)
    others = jnp.max(jnp.where(hits, -jnp.inf, summed), axis=1)
    second = jnp.where(repeats > 1, first, others)
    return (first, second)


def local(embedding, preference):
    rows_n = lax.axis_size("row")
    cols_n = lax.axis_size("col")
    row_idx = lax.axis_index("row")
    col_idx = lax.axis_index("col")
    mol = embedding.shape[2]
    width = embedding.shape[3]
    row_count = mol * cols_n
    col_count = mol * rows_n
    colb, rowb = distribute(embedding.reshape(mol, width), rows_n, cols_n)
    column_block = colb.reshape(col_count, width)
    row_block = rowb.reshape(row_count, width)
    row_start = row_idx * row_count
    col_start = col_idx * col_count
    sim, diagonal = similarity(row_block, column_block, row_start, col_start, preference)
    resp = jnp.zeros_like(sim)
    avail = jnp.zeros_like(sim)
    for step in range(ITERS):
        summed = avail + sim
        local_first, local_second = top_two(summed)
        both = gather(jnp.stack([local_first, local_second]), "col", cols_n, 1 + 2 * step)
        firsts = both[:, 0, :]
        seconds = both[:, 1, :]
        first = jnp.max(firsts, axis=0)
        at_top = firsts == first[None, :]
        repeats = jnp.sum(at_top.astype(jnp.int32), axis=0)
        others = jnp.max(jnp.where(at_top, -jnp.inf, firsts), axis=0)
        second = jnp.where(repeats > 1, first, jnp.maximum(jnp.max(seconds, axis=0), others))
        fresh = sim - jnp.where(summed == first[:, None], second[:, None], first[:, None])
        resp = DAMPING * resp + (1.0 - DAMPING) * fresh
        positive = jnp.where(diagonal, resp, jnp.maximum(resp, 0.0))
        partial = jnp.sum(positive, axis=0)
        colsum = jnp.sum(gather(partial[None, :], "row", rows_n, 2 + 2 * step), axis=(0, 1))
        renew = colsum[None, :] - positive
        renew = jnp.where(diagonal, renew, jnp.minimum(renew, 0.0))
        avail = DAMPING * avail + (1.0 - DAMPING) * renew
    return (resp, avail)


def solution(mesh):
    placed = (P("col", "row", None, None), P("row"))
    return jax.shard_map(
        local,
        mesh=mesh,
        in_specs=placed,
        out_specs=(P("row", "col"), P("row", "col")),
        check_vma=False,
    )
```

```python
import functools

import jax
import jax.numpy as jnp
from jax import lax
from jax.experimental import pallas as pl
from jax.experimental.pallas import tpu as pltpu
from jax.sharding import PartitionSpec as P

ITERS = 2


DAMPING = 0.5

INNER = 8

MESH = pl.DeviceIdType.MESH
VMEM = pl.BlockSpec(memory_space=pltpu.VMEM)


def params(cid):
    return pltpu.CompilerParams(collective_id=cid, has_side_effects=True)


def embed_kernel(n_row, n_col, inner, chunk_ref, colb_ref, rowb_ref, send_z, send_y, send_r, recv_c, recv_b, recv_r):
    r = lax.axis_index("row")
    c = lax.axis_index("col")
    outer = n_row // inner
    y = r // inner
    z = r % inner
    g = c * n_row + r
    target_row = g // n_col
    my_slot = g % n_col
    zpeers = [(y * inner + lax.rem(z + d, inner), c) for d in range(1, inner)]
    ypeers = [(lax.rem(y + d, outer) * inner + z, c) for d in range(1, outer)]
    targets = [(target_row, j) for j in range(n_col)]
    sources = []
    for s in range(n_col):
        gs = r * n_col + s
        sources.append((gs % n_row, gs // n_row))

    def differs(dev):
        return jnp.logical_or(dev[0] != r, dev[1] != c)

    barrier = pltpu.get_barrier_semaphore()
    for dev in zpeers + ypeers:
        pl.semaphore_signal(barrier, inc=1, device_id=dev, device_id_type=MESH)
    for dev in targets + sources:
        @pl.when(differs(dev))
        def _():
            pl.semaphore_signal(barrier, inc=1, device_id=dev, device_id_type=MESH)
    self_in = (target_row == r).astype(jnp.int32)
    pl.semaphore_wait(barrier, (inner - 1) + (outer - 1) + 2 * (n_col - self_in))

    pltpu.make_async_copy(chunk_ref, colb_ref.at[r], recv_c.at[z]).start()
    zcopies = []
    for i, dev in enumerate(zpeers):
        cp = pltpu.make_async_remote_copy(
            src_ref=chunk_ref, dst_ref=colb_ref.at[r], send_sem=send_z.at[i],
            recv_sem=recv_c.at[z], device_id=dev, device_id_type=MESH)
        cp.start()
        zcopies.append(cp)
    row_copies = []
    for j, dev in enumerate(targets):
        cp = pltpu.make_async_remote_copy(
            src_ref=chunk_ref, dst_ref=rowb_ref.at[my_slot], send_sem=send_r.at[j],
            recv_sem=recv_r.at[my_slot], device_id=dev, device_id_type=MESH)
        row_copies.append(cp)

        @pl.when(differs(dev))
        def _():
            cp.start()

        @pl.when(jnp.logical_not(differs(dev)))
        def _():
            pltpu.make_async_copy(chunk_ref, rowb_ref.at[my_slot], recv_r.at[my_slot]).start()

    for s in range(inner):
        pltpu.make_async_copy(chunk_ref, colb_ref.at[y * inner + s], recv_c.at[s]).wait()
    block = colb_ref.at[pl.ds(y * inner, inner)]
    ycopies = []
    for i, dev in enumerate(ypeers):
        cp = pltpu.make_async_remote_copy(
            src_ref=block, dst_ref=block, send_sem=send_y.at[i],
            recv_sem=recv_b.at[y], device_id=dev, device_id_type=MESH)
        cp.start()
        ycopies.append(cp)

    for cp in zcopies + ycopies:
        cp.wait_send()
    for j, dev in enumerate(targets):
        @pl.when(differs(dev))
        def _():
            row_copies[j].wait_send()
    for d in range(1, outer):
        yo = lax.rem(y + d, outer)
        other = colb_ref.at[pl.ds(yo * inner, inner)]
        pltpu.make_async_copy(other, other, recv_b.at[yo]).wait()
    for s in range(n_col):
        pltpu.make_async_copy(chunk_ref, rowb_ref.at[s], recv_r.at[s]).wait()


def distribute(chunk, n_row, n_col, inner):
    mol, width = chunk.shape
    outer = n_row // inner
    return pl.pallas_call(
        functools.partial(embed_kernel, n_row, n_col, inner),
        out_shape=(jax.ShapeDtypeStruct((n_row, mol, width), chunk.dtype),
                   jax.ShapeDtypeStruct((n_col, mol, width), chunk.dtype)),
        in_specs=[VMEM],
        out_specs=(VMEM, VMEM),
        scratch_shapes=[
            pltpu.SemaphoreType.DMA((inner - 1,)),
            pltpu.SemaphoreType.DMA((outer - 1,)),
            pltpu.SemaphoreType.DMA((n_col,)),
            pltpu.SemaphoreType.DMA((inner,)),
            pltpu.SemaphoreType.DMA((outer,)),
            pltpu.SemaphoreType.DMA((n_col,)),
        ],
        compiler_params=params(0),
    )(chunk)


def colsum_kernel(n, inner, part_ref, out_ref, buf1, zsum, buf2, send_z, send_y, recv_z, recv_y):
    r = lax.axis_index("row")
    outer = n // inner
    y = r // inner
    z = r % inner
    zpeers = [y * inner + lax.rem(z + d, inner) for d in range(1, inner)]
    ypeers = [lax.rem(y + d, outer) * inner + z for d in range(1, outer)]
    barrier = pltpu.get_barrier_semaphore()
    for p in zpeers + ypeers:
        pl.semaphore_signal(barrier, inc=1, device_id={"row": p}, device_id_type=MESH)
    pl.semaphore_wait(barrier, (inner - 1) + (outer - 1))
    pltpu.make_async_copy(part_ref, buf1.at[pl.ds(z, 1)], recv_z.at[z]).start()
    zcopies = []
    for i, p in enumerate(zpeers):
        cp = pltpu.make_async_remote_copy(
            src_ref=part_ref, dst_ref=buf1.at[pl.ds(z, 1)], send_sem=send_z.at[i],
            recv_sem=recv_z.at[z], device_id={"row": p}, device_id_type=MESH)
        cp.start()
        zcopies.append(cp)
    for s in range(inner):
        pltpu.make_async_copy(part_ref, buf1.at[pl.ds(s, 1)], recv_z.at[s]).wait()
    zsum[...] = jnp.sum(buf1[...], axis=0, keepdims=True)
    pltpu.make_async_copy(zsum, buf2.at[pl.ds(y, 1)], recv_y.at[y]).start()
    ycopies = []
    for i, p in enumerate(ypeers):
        cp = pltpu.make_async_remote_copy(
            src_ref=zsum, dst_ref=buf2.at[pl.ds(y, 1)], send_sem=send_y.at[i],
            recv_sem=recv_y.at[y], device_id={"row": p}, device_id_type=MESH)
        cp.start()
        ycopies.append(cp)
    for cp in zcopies + ycopies:
        cp.wait_send()
    for s in range(outer):
        pltpu.make_async_copy(zsum, buf2.at[pl.ds(s, 1)], recv_y.at[s]).wait()
    out_ref[...] = jnp.sum(buf2[...], axis=0, keepdims=True)


def row_sum(part, n, inner, cid):
    outer = n // inner
    width = part.shape[1]
    return pl.pallas_call(
        functools.partial(colsum_kernel, n, inner),
        out_shape=jax.ShapeDtypeStruct((1, width), part.dtype),
        in_specs=[VMEM],
        out_specs=VMEM,
        scratch_shapes=[
            pltpu.VMEM((inner, width), part.dtype),
            pltpu.VMEM((1, width), part.dtype),
            pltpu.VMEM((outer, width), part.dtype),
            pltpu.SemaphoreType.DMA((inner - 1,)),
            pltpu.SemaphoreType.DMA((outer - 1,)),
            pltpu.SemaphoreType.DMA((inner,)),
            pltpu.SemaphoreType.DMA((outer,)),
        ],
        compiler_params=params(cid),
    )(part)


def gather_kernel(axis, n, src_ref, out_ref, send_sem, recv_sem):
    me = lax.axis_index(axis)
    peers = [lax.rem(me + d, n) for d in range(1, n)]
    barrier = pltpu.get_barrier_semaphore()
    for p in peers:
        pl.semaphore_signal(barrier, inc=1, device_id={axis: p}, device_id_type=MESH)
    pl.semaphore_wait(barrier, n - 1)
    pltpu.make_async_copy(src_ref, out_ref.at[me], recv_sem.at[me]).start()
    copies = []
    for i, p in enumerate(peers):
        cp = pltpu.make_async_remote_copy(
            src_ref=src_ref, dst_ref=out_ref.at[me], send_sem=send_sem.at[i],
            recv_sem=recv_sem.at[me], device_id={axis: p}, device_id_type=MESH)
        cp.start()
        copies.append(cp)
    for cp in copies:
        cp.wait_send()
    for s in range(n):
        pltpu.make_async_copy(src_ref, out_ref.at[s], recv_sem.at[s]).wait()


def gather(x, axis, n, cid):
    return pl.pallas_call(
        functools.partial(gather_kernel, axis, n),
        out_shape=jax.ShapeDtypeStruct((n,) + x.shape, x.dtype),
        in_specs=[VMEM],
        out_specs=VMEM,
        scratch_shapes=[
            pltpu.SemaphoreType.DMA((n - 1,)),
            pltpu.SemaphoreType.DMA((n,)),
        ],
        compiler_params=params(cid),
    )(x)


def similarity(row_emb, col_emb, row_start, col_start, pref_rows):
    cross = lax.dot_general(
        row_emb, col_emb, (((1,), (1,)), ((), ())), preferred_element_type=jnp.float32
    )
    row_vals = row_emb.astype(jnp.float32)
    col_vals = col_emb.astype(jnp.float32)
    row_sq = jnp.sum(row_vals * row_vals, axis=1)
    col_sq = jnp.sum(col_vals * col_vals, axis=1)
    dist = 2.0 * cross - row_sq[:, None] - col_sq[None, :]
    row_ids = row_start + jnp.arange(row_emb.shape[0], dtype=jnp.int32)
    col_ids = col_start + jnp.arange(col_emb.shape[0], dtype=jnp.int32)
    diagonal = row_ids[:, None] == col_ids[None, :]
    return (jnp.where(diagonal, pref_rows[:, None], dist), diagonal)


def top_two(summed):
    first = jnp.max(summed, axis=1)
    hits = summed == first[:, None]
    repeats = jnp.sum(hits.astype(jnp.int32), axis=1)
    others = jnp.max(jnp.where(hits, -jnp.inf, summed), axis=1)
    second = jnp.where(repeats > 1, first, others)
    return (first, second)


def local(embedding, preference):
    rows_n = lax.axis_size("row")
    cols_n = lax.axis_size("col")
    row_idx = lax.axis_index("row")
    col_idx = lax.axis_index("col")
    mol = embedding.shape[2]
    width = embedding.shape[3]
    row_count = mol * cols_n
    col_count = mol * rows_n
    colb, rowb = distribute(embedding.reshape(mol, width), rows_n, cols_n, INNER)
    column_block = colb.reshape(col_count, width)
    row_block = rowb.reshape(row_count, width)
    row_start = row_idx * row_count
    col_start = col_idx * col_count
    sim, diagonal = similarity(row_block, column_block, row_start, col_start, preference)
    resp = jnp.zeros_like(sim)
    avail = jnp.zeros_like(sim)
    for step in range(ITERS):
        summed = avail + sim
        local_first, local_second = top_two(summed)
        both = gather(jnp.stack([local_first, local_second]), "col", cols_n, 1 + 2 * step)
        firsts = both[:, 0, :]
        seconds = both[:, 1, :]
        first = jnp.max(firsts, axis=0)
        at_top = firsts == first[None, :]
        repeats = jnp.sum(at_top.astype(jnp.int32), axis=0)
        others = jnp.max(jnp.where(at_top, -jnp.inf, firsts), axis=0)
        second = jnp.where(repeats > 1, first, jnp.maximum(jnp.max(seconds, axis=0), others))
        fresh = sim - jnp.where(summed == first[:, None], second[:, None], first[:, None])
        resp = DAMPING * resp + (1.0 - DAMPING) * fresh
        positive = jnp.where(diagonal, resp, jnp.maximum(resp, 0.0))
        partial = jnp.sum(positive, axis=0)
        colsum = row_sum(partial[None, :], rows_n, INNER, 2 + 2 * step)[0]
        renew = colsum[None, :] - positive
        renew = jnp.where(diagonal, renew, jnp.minimum(renew, 0.0))
        avail = DAMPING * avail + (1.0 - DAMPING) * renew
    return (resp, avail)


def solution(mesh):
    placed = (P("col", "row", None, None), P("row"))
    return jax.shard_map(
        local,
        mesh=mesh,
        in_specs=placed,
        out_specs=(P("row", "col"), P("row", "col")),
        check_vma=False,
    )
```

```python
import functools

import jax
import jax.numpy as jnp
from jax import lax
from jax.experimental import pallas as pl
from jax.experimental.pallas import tpu as pltpu
from jax.sharding import PartitionSpec as P

ITERS = 2


DAMPING = 0.5

INNER = 8

MESH = pl.DeviceIdType.MESH
VMEM = pl.BlockSpec(memory_space=pltpu.VMEM)


def params(cid):
    return pltpu.CompilerParams(collective_id=cid, has_side_effects=True)


def embed_kernel(n_row, n_col, inner, chunk_ref, colb_ref, rowb_ref, send_z, send_y, send_r, recv_c, recv_b, recv_r):
    r = lax.axis_index("row")
    c = lax.axis_index("col")
    outer = n_row // inner
    y = r // inner
    z = r % inner
    g = c * n_row + r
    target_row = g // n_col
    my_slot = g % n_col
    zpeers = [(y * inner + lax.rem(z + d, inner), c) for d in range(1, inner)]
    ypeers = [(lax.rem(y + d, outer) * inner + z, c) for d in range(1, outer)]
    targets = [(target_row, j) for j in range(n_col)]
    sources = []
    for s in range(n_col):
        gs = r * n_col + s
        sources.append((gs % n_row, gs // n_row))

    def differs(dev):
        return jnp.logical_or(dev[0] != r, dev[1] != c)

    barrier = pltpu.get_barrier_semaphore()
    for dev in zpeers + ypeers:
        pl.semaphore_signal(barrier, inc=1, device_id=dev, device_id_type=MESH)
    for dev in targets + sources:
        @pl.when(differs(dev))
        def _():
            pl.semaphore_signal(barrier, inc=1, device_id=dev, device_id_type=MESH)
    self_in = (target_row == r).astype(jnp.int32)
    pl.semaphore_wait(barrier, (inner - 1) + (outer - 1) + 2 * (n_col - self_in))

    pltpu.make_async_copy(chunk_ref, colb_ref.at[r], recv_c.at[z]).start()
    zcopies = []
    for i, dev in enumerate(zpeers):
        cp = pltpu.make_async_remote_copy(
            src_ref=chunk_ref, dst_ref=colb_ref.at[r], send_sem=send_z.at[i],
            recv_sem=recv_c.at[z], device_id=dev, device_id_type=MESH)
        cp.start()
        zcopies.append(cp)
    row_copies = []
    for j, dev in enumerate(targets):
        cp = pltpu.make_async_remote_copy(
            src_ref=chunk_ref, dst_ref=rowb_ref.at[my_slot], send_sem=send_r.at[j],
            recv_sem=recv_r.at[my_slot], device_id=dev, device_id_type=MESH)
        row_copies.append(cp)

        @pl.when(differs(dev))
        def _():
            cp.start()

        @pl.when(jnp.logical_not(differs(dev)))
        def _():
            pltpu.make_async_copy(chunk_ref, rowb_ref.at[my_slot], recv_r.at[my_slot]).start()

    for s in range(inner):
        pltpu.make_async_copy(chunk_ref, colb_ref.at[y * inner + s], recv_c.at[s]).wait()
    block = colb_ref.at[pl.ds(y * inner, inner)]
    ycopies = []
    for i, dev in enumerate(ypeers):
        cp = pltpu.make_async_remote_copy(
            src_ref=block, dst_ref=block, send_sem=send_y.at[i],
            recv_sem=recv_b.at[y], device_id=dev, device_id_type=MESH)
        cp.start()
        ycopies.append(cp)

    for cp in zcopies + ycopies:
        cp.wait_send()
    for j, dev in enumerate(targets):
        @pl.when(differs(dev))
        def _():
            row_copies[j].wait_send()
    for d in range(1, outer):
        yo = lax.rem(y + d, outer)
        other = colb_ref.at[pl.ds(yo * inner, inner)]
        pltpu.make_async_copy(other, other, recv_b.at[yo]).wait()
    for s in range(n_col):
        pltpu.make_async_copy(chunk_ref, rowb_ref.at[s], recv_r.at[s]).wait()


def distribute(chunk, n_row, n_col, inner):
    mol, width = chunk.shape
    outer = n_row // inner
    return pl.pallas_call(
        functools.partial(embed_kernel, n_row, n_col, inner),
        out_shape=(jax.ShapeDtypeStruct((n_row, mol, width), chunk.dtype),
                   jax.ShapeDtypeStruct((n_col, mol, width), chunk.dtype)),
        in_specs=[VMEM],
        out_specs=(VMEM, VMEM),
        scratch_shapes=[
            pltpu.SemaphoreType.DMA((inner - 1,)),
            pltpu.SemaphoreType.DMA((outer - 1,)),
            pltpu.SemaphoreType.DMA((n_col,)),
            pltpu.SemaphoreType.DMA((inner,)),
            pltpu.SemaphoreType.DMA((outer,)),
            pltpu.SemaphoreType.DMA((n_col,)),
        ],
        compiler_params=params(0),
    )(chunk)


def colsum_kernel(n, inner, part_ref, out_ref, buf1, zsum, buf2, send_z, send_y, recv_z, recv_y):
    r = lax.axis_index("row")
    outer = n // inner
    y = r // inner
    z = r % inner
    zpeers = [y * inner + lax.rem(z + d, inner) for d in range(1, inner)]
    ypeers = [lax.rem(y + d, outer) * inner + z for d in range(1, outer)]
    barrier = pltpu.get_barrier_semaphore()
    for p in zpeers + ypeers:
        pl.semaphore_signal(barrier, inc=1, device_id={"row": p}, device_id_type=MESH)
    pl.semaphore_wait(barrier, (inner - 1) + (outer - 1))
    pltpu.make_async_copy(part_ref, buf1.at[pl.ds(z, 1)], recv_z.at[z]).start()
    zcopies = []
    for i, p in enumerate(zpeers):
        cp = pltpu.make_async_remote_copy(
            src_ref=part_ref, dst_ref=buf1.at[pl.ds(z, 1)], send_sem=send_z.at[i],
            recv_sem=recv_z.at[z], device_id={"row": p}, device_id_type=MESH)
        cp.start()
        zcopies.append(cp)
    for s in range(inner):
        pltpu.make_async_copy(part_ref, buf1.at[pl.ds(s, 1)], recv_z.at[s]).wait()
    zsum[...] = jnp.sum(buf1[...], axis=0, keepdims=True)
    pltpu.make_async_copy(zsum, buf2.at[pl.ds(y, 1)], recv_y.at[y]).start()
    ycopies = []
    for i, p in enumerate(ypeers):
        cp = pltpu.make_async_remote_copy(
            src_ref=zsum, dst_ref=buf2.at[pl.ds(y, 1)], send_sem=send_y.at[i],
            recv_sem=recv_y.at[y], device_id={"row": p}, device_id_type=MESH)
        cp.start()
        ycopies.append(cp)
    for cp in zcopies + ycopies:
        cp.wait_send()
    for s in range(outer):
        pltpu.make_async_copy(zsum, buf2.at[pl.ds(s, 1)], recv_y.at[s]).wait()
    out_ref[...] = jnp.sum(buf2[...], axis=0, keepdims=True)


def row_sum(part, n, inner, cid):
    outer = n // inner
    width = part.shape[1]
    return pl.pallas_call(
        functools.partial(colsum_kernel, n, inner),
        out_shape=jax.ShapeDtypeStruct((1, width), part.dtype),
        in_specs=[VMEM],
        out_specs=VMEM,
        scratch_shapes=[
            pltpu.VMEM((inner, width), part.dtype),
            pltpu.VMEM((1, width), part.dtype),
            pltpu.VMEM((outer, width), part.dtype),
            pltpu.SemaphoreType.DMA((inner - 1,)),
            pltpu.SemaphoreType.DMA((outer - 1,)),
            pltpu.SemaphoreType.DMA((inner,)),
            pltpu.SemaphoreType.DMA((outer,)),
        ],
        compiler_params=params(cid),
    )(part)


def gather_kernel(axis, n, src_ref, out_ref, send_sem, recv_sem):
    me = lax.axis_index(axis)
    peers = [lax.rem(me + d, n) for d in range(1, n)]
    barrier = pltpu.get_barrier_semaphore()
    for p in peers:
        pl.semaphore_signal(barrier, inc=1, device_id={axis: p}, device_id_type=MESH)
    pl.semaphore_wait(barrier, n - 1)
    pltpu.make_async_copy(src_ref, out_ref.at[me], recv_sem.at[me]).start()
    copies = []
    for i, p in enumerate(peers):
        cp = pltpu.make_async_remote_copy(
            src_ref=src_ref, dst_ref=out_ref.at[me], send_sem=send_sem.at[i],
            recv_sem=recv_sem.at[me], device_id={axis: p}, device_id_type=MESH)
        cp.start()
        copies.append(cp)
    for cp in copies:
        cp.wait_send()
    for s in range(n):
        pltpu.make_async_copy(src_ref, out_ref.at[s], recv_sem.at[s]).wait()


def gather(x, axis, n, cid):
    return pl.pallas_call(
        functools.partial(gather_kernel, axis, n),
        out_shape=jax.ShapeDtypeStruct((n,) + x.shape, x.dtype),
        in_specs=[VMEM],
        out_specs=VMEM,
        scratch_shapes=[
            pltpu.SemaphoreType.DMA((n - 1,)),
            pltpu.SemaphoreType.DMA((n,)),
        ],
        compiler_params=params(cid),
    )(x)


def iteration_kernel(n_row, n_col, inner, chunk, first_step, *refs):
    if first_step:
        (sim_ref, resp_out, avail_out, fcol, scol, pack, buf_f, buf_s, zpart, buf1, zsum, buf2,
         send_t, recv_t, send_z, send_y, recv_z, recv_y) = refs
        avail_ref = resp_ref = None
    else:
        (sim_ref, avail_ref, resp_ref, resp_out, avail_out, fcol, scol, pack, buf_f, buf_s, zpart,
         buf1, zsum, buf2, send_t, recv_t, send_z, send_y, recv_z, recv_y) = refs
    rows, cols = sim_ref.shape
    r = lax.axis_index("row")
    c = lax.axis_index("col")
    outer = n_row // inner
    y = r // inner
    z = r % inner
    cpeers = [lax.rem(c + d, n_col) for d in range(1, n_col)]
    zpeers = [y * inner + lax.rem(z + d, inner) for d in range(1, inner)]
    ypeers = [lax.rem(y + d, outer) * inner + z for d in range(1, outer)]
    barrier = pltpu.get_barrier_semaphore()
    for p in cpeers:
        pl.semaphore_signal(barrier, inc=1, device_id={"col": p}, device_id_type=MESH)
    for p in zpeers + ypeers:
        pl.semaphore_signal(barrier, inc=1, device_id={"row": p}, device_id_type=MESH)
    pl.semaphore_wait(barrier, (n_col - 1) + (inner - 1) + (outer - 1))

    row_start = r * rows
    col_start = c * cols
    n_chunks = rows // chunk

    def summed_at(i0):
        s = sim_ref[pl.ds(i0, chunk), :]
        if first_step:
            return s, s
        return s, avail_ref[pl.ds(i0, chunk), :] + s

    def top_body(i, carry):
        i0 = pl.multiple_of(i * chunk, chunk)
        s, summed = summed_at(i0)
        first = jnp.max(summed, axis=1, keepdims=True)
        hits = summed == first
        repeats = jnp.sum(hits.astype(jnp.float32), axis=1, keepdims=True)
        others = jnp.max(jnp.where(hits, -jnp.inf, summed), axis=1, keepdims=True)
        second = jnp.where(repeats > 1.0, first, others)
        fcol[pl.ds(i0, chunk), :] = jnp.broadcast_to(first, (chunk, 128))
        scol[pl.ds(i0, chunk), :] = jnp.broadcast_to(second, (chunk, 128))
        return carry

    lax.fori_loop(0, n_chunks, top_body, 0)
    pack[0:1, :] = fcol[...].T[0:1, :]
    pack[1:2, :] = scol[...].T[0:1, :]

    tcopies = []
    for k, (src, dst) in enumerate(((pack.at[0:1], buf_f), (pack.at[1:2], buf_s))):
        pltpu.make_async_copy(src, dst.at[pl.ds(c, 1)], recv_t.at[k, c]).start()
        for i, p in enumerate(cpeers):
            cp = pltpu.make_async_remote_copy(
                src_ref=src, dst_ref=dst.at[pl.ds(c, 1)], send_sem=send_t.at[k, i],
                recv_sem=recv_t.at[k, c], device_id={"col": p}, device_id_type=MESH)
            cp.start()
            tcopies.append(cp)
    for k, dst in enumerate((buf_f, buf_s)):
        for s in range(n_col):
            pltpu.make_async_copy(pack.at[0:1], dst.at[pl.ds(s, 1)], recv_t.at[k, s]).wait()
    firsts = buf_f[...]
    seconds = buf_s[...]
    first = jnp.max(firsts, axis=0, keepdims=True)
    at_top = firsts == first
    repeats = jnp.sum(at_top.astype(jnp.float32), axis=0, keepdims=True)
    others = jnp.max(jnp.where(at_top, -jnp.inf, firsts), axis=0, keepdims=True)
    second = jnp.where(repeats > 1.0, first, jnp.maximum(jnp.max(seconds, axis=0, keepdims=True), others))
    fcol[...] = jnp.broadcast_to(first, (128, rows)).T
    scol[...] = jnp.broadcast_to(second, (128, rows)).T

    col_ids = col_start + lax.broadcasted_iota(jnp.int32, (chunk, cols), 1)

    def diag_at(i0):
        row_ids = row_start + i0 + lax.broadcasted_iota(jnp.int32, (chunk, cols), 0)
        return row_ids == col_ids

    def resp_body(i, acc):
        i0 = pl.multiple_of(i * chunk, chunk)
        s, summed = summed_at(i0)
        f = fcol[pl.ds(i0, chunk), 0:1]
        sc = scol[pl.ds(i0, chunk), 0:1]
        fresh = s - jnp.where(summed == f, sc, f)
        if first_step:
            resp = (1.0 - DAMPING) * fresh
        else:
            resp = DAMPING * resp_ref[pl.ds(i0, chunk), :] + (1.0 - DAMPING) * fresh
        resp_out[pl.ds(i0, chunk), :] = resp
        positive = jnp.where(diag_at(i0), resp, jnp.maximum(resp, 0.0))
        return acc + jnp.sum(positive, axis=0, keepdims=True)

    zpart[...] = lax.fori_loop(0, n_chunks, resp_body, jnp.zeros((1, cols), jnp.float32))

    pltpu.make_async_copy(zpart, buf1.at[pl.ds(z, 1)], recv_z.at[z]).start()
    zcopies = []
    for i, p in enumerate(zpeers):
        cp = pltpu.make_async_remote_copy(
            src_ref=zpart, dst_ref=buf1.at[pl.ds(z, 1)], send_sem=send_z.at[i],
            recv_sem=recv_z.at[z], device_id={"row": p}, device_id_type=MESH)
        cp.start()
        zcopies.append(cp)
    for s in range(inner):
        pltpu.make_async_copy(zpart, buf1.at[pl.ds(s, 1)], recv_z.at[s]).wait()
    zsum[...] = jnp.sum(buf1[...], axis=0, keepdims=True)
    pltpu.make_async_copy(zsum, buf2.at[pl.ds(y, 1)], recv_y.at[y]).start()
    ycopies = []
    for i, p in enumerate(ypeers):
        cp = pltpu.make_async_remote_copy(
            src_ref=zsum, dst_ref=buf2.at[pl.ds(y, 1)], send_sem=send_y.at[i],
            recv_sem=recv_y.at[y], device_id={"row": p}, device_id_type=MESH)
        cp.start()
        ycopies.append(cp)
    for s in range(outer):
        pltpu.make_async_copy(zsum, buf2.at[pl.ds(s, 1)], recv_y.at[s]).wait()
    colsum = jnp.sum(buf2[...], axis=0, keepdims=True)

    def avail_body(i, carry):
        i0 = pl.multiple_of(i * chunk, chunk)
        resp = resp_out[pl.ds(i0, chunk), :]
        diag = diag_at(i0)
        positive = jnp.where(diag, resp, jnp.maximum(resp, 0.0))
        renew = colsum - positive
        renew = jnp.where(diag, renew, jnp.minimum(renew, 0.0))
        if first_step:
            avail_out[pl.ds(i0, chunk), :] = (1.0 - DAMPING) * renew
        else:
            avail_out[pl.ds(i0, chunk), :] = DAMPING * avail_ref[pl.ds(i0, chunk), :] + (1.0 - DAMPING) * renew
        return carry

    lax.fori_loop(0, n_chunks, avail_body, 0)
    for cp in tcopies + zcopies + ycopies:
        cp.wait_send()


def iterate(sim, avail, resp, n_row, n_col, inner, cid):
    rows, cols = sim.shape
    outer = n_row // inner
    first_step = avail is None
    operands = (sim,) if first_step else (sim, avail, resp)
    f32 = jnp.float32
    return pl.pallas_call(
        functools.partial(iteration_kernel, n_row, n_col, inner, 32, first_step),
        out_shape=(jax.ShapeDtypeStruct((rows, cols), f32), jax.ShapeDtypeStruct((rows, cols), f32)),
        in_specs=[VMEM] * len(operands),
        out_specs=(VMEM, VMEM),
        scratch_shapes=[
            pltpu.VMEM((rows, 128), f32),
            pltpu.VMEM((rows, 128), f32),
            pltpu.VMEM((2, rows), f32),
            pltpu.VMEM((n_col, rows), f32),
            pltpu.VMEM((n_col, rows), f32),
            pltpu.VMEM((1, cols), f32),
            pltpu.VMEM((inner, cols), f32),
            pltpu.VMEM((1, cols), f32),
            pltpu.VMEM((outer, cols), f32),
            pltpu.SemaphoreType.DMA((2, n_col - 1)),
            pltpu.SemaphoreType.DMA((2, n_col)),
            pltpu.SemaphoreType.DMA((inner - 1,)),
            pltpu.SemaphoreType.DMA((outer - 1,)),
            pltpu.SemaphoreType.DMA((inner,)),
            pltpu.SemaphoreType.DMA((outer,)),
        ],
        compiler_params=pltpu.CompilerParams(
            collective_id=cid, has_side_effects=True, vmem_limit_bytes=60 * 1024 * 1024),
    )(*operands)


def similarity(row_emb, col_emb, row_start, col_start, pref_rows):
    cross = lax.dot_general(
        row_emb, col_emb, (((1,), (1,)), ((), ())), preferred_element_type=jnp.float32
    )
    row_vals = row_emb.astype(jnp.float32)
    col_vals = col_emb.astype(jnp.float32)
    row_sq = jnp.sum(row_vals * row_vals, axis=1)
    col_sq = jnp.sum(col_vals * col_vals, axis=1)
    dist = 2.0 * cross - row_sq[:, None] - col_sq[None, :]
    row_ids = row_start + jnp.arange(row_emb.shape[0], dtype=jnp.int32)
    col_ids = col_start + jnp.arange(col_emb.shape[0], dtype=jnp.int32)
    diagonal = row_ids[:, None] == col_ids[None, :]
    return (jnp.where(diagonal, pref_rows[:, None], dist), diagonal)


def top_two(summed):
    first = jnp.max(summed, axis=1)
    hits = summed == first[:, None]
    repeats = jnp.sum(hits.astype(jnp.int32), axis=1)
    others = jnp.max(jnp.where(hits, -jnp.inf, summed), axis=1)
    second = jnp.where(repeats > 1, first, others)
    return (first, second)


def local(embedding, preference):
    rows_n = lax.axis_size("row")
    cols_n = lax.axis_size("col")
    row_idx = lax.axis_index("row")
    col_idx = lax.axis_index("col")
    mol = embedding.shape[2]
    width = embedding.shape[3]
    row_count = mol * cols_n
    col_count = mol * rows_n
    colb, rowb = distribute(embedding.reshape(mol, width), rows_n, cols_n, INNER)
    column_block = colb.reshape(col_count, width)
    row_block = rowb.reshape(row_count, width)
    row_start = row_idx * row_count
    col_start = col_idx * col_count
    sim, unused = similarity(row_block, column_block, row_start, col_start, preference)
    avail = resp = None
    for step in range(ITERS):
        resp, avail = iterate(sim, avail, resp, rows_n, cols_n, INNER, 1 + step)
    return (resp, avail)


def solution(mesh):
    placed = (P("col", "row", None, None), P("row"))
    return jax.shard_map(
        local,
        mesh=mesh,
        in_specs=placed,
        out_specs=(P("row", "col"), P("row", "col")),
        check_vma=False,
    )
```

```python
import functools

import jax
import jax.numpy as jnp
from jax import lax
from jax.experimental import pallas as pl
from jax.experimental.pallas import tpu as pltpu
from jax.sharding import PartitionSpec as P

ITERS = 2


DAMPING = 0.5

INNER = 8

MESH = pl.DeviceIdType.MESH
VMEM = pl.BlockSpec(memory_space=pltpu.VMEM)


def params(cid):
    return pltpu.CompilerParams(collective_id=cid, has_side_effects=True)


def embed_kernel(n_row, n_col, inner, chunk_ref, colb_ref, rowb_ref, send_z, send_y, send_r, recv_c, recv_b, recv_r):
    r = lax.axis_index("row")
    c = lax.axis_index("col")
    outer = n_row // inner
    y = r // inner
    z = r % inner
    g = c * n_row + r
    target_row = g // n_col
    my_slot = g % n_col
    zpeers = [(y * inner + lax.rem(z + d, inner), c) for d in range(1, inner)]
    ypeers = [(lax.rem(y + d, outer) * inner + z, c) for d in range(1, outer)]
    targets = [(target_row, j) for j in range(n_col)]
    sources = []
    for s in range(n_col):
        gs = r * n_col + s
        sources.append((gs % n_row, gs // n_row))

    def differs(dev):
        return jnp.logical_or(dev[0] != r, dev[1] != c)

    barrier = pltpu.get_barrier_semaphore()
    for dev in zpeers + ypeers:
        pl.semaphore_signal(barrier, inc=1, device_id=dev, device_id_type=MESH)
    for dev in targets + sources:
        @pl.when(differs(dev))
        def _():
            pl.semaphore_signal(barrier, inc=1, device_id=dev, device_id_type=MESH)
    self_in = (target_row == r).astype(jnp.int32)
    pl.semaphore_wait(barrier, (inner - 1) + (outer - 1) + 2 * (n_col - self_in))

    pltpu.make_async_copy(chunk_ref, colb_ref.at[r], recv_c.at[z]).start()
    zcopies = []
    for i, dev in enumerate(zpeers):
        cp = pltpu.make_async_remote_copy(
            src_ref=chunk_ref, dst_ref=colb_ref.at[r], send_sem=send_z.at[i],
            recv_sem=recv_c.at[z], device_id=dev, device_id_type=MESH)
        cp.start()
        zcopies.append(cp)
    row_copies = []
    for j, dev in enumerate(targets):
        cp = pltpu.make_async_remote_copy(
            src_ref=chunk_ref, dst_ref=rowb_ref.at[my_slot], send_sem=send_r.at[j],
            recv_sem=recv_r.at[my_slot], device_id=dev, device_id_type=MESH)
        row_copies.append(cp)

        @pl.when(differs(dev))
        def _():
            cp.start()

        @pl.when(jnp.logical_not(differs(dev)))
        def _():
            pltpu.make_async_copy(chunk_ref, rowb_ref.at[my_slot], recv_r.at[my_slot]).start()

    for s in range(inner):
        pltpu.make_async_copy(chunk_ref, colb_ref.at[y * inner + s], recv_c.at[s]).wait()
    block = colb_ref.at[pl.ds(y * inner, inner)]
    ycopies = []
    for i, dev in enumerate(ypeers):
        cp = pltpu.make_async_remote_copy(
            src_ref=block, dst_ref=block, send_sem=send_y.at[i],
            recv_sem=recv_b.at[y], device_id=dev, device_id_type=MESH)
        cp.start()
        ycopies.append(cp)

    for cp in zcopies + ycopies:
        cp.wait_send()
    for j, dev in enumerate(targets):
        @pl.when(differs(dev))
        def _():
            row_copies[j].wait_send()
    for d in range(1, outer):
        yo = lax.rem(y + d, outer)
        other = colb_ref.at[pl.ds(yo * inner, inner)]
        pltpu.make_async_copy(other, other, recv_b.at[yo]).wait()
    for s in range(n_col):
        pltpu.make_async_copy(chunk_ref, rowb_ref.at[s], recv_r.at[s]).wait()


def distribute(chunk, n_row, n_col, inner):
    mol, width = chunk.shape
    outer = n_row // inner
    return pl.pallas_call(
        functools.partial(embed_kernel, n_row, n_col, inner),
        out_shape=(jax.ShapeDtypeStruct((n_row, mol, width), chunk.dtype),
                   jax.ShapeDtypeStruct((n_col, mol, width), chunk.dtype)),
        in_specs=[VMEM],
        out_specs=(VMEM, VMEM),
        scratch_shapes=[
            pltpu.SemaphoreType.DMA((inner - 1,)),
            pltpu.SemaphoreType.DMA((outer - 1,)),
            pltpu.SemaphoreType.DMA((n_col,)),
            pltpu.SemaphoreType.DMA((inner,)),
            pltpu.SemaphoreType.DMA((outer,)),
            pltpu.SemaphoreType.DMA((n_col,)),
        ],
        compiler_params=params(0),
    )(chunk)


def colsum_kernel(n, inner, part_ref, out_ref, buf1, zsum, buf2, send_z, send_y, recv_z, recv_y):
    r = lax.axis_index("row")
    outer = n // inner
    y = r // inner
    z = r % inner
    zpeers = [y * inner + lax.rem(z + d, inner) for d in range(1, inner)]
    ypeers = [lax.rem(y + d, outer) * inner + z for d in range(1, outer)]
    barrier = pltpu.get_barrier_semaphore()
    for p in zpeers + ypeers:
        pl.semaphore_signal(barrier, inc=1, device_id={"row": p}, device_id_type=MESH)
    pl.semaphore_wait(barrier, (inner - 1) + (outer - 1))
    pltpu.make_async_copy(part_ref, buf1.at[pl.ds(z, 1)], recv_z.at[z]).start()
    zcopies = []
    for i, p in enumerate(zpeers):
        cp = pltpu.make_async_remote_copy(
            src_ref=part_ref, dst_ref=buf1.at[pl.ds(z, 1)], send_sem=send_z.at[i],
            recv_sem=recv_z.at[z], device_id={"row": p}, device_id_type=MESH)
        cp.start()
        zcopies.append(cp)
    for s in range(inner):
        pltpu.make_async_copy(part_ref, buf1.at[pl.ds(s, 1)], recv_z.at[s]).wait()
    zsum[...] = jnp.sum(buf1[...], axis=0, keepdims=True)
    pltpu.make_async_copy(zsum, buf2.at[pl.ds(y, 1)], recv_y.at[y]).start()
    ycopies = []
    for i, p in enumerate(ypeers):
        cp = pltpu.make_async_remote_copy(
            src_ref=zsum, dst_ref=buf2.at[pl.ds(y, 1)], send_sem=send_y.at[i],
            recv_sem=recv_y.at[y], device_id={"row": p}, device_id_type=MESH)
        cp.start()
        ycopies.append(cp)
    for cp in zcopies + ycopies:
        cp.wait_send()
    for s in range(outer):
        pltpu.make_async_copy(zsum, buf2.at[pl.ds(s, 1)], recv_y.at[s]).wait()
    out_ref[...] = jnp.sum(buf2[...], axis=0, keepdims=True)


def row_sum(part, n, inner, cid):
    outer = n // inner
    width = part.shape[1]
    return pl.pallas_call(
        functools.partial(colsum_kernel, n, inner),
        out_shape=jax.ShapeDtypeStruct((1, width), part.dtype),
        in_specs=[VMEM],
        out_specs=VMEM,
        scratch_shapes=[
            pltpu.VMEM((inner, width), part.dtype),
            pltpu.VMEM((1, width), part.dtype),
            pltpu.VMEM((outer, width), part.dtype),
            pltpu.SemaphoreType.DMA((inner - 1,)),
            pltpu.SemaphoreType.DMA((outer - 1,)),
            pltpu.SemaphoreType.DMA((inner,)),
            pltpu.SemaphoreType.DMA((outer,)),
        ],
        compiler_params=params(cid),
    )(part)


def gather_kernel(axis, n, src_ref, out_ref, send_sem, recv_sem):
    me = lax.axis_index(axis)
    peers = [lax.rem(me + d, n) for d in range(1, n)]
    barrier = pltpu.get_barrier_semaphore()
    for p in peers:
        pl.semaphore_signal(barrier, inc=1, device_id={axis: p}, device_id_type=MESH)
    pl.semaphore_wait(barrier, n - 1)
    pltpu.make_async_copy(src_ref, out_ref.at[me], recv_sem.at[me]).start()
    copies = []
    for i, p in enumerate(peers):
        cp = pltpu.make_async_remote_copy(
            src_ref=src_ref, dst_ref=out_ref.at[me], send_sem=send_sem.at[i],
            recv_sem=recv_sem.at[me], device_id={axis: p}, device_id_type=MESH)
        cp.start()
        copies.append(cp)
    for cp in copies:
        cp.wait_send()
    for s in range(n):
        pltpu.make_async_copy(src_ref, out_ref.at[s], recv_sem.at[s]).wait()


def gather(x, axis, n, cid):
    return pl.pallas_call(
        functools.partial(gather_kernel, axis, n),
        out_shape=jax.ShapeDtypeStruct((n,) + x.shape, x.dtype),
        in_specs=[VMEM],
        out_specs=VMEM,
        scratch_shapes=[
            pltpu.SemaphoreType.DMA((n - 1,)),
            pltpu.SemaphoreType.DMA((n,)),
        ],
        compiler_params=params(cid),
    )(x)


def ap_kernel(n_row, n_col, inner, chunk, iters, rowb_ref, colb_ref, prefc_ref, resp_out, avail_out,
              sim_s, resp_s, avail_s, fcol, scol, cq, pack, buf_f, buf_s, zpart, buf1, zsum, buf2,
              send_t, recv_t, send_z, send_y, recv_z, recv_y):
    rows, cols = sim_s.shape
    r = lax.axis_index("row")
    c = lax.axis_index("col")
    outer = n_row // inner
    y = r // inner
    z = r % inner
    cpeers = [lax.rem(c + d, n_col) for d in range(1, n_col)]
    zpeers = [y * inner + lax.rem(z + d, inner) for d in range(1, inner)]
    ypeers = [lax.rem(y + d, outer) * inner + z for d in range(1, outer)]
    barrier = pltpu.get_barrier_semaphore()
    for p in cpeers:
        pl.semaphore_signal(barrier, inc=1, device_id={"col": p}, device_id_type=MESH)
    for p in zpeers + ypeers:
        pl.semaphore_signal(barrier, inc=1, device_id={"row": p}, device_id_type=MESH)

    row_start = r * rows
    col_start = c * cols
    n_chunks = rows // chunk
    col_ids = col_start + lax.broadcasted_iota(jnp.int32, (chunk, cols), 1)

    def diag_at(i0):
        row_ids = row_start + i0 + lax.broadcasted_iota(jnp.int32, (chunk, cols), 0)
        return row_ids == col_ids

    def record_top(i0, summed):
        first = jnp.max(summed, axis=1, keepdims=True)
        hits = summed == first
        repeats = jnp.sum(hits.astype(jnp.float32), axis=1, keepdims=True)
        others = jnp.max(jnp.where(hits, -jnp.inf, summed), axis=1, keepdims=True)
        second = jnp.where(repeats > 1.0, first, others)
        fcol[pl.ds(i0, chunk), :] = jnp.broadcast_to(first, (chunk, 128))
        scol[pl.ds(i0, chunk), :] = jnp.broadcast_to(second, (chunk, 128))

    cb = 128 if cols % 128 == 0 else cols
    for j in range(cols // cb):
        xc = colb_ref[pl.ds(j * cb, cb), :].astype(jnp.float32)
        qc = jnp.sum(xc * xc, axis=1, keepdims=True)
        cq[0:1, pl.ds(j * cb, cb)] = jnp.broadcast_to(qc, (cb, 128)).T[0:1, :]
    rb = 128 if rows % 128 == 0 else rows
    for j in range(rows // rb):
        sim_s[pl.ds(j * rb, rb), :] = lax.dot_general(
            rowb_ref[pl.ds(j * rb, rb), :], colb_ref[...], (((1,), (1,)), ((), ())),
            preferred_element_type=jnp.float32)

    def sim_body(i, carry):
        i0 = pl.multiple_of(i * chunk, chunk)
        xr = rowb_ref[pl.ds(i0, chunk), :].astype(jnp.float32)
        rq = jnp.sum(xr * xr, axis=1, keepdims=True)
        dist = 2.0 * sim_s[pl.ds(i0, chunk), :] - rq - cq[...]
        s = jnp.where(diag_at(i0), prefc_ref[pl.ds(i0, chunk), :], dist)
        sim_s[pl.ds(i0, chunk), :] = s
        record_top(i0, s)
        return carry

    lax.fori_loop(0, n_chunks, sim_body, 0)
    pl.semaphore_wait(barrier, (n_col - 1) + (inner - 1) + (outer - 1))

    copies = []
    for step in range(iters):
        first_step = step == 0
        last_step = step == iters - 1
        resp_prev, avail_prev = resp_s, avail_s
        resp_new, avail_new = (resp_out, avail_out) if last_step else (resp_s, avail_s)
        pk = pack.at[step]
        pk[0:1, :] = fcol[...].T[0:1, :]
        pk[1:2, :] = scol[...].T[0:1, :]
        for k, dst in enumerate((buf_f.at[step], buf_s.at[step])):
            src = pk.at[pl.ds(k, 1)]
            pltpu.make_async_copy(src, dst.at[pl.ds(c, 1)], recv_t.at[step, k, c]).start()
            for i, p in enumerate(cpeers):
                cp = pltpu.make_async_remote_copy(
                    src_ref=src, dst_ref=dst.at[pl.ds(c, 1)], send_sem=send_t.at[step, k, i],
                    recv_sem=recv_t.at[step, k, c], device_id={"col": p}, device_id_type=MESH)
                cp.start()
                copies.append(cp)
        for k, dst in enumerate((buf_f.at[step], buf_s.at[step])):
            for s in range(n_col):
                pltpu.make_async_copy(pk.at[pl.ds(0, 1)], dst.at[pl.ds(s, 1)], recv_t.at[step, k, s]).wait()
        firsts = buf_f[step]
        seconds = buf_s[step]
        first = jnp.max(firsts, axis=0, keepdims=True)
        at_top = firsts == first
        repeats = jnp.sum(at_top.astype(jnp.float32), axis=0, keepdims=True)
        others = jnp.max(jnp.where(at_top, -jnp.inf, firsts), axis=0, keepdims=True)
        second = jnp.where(repeats > 1.0, first, jnp.maximum(jnp.max(seconds, axis=0, keepdims=True), others))
        fcol[...] = jnp.broadcast_to(first, (128, rows)).T
        scol[...] = jnp.broadcast_to(second, (128, rows)).T

        def resp_body(i, acc):
            i0 = pl.multiple_of(i * chunk, chunk)
            s = sim_s[pl.ds(i0, chunk), :]
            summed = s if first_step else avail_prev[pl.ds(i0, chunk), :] + s
            f = fcol[pl.ds(i0, chunk), 0:1]
            sc = scol[pl.ds(i0, chunk), 0:1]
            fresh = s - jnp.where(summed == f, sc, f)
            if first_step:
                resp = (1.0 - DAMPING) * fresh
            else:
                resp = DAMPING * resp_prev[pl.ds(i0, chunk), :] + (1.0 - DAMPING) * fresh
            resp_new[pl.ds(i0, chunk), :] = resp
            positive = jnp.where(diag_at(i0), resp, jnp.maximum(resp, 0.0))
            return acc + jnp.sum(positive, axis=0, keepdims=True)

        zp = zpart.at[step]
        zp[...] = lax.fori_loop(0, n_chunks, resp_body, jnp.zeros((1, cols), jnp.float32))

        b1 = buf1.at[step]
        pltpu.make_async_copy(zp, b1.at[pl.ds(z, 1)], recv_z.at[step, z]).start()
        for i, p in enumerate(zpeers):
            cp = pltpu.make_async_remote_copy(
                src_ref=zp, dst_ref=b1.at[pl.ds(z, 1)], send_sem=send_z.at[step, i],
                recv_sem=recv_z.at[step, z], device_id={"row": p}, device_id_type=MESH)
            cp.start()
            copies.append(cp)
        for s in range(inner):
            pltpu.make_async_copy(zp, b1.at[pl.ds(s, 1)], recv_z.at[step, s]).wait()
        zs = zsum.at[step]
        zs[...] = jnp.sum(b1[...], axis=0, keepdims=True)
        b2 = buf2.at[step]
        pltpu.make_async_copy(zs, b2.at[pl.ds(y, 1)], recv_y.at[step, y]).start()
        for i, p in enumerate(ypeers):
            cp = pltpu.make_async_remote_copy(
                src_ref=zs, dst_ref=b2.at[pl.ds(y, 1)], send_sem=send_y.at[step, i],
                recv_sem=recv_y.at[step, y], device_id={"row": p}, device_id_type=MESH)
            cp.start()
            copies.append(cp)
        for s in range(outer):
            pltpu.make_async_copy(zs, b2.at[pl.ds(s, 1)], recv_y.at[step, s]).wait()
        colsum = jnp.sum(b2[...], axis=0, keepdims=True)

        def avail_body(i, carry):
            i0 = pl.multiple_of(i * chunk, chunk)
            resp = resp_new[pl.ds(i0, chunk), :]
            diag = diag_at(i0)
            positive = jnp.where(diag, resp, jnp.maximum(resp, 0.0))
            renew = colsum - positive
            renew = jnp.where(diag, renew, jnp.minimum(renew, 0.0))
            if first_step:
                avail = (1.0 - DAMPING) * renew
            else:
                avail = DAMPING * avail_prev[pl.ds(i0, chunk), :] + (1.0 - DAMPING) * renew
            avail_new[pl.ds(i0, chunk), :] = avail
            if not last_step:
                record_top(i0, avail + sim_s[pl.ds(i0, chunk), :])
            return carry

        lax.fori_loop(0, n_chunks, avail_body, 0)
    for cp in copies:
        cp.wait_send()


def propagate(rowb, colb, prefc, n_row, n_col, inner, iters, cid):
    rows, cols = rowb.shape[0], colb.shape[0]
    outer = n_row // inner
    f32 = jnp.float32
    return pl.pallas_call(
        functools.partial(ap_kernel, n_row, n_col, inner, 32, iters),
        out_shape=(jax.ShapeDtypeStruct((rows, cols), f32), jax.ShapeDtypeStruct((rows, cols), f32)),
        in_specs=[VMEM] * 3,
        out_specs=(VMEM, VMEM),
        scratch_shapes=[
            pltpu.VMEM((rows, cols), f32),
            pltpu.VMEM((rows, cols), f32),
            pltpu.VMEM((rows, cols), f32),
            pltpu.VMEM((rows, 128), f32),
            pltpu.VMEM((rows, 128), f32),
            pltpu.VMEM((1, cols), f32),
            pltpu.VMEM((iters, 2, rows), f32),
            pltpu.VMEM((iters, n_col, rows), f32),
            pltpu.VMEM((iters, n_col, rows), f32),
            pltpu.VMEM((iters, 1, cols), f32),
            pltpu.VMEM((iters, inner, cols), f32),
            pltpu.VMEM((iters, 1, cols), f32),
            pltpu.VMEM((iters, outer, cols), f32),
            pltpu.SemaphoreType.DMA((iters, 2, n_col - 1)),
            pltpu.SemaphoreType.DMA((iters, 2, n_col)),
            pltpu.SemaphoreType.DMA((iters, inner - 1)),
            pltpu.SemaphoreType.DMA((iters, outer - 1)),
            pltpu.SemaphoreType.DMA((iters, inner)),
            pltpu.SemaphoreType.DMA((iters, outer)),
        ],
        compiler_params=pltpu.CompilerParams(
            collective_id=cid, has_side_effects=True, vmem_limit_bytes=60 * 1024 * 1024),
    )(rowb, colb, prefc)


def similarity(row_emb, col_emb, row_start, col_start, pref_rows):
    cross = lax.dot_general(
        row_emb, col_emb, (((1,), (1,)), ((), ())), preferred_element_type=jnp.float32
    )
    row_vals = row_emb.astype(jnp.float32)
    col_vals = col_emb.astype(jnp.float32)
    row_sq = jnp.sum(row_vals * row_vals, axis=1)
    col_sq = jnp.sum(col_vals * col_vals, axis=1)
    dist = 2.0 * cross - row_sq[:, None] - col_sq[None, :]
    row_ids = row_start + jnp.arange(row_emb.shape[0], dtype=jnp.int32)
    col_ids = col_start + jnp.arange(col_emb.shape[0], dtype=jnp.int32)
    diagonal = row_ids[:, None] == col_ids[None, :]
    return (jnp.where(diagonal, pref_rows[:, None], dist), diagonal)


def top_two(summed):
    first = jnp.max(summed, axis=1)
    hits = summed == first[:, None]
    repeats = jnp.sum(hits.astype(jnp.int32), axis=1)
    others = jnp.max(jnp.where(hits, -jnp.inf, summed), axis=1)
    second = jnp.where(repeats > 1, first, others)
    return (first, second)


def local(embedding, preference):
    rows_n = lax.axis_size("row")
    cols_n = lax.axis_size("col")
    row_idx = lax.axis_index("row")
    col_idx = lax.axis_index("col")
    mol = embedding.shape[2]
    width = embedding.shape[3]
    row_count = mol * cols_n
    col_count = mol * rows_n
    colb, rowb = distribute(embedding.reshape(mol, width), rows_n, cols_n, INNER)
    column_block = colb.reshape(col_count, width)
    row_block = rowb.reshape(row_count, width)
    resp, avail = propagate(row_block, column_block, preference.reshape(row_count, 1), rows_n, cols_n, INNER, ITERS, 1)
    return (resp, avail)


def solution(mesh):
    placed = (P("col", "row", None, None), P("row"))
    return jax.shard_map(
        local,
        mesh=mesh,
        in_specs=placed,
        out_specs=(P("row", "col"), P("row", "col")),
        check_vma=False,
    )
```

```python
import functools

import jax
import jax.numpy as jnp
from jax import lax
from jax.experimental import pallas as pl
from jax.experimental.pallas import tpu as pltpu
from jax.sharding import PartitionSpec as P

ITERS = 2


DAMPING = 0.5

INNER = 8

MESH = pl.DeviceIdType.MESH
VMEM = pl.BlockSpec(memory_space=pltpu.VMEM)


def params(cid):
    return pltpu.CompilerParams(collective_id=cid, has_side_effects=True)


def embed_kernel(n_row, n_col, inner, chunk_ref, colb_ref, rowb_ref, send_z, send_y, send_r, recv_c, recv_b, recv_r):
    r = lax.axis_index("row")
    c = lax.axis_index("col")
    outer = n_row // inner
    y = r // inner
    z = r % inner
    g = c * n_row + r
    target_row = g // n_col
    my_slot = g % n_col
    zpeers = [(y * inner + lax.rem(z + d, inner), c) for d in range(1, inner)]
    ypeers = [(lax.rem(y + d, outer) * inner + z, c) for d in range(1, outer)]
    targets = [(target_row, j) for j in range(n_col)]
    sources = []
    for s in range(n_col):
        gs = r * n_col + s
        sources.append((gs % n_row, gs // n_row))

    def differs(dev):
        return jnp.logical_or(dev[0] != r, dev[1] != c)

    barrier = pltpu.get_barrier_semaphore()
    for dev in zpeers + ypeers:
        pl.semaphore_signal(barrier, inc=1, device_id=dev, device_id_type=MESH)
    for dev in targets + sources:
        @pl.when(differs(dev))
        def _():
            pl.semaphore_signal(barrier, inc=1, device_id=dev, device_id_type=MESH)
    self_in = (target_row == r).astype(jnp.int32)
    pl.semaphore_wait(barrier, (inner - 1) + (outer - 1) + 2 * (n_col - self_in))

    pltpu.make_async_copy(chunk_ref, colb_ref.at[r], recv_c.at[z]).start()
    zcopies = []
    for i, dev in enumerate(zpeers):
        cp = pltpu.make_async_remote_copy(
            src_ref=chunk_ref, dst_ref=colb_ref.at[r], send_sem=send_z.at[i],
            recv_sem=recv_c.at[z], device_id=dev, device_id_type=MESH)
        cp.start()
        zcopies.append(cp)
    row_copies = []
    for j, dev in enumerate(targets):
        cp = pltpu.make_async_remote_copy(
            src_ref=chunk_ref, dst_ref=rowb_ref.at[my_slot], send_sem=send_r.at[j],
            recv_sem=recv_r.at[my_slot], device_id=dev, device_id_type=MESH)
        row_copies.append(cp)

        @pl.when(differs(dev))
        def _():
            cp.start()

        @pl.when(jnp.logical_not(differs(dev)))
        def _():
            pltpu.make_async_copy(chunk_ref, rowb_ref.at[my_slot], recv_r.at[my_slot]).start()

    for s in range(inner):
        pltpu.make_async_copy(chunk_ref, colb_ref.at[y * inner + s], recv_c.at[s]).wait()
    block = colb_ref.at[pl.ds(y * inner, inner)]
    ycopies = []
    for i, dev in enumerate(ypeers):
        cp = pltpu.make_async_remote_copy(
            src_ref=block, dst_ref=block, send_sem=send_y.at[i],
            recv_sem=recv_b.at[y], device_id=dev, device_id_type=MESH)
        cp.start()
        ycopies.append(cp)

    for cp in zcopies + ycopies:
        cp.wait_send()
    for j, dev in enumerate(targets):
        @pl.when(differs(dev))
        def _():
            row_copies[j].wait_send()
    for d in range(1, outer):
        yo = lax.rem(y + d, outer)
        other = colb_ref.at[pl.ds(yo * inner, inner)]
        pltpu.make_async_copy(other, other, recv_b.at[yo]).wait()
    for s in range(n_col):
        pltpu.make_async_copy(chunk_ref, rowb_ref.at[s], recv_r.at[s]).wait()


def distribute(chunk, n_row, n_col, inner):
    mol, width = chunk.shape
    outer = n_row // inner
    return pl.pallas_call(
        functools.partial(embed_kernel, n_row, n_col, inner),
        out_shape=(jax.ShapeDtypeStruct((n_row, mol, width), chunk.dtype),
                   jax.ShapeDtypeStruct((n_col, mol, width), chunk.dtype)),
        in_specs=[VMEM],
        out_specs=(VMEM, VMEM),
        scratch_shapes=[
            pltpu.SemaphoreType.DMA((inner - 1,)),
            pltpu.SemaphoreType.DMA((outer - 1,)),
            pltpu.SemaphoreType.DMA((n_col,)),
            pltpu.SemaphoreType.DMA((inner,)),
            pltpu.SemaphoreType.DMA((outer,)),
            pltpu.SemaphoreType.DMA((n_col,)),
        ],
        compiler_params=params(0),
    )(chunk)


def colsum_kernel(n, inner, part_ref, out_ref, buf1, zsum, buf2, send_z, send_y, recv_z, recv_y):
    r = lax.axis_index("row")
    outer = n // inner
    y = r // inner
    z = r % inner
    zpeers = [y * inner + lax.rem(z + d, inner) for d in range(1, inner)]
    ypeers = [lax.rem(y + d, outer) * inner + z for d in range(1, outer)]
    barrier = pltpu.get_barrier_semaphore()
    for p in zpeers + ypeers:
        pl.semaphore_signal(barrier, inc=1, device_id={"row": p}, device_id_type=MESH)
    pl.semaphore_wait(barrier, (inner - 1) + (outer - 1))
    pltpu.make_async_copy(part_ref, buf1.at[pl.ds(z, 1)], recv_z.at[z]).start()
    zcopies = []
    for i, p in enumerate(zpeers):
        cp = pltpu.make_async_remote_copy(
            src_ref=part_ref, dst_ref=buf1.at[pl.ds(z, 1)], send_sem=send_z.at[i],
            recv_sem=recv_z.at[z], device_id={"row": p}, device_id_type=MESH)
        cp.start()
        zcopies.append(cp)
    for s in range(inner):
        pltpu.make_async_copy(part_ref, buf1.at[pl.ds(s, 1)], recv_z.at[s]).wait()
    zsum[...] = jnp.sum(buf1[...], axis=0, keepdims=True)
    pltpu.make_async_copy(zsum, buf2.at[pl.ds(y, 1)], recv_y.at[y]).start()
    ycopies = []
    for i, p in enumerate(ypeers):
        cp = pltpu.make_async_remote_copy(
            src_ref=zsum, dst_ref=buf2.at[pl.ds(y, 1)], send_sem=send_y.at[i],
            recv_sem=recv_y.at[y], device_id={"row": p}, device_id_type=MESH)
        cp.start()
        ycopies.append(cp)
    for cp in zcopies + ycopies:
        cp.wait_send()
    for s in range(outer):
        pltpu.make_async_copy(zsum, buf2.at[pl.ds(s, 1)], recv_y.at[s]).wait()
    out_ref[...] = jnp.sum(buf2[...], axis=0, keepdims=True)


def row_sum(part, n, inner, cid):
    outer = n // inner
    width = part.shape[1]
    return pl.pallas_call(
        functools.partial(colsum_kernel, n, inner),
        out_shape=jax.ShapeDtypeStruct((1, width), part.dtype),
        in_specs=[VMEM],
        out_specs=VMEM,
        scratch_shapes=[
            pltpu.VMEM((inner, width), part.dtype),
            pltpu.VMEM((1, width), part.dtype),
            pltpu.VMEM((outer, width), part.dtype),
            pltpu.SemaphoreType.DMA((inner - 1,)),
            pltpu.SemaphoreType.DMA((outer - 1,)),
            pltpu.SemaphoreType.DMA((inner,)),
            pltpu.SemaphoreType.DMA((outer,)),
        ],
        compiler_params=params(cid),
    )(part)


def gather_kernel(axis, n, src_ref, out_ref, send_sem, recv_sem):
    me = lax.axis_index(axis)
    peers = [lax.rem(me + d, n) for d in range(1, n)]
    barrier = pltpu.get_barrier_semaphore()
    for p in peers:
        pl.semaphore_signal(barrier, inc=1, device_id={axis: p}, device_id_type=MESH)
    pl.semaphore_wait(barrier, n - 1)
    pltpu.make_async_copy(src_ref, out_ref.at[me], recv_sem.at[me]).start()
    copies = []
    for i, p in enumerate(peers):
        cp = pltpu.make_async_remote_copy(
            src_ref=src_ref, dst_ref=out_ref.at[me], send_sem=send_sem.at[i],
            recv_sem=recv_sem.at[me], device_id={axis: p}, device_id_type=MESH)
        cp.start()
        copies.append(cp)
    for cp in copies:
        cp.wait_send()
    for s in range(n):
        pltpu.make_async_copy(src_ref, out_ref.at[s], recv_sem.at[s]).wait()


def gather(x, axis, n, cid):
    return pl.pallas_call(
        functools.partial(gather_kernel, axis, n),
        out_shape=jax.ShapeDtypeStruct((n,) + x.shape, x.dtype),
        in_specs=[VMEM],
        out_specs=VMEM,
        scratch_shapes=[
            pltpu.SemaphoreType.DMA((n - 1,)),
            pltpu.SemaphoreType.DMA((n,)),
        ],
        compiler_params=params(cid),
    )(x)


def ap_kernel(n_row, n_col, inner, chunk, iters, chunk_ref, prefr_ref, resp_out, avail_out,
              colb3, rowb3, prefc, sim_s, resp_s, avail_s, fcol, scol, cq, pack, buf_f, buf_s, zpart, buf1,
              zsum, buf2, e_send_z, e_send_y, e_send_r, e_recv_c, e_recv_b, e_recv_r,
              send_t, recv_t, send_z, send_y, recv_z, recv_y):
    rows, cols = sim_s.shape
    r = lax.axis_index("row")
    c = lax.axis_index("col")
    outer = n_row // inner
    y = r // inner
    z = r % inner
    cpeers = [lax.rem(c + d, n_col) for d in range(1, n_col)]
    zpeers = [y * inner + lax.rem(z + d, inner) for d in range(1, inner)]
    ypeers = [lax.rem(y + d, outer) * inner + z for d in range(1, outer)]
    g = c * n_row + r
    target_row = g // n_col
    my_slot = g % n_col
    targets = [(target_row, j) for j in range(n_col)]
    sources = []
    for s in range(n_col):
        gs = r * n_col + s
        sources.append((gs % n_row, gs // n_row))

    def differs(dev):
        return jnp.logical_or(dev[0] != r, dev[1] != c)

    barrier = pltpu.get_barrier_semaphore()
    for p in cpeers:
        pl.semaphore_signal(barrier, inc=1, device_id={"col": p}, device_id_type=MESH)
    for p in zpeers + ypeers:
        pl.semaphore_signal(barrier, inc=1, device_id={"row": p}, device_id_type=MESH)
    for dev in targets + sources:
        @pl.when(differs(dev))
        def _():
            pl.semaphore_signal(barrier, inc=1, device_id=dev, device_id_type=MESH)
    self_in = (target_row == r).astype(jnp.int32)
    pl.semaphore_wait(barrier, (n_col - 1) + (inner - 1) + (outer - 1) + 2 * (n_col - self_in))

    copies = []
    pltpu.make_async_copy(chunk_ref, colb3.at[r], e_recv_c.at[z]).start()
    for i, p in enumerate(zpeers):
        cp = pltpu.make_async_remote_copy(
            src_ref=chunk_ref, dst_ref=colb3.at[r], send_sem=e_send_z.at[i],
            recv_sem=e_recv_c.at[z], device_id={"row": p}, device_id_type=MESH)
        cp.start()
        copies.append(cp)
    row_copies = []
    for j, dev in enumerate(targets):
        cp = pltpu.make_async_remote_copy(
            src_ref=chunk_ref, dst_ref=rowb3.at[my_slot], send_sem=e_send_r.at[j],
            recv_sem=e_recv_r.at[my_slot], device_id=dev, device_id_type=MESH)
        row_copies.append(cp)

        @pl.when(differs(dev))
        def _():
            cp.start()

        @pl.when(jnp.logical_not(differs(dev)))
        def _():
            pltpu.make_async_copy(chunk_ref, rowb3.at[my_slot], e_recv_r.at[my_slot]).start()

    prefc[...] = jnp.broadcast_to(prefr_ref[...], (128, rows)).T
    for s in range(inner):
        pltpu.make_async_copy(chunk_ref, colb3.at[y * inner + s], e_recv_c.at[s]).wait()
    block = colb3.at[pl.ds(y * inner, inner)]
    for i, p in enumerate(ypeers):
        cp = pltpu.make_async_remote_copy(
            src_ref=block, dst_ref=block, send_sem=e_send_y.at[i],
            recv_sem=e_recv_b.at[y], device_id={"row": p}, device_id_type=MESH)
        cp.start()
        copies.append(cp)
    for d in range(1, outer):
        yo = lax.rem(y + d, outer)
        other = colb3.at[pl.ds(yo * inner, inner)]
        pltpu.make_async_copy(other, other, e_recv_b.at[yo]).wait()
    for s in range(n_col):
        pltpu.make_async_copy(chunk_ref, rowb3.at[s], e_recv_r.at[s]).wait()
    mol = chunk_ref.shape[0]
    colb_ref = colb3
    rowb_ref = rowb3

    def colb_rows(start, size):
        return colb_ref[pl.ds(start // mol, size // mol)].reshape(size, -1)

    def rowb_rows(start, size):
        return rowb_ref[pl.ds(start // mol, size // mol)].reshape(size, -1)

    row_start = r * rows
    col_start = c * cols
    n_chunks = rows // chunk
    col_ids = col_start + lax.broadcasted_iota(jnp.int32, (chunk, cols), 1)

    def diag_at(i0):
        row_ids = row_start + i0 + lax.broadcasted_iota(jnp.int32, (chunk, cols), 0)
        return row_ids == col_ids

    def record_top(i0, summed):
        first = jnp.max(summed, axis=1, keepdims=True)
        hits = summed == first
        repeats = jnp.sum(hits.astype(jnp.float32), axis=1, keepdims=True)
        others = jnp.max(jnp.where(hits, -jnp.inf, summed), axis=1, keepdims=True)
        second = jnp.where(repeats > 1.0, first, others)
        fcol[pl.ds(i0, chunk), :] = jnp.broadcast_to(first, (chunk, 128))
        scol[pl.ds(i0, chunk), :] = jnp.broadcast_to(second, (chunk, 128))

    colb_all = colb_ref[...].reshape(cols, -1)
    rowb_all = rowb_ref[...].reshape(rows, -1)
    cb = 128 if cols % 128 == 0 else cols
    for j in range(cols // cb):
        xc = colb_all[j * cb:(j + 1) * cb, :].astype(jnp.float32)
        qc = jnp.sum(xc * xc, axis=1, keepdims=True)
        cq[0:1, pl.ds(j * cb, cb)] = jnp.broadcast_to(qc, (cb, 128)).T[0:1, :]
    xr = rowb_all.astype(jnp.float32)
    rq_s = fcol
    rq_s[...] = jnp.broadcast_to(jnp.sum(xr * xr, axis=1, keepdims=True), (rows, 128))
    rb = 128 if rows % 128 == 0 else rows
    for j in range(rows // rb):
        sim_s[pl.ds(j * rb, rb), :] = lax.dot_general(
            rowb_all[j * rb:(j + 1) * rb, :], colb_all, (((1,), (1,)), ((), ())),
            preferred_element_type=jnp.float32)

    def sim_body(i, carry):
        i0 = pl.multiple_of(i * chunk, chunk)
        rq = rq_s[pl.ds(i0, chunk), 0:1]
        dist = 2.0 * sim_s[pl.ds(i0, chunk), :] - rq - cq[...]
        s = jnp.where(diag_at(i0), prefc[pl.ds(i0, chunk), 0:1], dist)
        sim_s[pl.ds(i0, chunk), :] = s
        record_top(i0, s)
        return carry

    lax.fori_loop(0, n_chunks, sim_body, 0)
    for step in range(iters):
        first_step = step == 0
        last_step = step == iters - 1
        resp_prev, avail_prev = resp_s, avail_s
        resp_new, avail_new = (resp_out, avail_out) if last_step else (resp_s, avail_s)
        pk = pack.at[step]
        pk[0:1, :] = fcol[...].T[0:1, :]
        pk[1:2, :] = scol[...].T[0:1, :]
        for k, dst in enumerate((buf_f.at[step], buf_s.at[step])):
            src = pk.at[pl.ds(k, 1)]
            pltpu.make_async_copy(src, dst.at[pl.ds(c, 1)], recv_t.at[step, k, c]).start()
            for i, p in enumerate(cpeers):
                cp = pltpu.make_async_remote_copy(
                    src_ref=src, dst_ref=dst.at[pl.ds(c, 1)], send_sem=send_t.at[step, k, i],
                    recv_sem=recv_t.at[step, k, c], device_id={"col": p}, device_id_type=MESH)
                cp.start()
                copies.append(cp)
        for k, dst in enumerate((buf_f.at[step], buf_s.at[step])):
            for s in range(n_col):
                pltpu.make_async_copy(pk.at[pl.ds(0, 1)], dst.at[pl.ds(s, 1)], recv_t.at[step, k, s]).wait()
        firsts = buf_f[step]
        seconds = buf_s[step]
        first = jnp.max(firsts, axis=0, keepdims=True)
        at_top = firsts == first
        repeats = jnp.sum(at_top.astype(jnp.float32), axis=0, keepdims=True)
        others = jnp.max(jnp.where(at_top, -jnp.inf, firsts), axis=0, keepdims=True)
        second = jnp.where(repeats > 1.0, first, jnp.maximum(jnp.max(seconds, axis=0, keepdims=True), others))
        fcol[...] = jnp.broadcast_to(first, (128, rows)).T
        scol[...] = jnp.broadcast_to(second, (128, rows)).T

        def resp_body(i, acc):
            i0 = pl.multiple_of(i * chunk, chunk)
            s = sim_s[pl.ds(i0, chunk), :]
            summed = s if first_step else avail_prev[pl.ds(i0, chunk), :] + s
            f = fcol[pl.ds(i0, chunk), 0:1]
            sc = scol[pl.ds(i0, chunk), 0:1]
            fresh = s - jnp.where(summed == f, sc, f)
            if first_step:
                resp = (1.0 - DAMPING) * fresh
            else:
                resp = DAMPING * resp_prev[pl.ds(i0, chunk), :] + (1.0 - DAMPING) * fresh
            resp_new[pl.ds(i0, chunk), :] = resp
            positive = jnp.where(diag_at(i0), resp, jnp.maximum(resp, 0.0))
            return acc + jnp.sum(positive, axis=0, keepdims=True)

        zp = zpart.at[step]
        zp[...] = lax.fori_loop(0, n_chunks, resp_body, jnp.zeros((1, cols), jnp.float32))

        b1 = buf1.at[step]
        pltpu.make_async_copy(zp, b1.at[pl.ds(z, 1)], recv_z.at[step, z]).start()
        for i, p in enumerate(zpeers):
            cp = pltpu.make_async_remote_copy(
                src_ref=zp, dst_ref=b1.at[pl.ds(z, 1)], send_sem=send_z.at[step, i],
                recv_sem=recv_z.at[step, z], device_id={"row": p}, device_id_type=MESH)
            cp.start()
            copies.append(cp)
        for s in range(inner):
            pltpu.make_async_copy(zp, b1.at[pl.ds(s, 1)], recv_z.at[step, s]).wait()
        zs = zsum.at[step]
        zs[...] = jnp.sum(b1[...], axis=0, keepdims=True)
        b2 = buf2.at[step]
        pltpu.make_async_copy(zs, b2.at[pl.ds(y, 1)], recv_y.at[step, y]).start()
        for i, p in enumerate(ypeers):
            cp = pltpu.make_async_remote_copy(
                src_ref=zs, dst_ref=b2.at[pl.ds(y, 1)], send_sem=send_y.at[step, i],
                recv_sem=recv_y.at[step, y], device_id={"row": p}, device_id_type=MESH)
            cp.start()
            copies.append(cp)
        for s in range(outer):
            pltpu.make_async_copy(zs, b2.at[pl.ds(s, 1)], recv_y.at[step, s]).wait()
        colsum = jnp.sum(b2[...], axis=0, keepdims=True)

        def avail_body(i, carry):
            i0 = pl.multiple_of(i * chunk, chunk)
            resp = resp_new[pl.ds(i0, chunk), :]
            diag = diag_at(i0)
            positive = jnp.where(diag, resp, jnp.maximum(resp, 0.0))
            renew = colsum - positive
            renew = jnp.where(diag, renew, jnp.minimum(renew, 0.0))
            if first_step:
                avail = (1.0 - DAMPING) * renew
            else:
                avail = DAMPING * avail_prev[pl.ds(i0, chunk), :] + (1.0 - DAMPING) * renew
            avail_new[pl.ds(i0, chunk), :] = avail
            if not last_step:
                record_top(i0, avail + sim_s[pl.ds(i0, chunk), :])
            return carry

        lax.fori_loop(0, n_chunks, avail_body, 0)
    for cp in copies:
        cp.wait_send()
    for j, dev in enumerate(targets):
        @pl.when(differs(dev))
        def _():
            row_copies[j].wait_send()


def propagate(chunk, pref_row, n_row, n_col, inner, iters, cid):
    mol, width = chunk.shape
    rows, cols = mol * n_col, mol * n_row
    outer = n_row // inner
    f32 = jnp.float32
    return pl.pallas_call(
        functools.partial(ap_kernel, n_row, n_col, inner, 32, iters),
        out_shape=(jax.ShapeDtypeStruct((rows, cols), f32), jax.ShapeDtypeStruct((rows, cols), f32)),
        in_specs=[VMEM] * 2,
        out_specs=(VMEM, VMEM),
        scratch_shapes=[
            pltpu.VMEM((n_row, mol, width), chunk.dtype),
            pltpu.VMEM((n_col, mol, width), chunk.dtype),
            pltpu.VMEM((rows, 128), f32),
            pltpu.VMEM((rows, cols), f32),
            pltpu.VMEM((rows, cols), f32),
            pltpu.VMEM((rows, cols), f32),
            pltpu.VMEM((rows, 128), f32),
            pltpu.VMEM((rows, 128), f32),
            pltpu.VMEM((1, cols), f32),
            pltpu.VMEM((iters, 2, rows), f32),
            pltpu.VMEM((iters, n_col, rows), f32),
            pltpu.VMEM((iters, n_col, rows), f32),
            pltpu.VMEM((iters, 1, cols), f32),
            pltpu.VMEM((iters, inner, cols), f32),
            pltpu.VMEM((iters, 1, cols), f32),
            pltpu.VMEM((iters, outer, cols), f32),
            pltpu.SemaphoreType.DMA((inner - 1,)),
            pltpu.SemaphoreType.DMA((outer - 1,)),
            pltpu.SemaphoreType.DMA((n_col,)),
            pltpu.SemaphoreType.DMA((inner,)),
            pltpu.SemaphoreType.DMA((outer,)),
            pltpu.SemaphoreType.DMA((n_col,)),
            pltpu.SemaphoreType.DMA((iters, 2, n_col - 1)),
            pltpu.SemaphoreType.DMA((iters, 2, n_col)),
            pltpu.SemaphoreType.DMA((iters, inner - 1)),
            pltpu.SemaphoreType.DMA((iters, outer - 1)),
            pltpu.SemaphoreType.DMA((iters, inner)),
            pltpu.SemaphoreType.DMA((iters, outer)),
        ],
        compiler_params=pltpu.CompilerParams(
            collective_id=cid, has_side_effects=True, vmem_limit_bytes=60 * 1024 * 1024),
    )(chunk, pref_row)


def similarity(row_emb, col_emb, row_start, col_start, pref_rows):
    cross = lax.dot_general(
        row_emb, col_emb, (((1,), (1,)), ((), ())), preferred_element_type=jnp.float32
    )
    row_vals = row_emb.astype(jnp.float32)
    col_vals = col_emb.astype(jnp.float32)
    row_sq = jnp.sum(row_vals * row_vals, axis=1)
    col_sq = jnp.sum(col_vals * col_vals, axis=1)
    dist = 2.0 * cross - row_sq[:, None] - col_sq[None, :]
    row_ids = row_start + jnp.arange(row_emb.shape[0], dtype=jnp.int32)
    col_ids = col_start + jnp.arange(col_emb.shape[0], dtype=jnp.int32)
    diagonal = row_ids[:, None] == col_ids[None, :]
    return (jnp.where(diagonal, pref_rows[:, None], dist), diagonal)


def top_two(summed):
    first = jnp.max(summed, axis=1)
    hits = summed == first[:, None]
    repeats = jnp.sum(hits.astype(jnp.int32), axis=1)
    others = jnp.max(jnp.where(hits, -jnp.inf, summed), axis=1)
    second = jnp.where(repeats > 1, first, others)
    return (first, second)


def local(embedding, preference):
    rows_n = lax.axis_size("row")
    cols_n = lax.axis_size("col")
    row_idx = lax.axis_index("row")
    col_idx = lax.axis_index("col")
    mol = embedding.shape[2]
    width = embedding.shape[3]
    row_count = mol * cols_n
    col_count = mol * rows_n
    resp, avail = propagate(embedding.reshape(mol, width), preference.reshape(1, row_count), rows_n, cols_n, INNER, ITERS, 0)
    return (resp, avail)


def solution(mesh):
    placed = (P("col", "row", None, None), P("row"))
    return jax.shard_map(
        local,
        mesh=mesh,
        in_specs=placed,
        out_specs=(P("row", "col"), P("row", "col")),
        check_vma=False,
    )
```

```python
import functools

import jax
import jax.numpy as jnp
from jax import lax
from jax.experimental import pallas as pl
from jax.experimental.pallas import tpu as pltpu
from jax.sharding import PartitionSpec as P

ITERS = 2


DAMPING = 0.5

INNER = 8

MESH = pl.DeviceIdType.MESH
VMEM = pl.BlockSpec(memory_space=pltpu.VMEM)


def params(cid):
    return pltpu.CompilerParams(collective_id=cid, has_side_effects=True)


def embed_kernel(n_row, n_col, inner, chunk_ref, colb_ref, rowb_ref, send_z, send_y, send_r, recv_c, recv_b, recv_r):
    r = lax.axis_index("row")
    c = lax.axis_index("col")
    outer = n_row // inner
    y = r // inner
    z = r % inner
    g = c * n_row + r
    target_row = g // n_col
    my_slot = g % n_col
    zpeers = [(y * inner + lax.rem(z + d, inner), c) for d in range(1, inner)]
    ypeers = [(lax.rem(y + d, outer) * inner + z, c) for d in range(1, outer)]
    targets = [(target_row, j) for j in range(n_col)]
    sources = []
    for s in range(n_col):
        gs = r * n_col + s
        sources.append((gs % n_row, gs // n_row))

    def differs(dev):
        return jnp.logical_or(dev[0] != r, dev[1] != c)

    barrier = pltpu.get_barrier_semaphore()
    for dev in zpeers + ypeers:
        pl.semaphore_signal(barrier, inc=1, device_id=dev, device_id_type=MESH)
    for dev in targets + sources:
        @pl.when(differs(dev))
        def _():
            pl.semaphore_signal(barrier, inc=1, device_id=dev, device_id_type=MESH)
    self_in = (target_row == r).astype(jnp.int32)
    pl.semaphore_wait(barrier, (inner - 1) + (outer - 1) + 2 * (n_col - self_in))

    pltpu.make_async_copy(chunk_ref, colb_ref.at[r], recv_c.at[z]).start()
    zcopies = []
    for i, dev in enumerate(zpeers):
        cp = pltpu.make_async_remote_copy(
            src_ref=chunk_ref, dst_ref=colb_ref.at[r], send_sem=send_z.at[i],
            recv_sem=recv_c.at[z], device_id=dev, device_id_type=MESH)
        cp.start()
        zcopies.append(cp)
    row_copies = []
    for j, dev in enumerate(targets):
        cp = pltpu.make_async_remote_copy(
            src_ref=chunk_ref, dst_ref=rowb_ref.at[my_slot], send_sem=send_r.at[j],
            recv_sem=recv_r.at[my_slot], device_id=dev, device_id_type=MESH)
        row_copies.append(cp)

        @pl.when(differs(dev))
        def _():
            cp.start()

        @pl.when(jnp.logical_not(differs(dev)))
        def _():
            pltpu.make_async_copy(chunk_ref, rowb_ref.at[my_slot], recv_r.at[my_slot]).start()

    for s in range(inner):
        pltpu.make_async_copy(chunk_ref, colb_ref.at[y * inner + s], recv_c.at[s]).wait()
    block = colb_ref.at[pl.ds(y * inner, inner)]
    ycopies = []
    for i, dev in enumerate(ypeers):
        cp = pltpu.make_async_remote_copy(
            src_ref=block, dst_ref=block, send_sem=send_y.at[i],
            recv_sem=recv_b.at[y], device_id=dev, device_id_type=MESH)
        cp.start()
        ycopies.append(cp)

    for cp in zcopies + ycopies:
        cp.wait_send()
    for j, dev in enumerate(targets):
        @pl.when(differs(dev))
        def _():
            row_copies[j].wait_send()
    for d in range(1, outer):
        yo = lax.rem(y + d, outer)
        other = colb_ref.at[pl.ds(yo * inner, inner)]
        pltpu.make_async_copy(other, other, recv_b.at[yo]).wait()
    for s in range(n_col):
        pltpu.make_async_copy(chunk_ref, rowb_ref.at[s], recv_r.at[s]).wait()


def distribute(chunk, n_row, n_col, inner):
    mol, width = chunk.shape
    outer = n_row // inner
    return pl.pallas_call(
        functools.partial(embed_kernel, n_row, n_col, inner),
        out_shape=(jax.ShapeDtypeStruct((n_row, mol, width), chunk.dtype),
                   jax.ShapeDtypeStruct((n_col, mol, width), chunk.dtype)),
        in_specs=[VMEM],
        out_specs=(VMEM, VMEM),
        scratch_shapes=[
            pltpu.SemaphoreType.DMA((inner - 1,)),
            pltpu.SemaphoreType.DMA((inner, outer - 1)),
            pltpu.SemaphoreType.DMA((n_col,)),
            pltpu.SemaphoreType.DMA((inner,)),
            pltpu.SemaphoreType.DMA((outer, inner)),
            pltpu.SemaphoreType.DMA((n_col,)),
        ],
        compiler_params=params(0),
    )(chunk)


def colsum_kernel(n, inner, part_ref, out_ref, buf1, zsum, buf2, send_z, send_y, recv_z, recv_y):
    r = lax.axis_index("row")
    outer = n // inner
    y = r // inner
    z = r % inner
    zpeers = [y * inner + lax.rem(z + d, inner) for d in range(1, inner)]
    ypeers = [lax.rem(y + d, outer) * inner + z for d in range(1, outer)]
    barrier = pltpu.get_barrier_semaphore()
    for p in zpeers + ypeers:
        pl.semaphore_signal(barrier, inc=1, device_id={"row": p}, device_id_type=MESH)
    pl.semaphore_wait(barrier, (inner - 1) + (outer - 1))
    pltpu.make_async_copy(part_ref, buf1.at[pl.ds(z, 1)], recv_z.at[z]).start()
    zcopies = []
    for i, p in enumerate(zpeers):
        cp = pltpu.make_async_remote_copy(
            src_ref=part_ref, dst_ref=buf1.at[pl.ds(z, 1)], send_sem=send_z.at[i],
            recv_sem=recv_z.at[z], device_id={"row": p}, device_id_type=MESH)
        cp.start()
        zcopies.append(cp)
    for s in range(inner):
        pltpu.make_async_copy(part_ref, buf1.at[pl.ds(s, 1)], recv_z.at[s]).wait()
    zsum[...] = jnp.sum(buf1[...], axis=0, keepdims=True)
    pltpu.make_async_copy(zsum, buf2.at[pl.ds(y, 1)], recv_y.at[y]).start()
    ycopies = []
    for i, p in enumerate(ypeers):
        cp = pltpu.make_async_remote_copy(
            src_ref=zsum, dst_ref=buf2.at[pl.ds(y, 1)], send_sem=send_y.at[i],
            recv_sem=recv_y.at[y], device_id={"row": p}, device_id_type=MESH)
        cp.start()
        ycopies.append(cp)
    for cp in zcopies + ycopies:
        cp.wait_send()
    for s in range(outer):
        pltpu.make_async_copy(zsum, buf2.at[pl.ds(s, 1)], recv_y.at[s]).wait()
    out_ref[...] = jnp.sum(buf2[...], axis=0, keepdims=True)


def row_sum(part, n, inner, cid):
    outer = n // inner
    width = part.shape[1]
    return pl.pallas_call(
        functools.partial(colsum_kernel, n, inner),
        out_shape=jax.ShapeDtypeStruct((1, width), part.dtype),
        in_specs=[VMEM],
        out_specs=VMEM,
        scratch_shapes=[
            pltpu.VMEM((inner, width), part.dtype),
            pltpu.VMEM((1, width), part.dtype),
            pltpu.VMEM((outer, width), part.dtype),
            pltpu.SemaphoreType.DMA((inner - 1,)),
            pltpu.SemaphoreType.DMA((outer - 1,)),
            pltpu.SemaphoreType.DMA((inner,)),
            pltpu.SemaphoreType.DMA((outer,)),
        ],
        compiler_params=params(cid),
    )(part)


def gather_kernel(axis, n, src_ref, out_ref, send_sem, recv_sem):
    me = lax.axis_index(axis)
    peers = [lax.rem(me + d, n) for d in range(1, n)]
    barrier = pltpu.get_barrier_semaphore()
    for p in peers:
        pl.semaphore_signal(barrier, inc=1, device_id={axis: p}, device_id_type=MESH)
    pl.semaphore_wait(barrier, n - 1)
    pltpu.make_async_copy(src_ref, out_ref.at[me], recv_sem.at[me]).start()
    copies = []
    for i, p in enumerate(peers):
        cp = pltpu.make_async_remote_copy(
            src_ref=src_ref, dst_ref=out_ref.at[me], send_sem=send_sem.at[i],
            recv_sem=recv_sem.at[me], device_id={axis: p}, device_id_type=MESH)
        cp.start()
        copies.append(cp)
    for cp in copies:
        cp.wait_send()
    for s in range(n):
        pltpu.make_async_copy(src_ref, out_ref.at[s], recv_sem.at[s]).wait()


def gather(x, axis, n, cid):
    return pl.pallas_call(
        functools.partial(gather_kernel, axis, n),
        out_shape=jax.ShapeDtypeStruct((n,) + x.shape, x.dtype),
        in_specs=[VMEM],
        out_specs=VMEM,
        scratch_shapes=[
            pltpu.SemaphoreType.DMA((n - 1,)),
            pltpu.SemaphoreType.DMA((n,)),
        ],
        compiler_params=params(cid),
    )(x)


def ap_kernel(n_row, n_col, inner, chunk, iters, chunk_ref, prefr_ref, resp_out, avail_out,
              colb3, rowb3, prefc, sim_s, resp_s, avail_s, fcol, scol, cq, pack, buf_f, buf_s, zpart, buf1,
              zsum, buf2, e_send_z, e_send_y, e_send_r, e_recv_c, e_recv_b, e_recv_r,
              send_t, recv_t, send_z, send_y, recv_z, recv_y):
    rows, cols = sim_s.shape
    r = lax.axis_index("row")
    c = lax.axis_index("col")
    outer = n_row // inner
    y = r // inner
    z = r % inner
    cpeers = [lax.rem(c + d, n_col) for d in range(1, n_col)]
    zpeers = [y * inner + lax.rem(z + d, inner) for d in range(1, inner)]
    ypeers = [lax.rem(y + d, outer) * inner + z for d in range(1, outer)]
    g = c * n_row + r
    target_row = g // n_col
    my_slot = g % n_col
    targets = [(target_row, j) for j in range(n_col)]
    sources = []
    for s in range(n_col):
        gs = r * n_col + s
        sources.append((gs % n_row, gs // n_row))

    def differs(dev):
        return jnp.logical_or(dev[0] != r, dev[1] != c)

    barrier = pltpu.get_barrier_semaphore()
    for p in cpeers:
        pl.semaphore_signal(barrier, inc=1, device_id={"col": p}, device_id_type=MESH)
    for p in zpeers + ypeers:
        pl.semaphore_signal(barrier, inc=1, device_id={"row": p}, device_id_type=MESH)
    for dev in targets + sources:
        @pl.when(differs(dev))
        def _():
            pl.semaphore_signal(barrier, inc=1, device_id=dev, device_id_type=MESH)
    self_in = (target_row == r).astype(jnp.int32)
    pl.semaphore_wait(barrier, (n_col - 1) + (inner - 1) + (outer - 1) + 2 * (n_col - self_in))

    copies = []
    pltpu.make_async_copy(chunk_ref, colb3.at[r], e_recv_c.at[z]).start()
    for i, p in enumerate(zpeers):
        cp = pltpu.make_async_remote_copy(
            src_ref=chunk_ref, dst_ref=colb3.at[r], send_sem=e_send_z.at[i],
            recv_sem=e_recv_c.at[z], device_id={"row": p}, device_id_type=MESH)
        cp.start()
        copies.append(cp)
    row_copies = []
    for j, dev in enumerate(targets):
        cp = pltpu.make_async_remote_copy(
            src_ref=chunk_ref, dst_ref=rowb3.at[my_slot], send_sem=e_send_r.at[j],
            recv_sem=e_recv_r.at[my_slot], device_id=dev, device_id_type=MESH)
        row_copies.append(cp)

        @pl.when(differs(dev))
        def _():
            cp.start()

        @pl.when(jnp.logical_not(differs(dev)))
        def _():
            pltpu.make_async_copy(chunk_ref, rowb3.at[my_slot], e_recv_r.at[my_slot]).start()

    prefc[...] = jnp.broadcast_to(prefr_ref[...], (128, rows)).T
    for d in range(inner):
        zs = lax.rem(z + d, inner)
        slot = colb3.at[y * inner + zs]
        pltpu.make_async_copy(chunk_ref, slot, e_recv_c.at[zs]).wait()
        for i, p in enumerate(ypeers):
            cp = pltpu.make_async_remote_copy(
                src_ref=slot, dst_ref=slot, send_sem=e_send_y.at[d, i],
                recv_sem=e_recv_b.at[y, zs], device_id={"row": p}, device_id_type=MESH)
            cp.start()
            copies.append(cp)
    for d in range(1, outer):
        yo = lax.rem(y + d, outer)
        for s in range(inner):
            other = colb3.at[yo * inner + s]
            pltpu.make_async_copy(other, other, e_recv_b.at[yo, s]).wait()
    for s in range(n_col):
        pltpu.make_async_copy(chunk_ref, rowb3.at[s], e_recv_r.at[s]).wait()
    mol = chunk_ref.shape[0]
    colb_ref = colb3
    rowb_ref = rowb3

    def colb_rows(start, size):
        return colb_ref[pl.ds(start // mol, size // mol)].reshape(size, -1)

    def rowb_rows(start, size):
        return rowb_ref[pl.ds(start // mol, size // mol)].reshape(size, -1)

    row_start = r * rows
    col_start = c * cols
    n_chunks = rows // chunk
    col_ids = col_start + lax.broadcasted_iota(jnp.int32, (chunk, cols), 1)

    def diag_at(i0):
        row_ids = row_start + i0 + lax.broadcasted_iota(jnp.int32, (chunk, cols), 0)
        return row_ids == col_ids

    def record_top(i0, summed):
        first = jnp.max(summed, axis=1, keepdims=True)
        hits = summed == first
        repeats = jnp.sum(hits.astype(jnp.float32), axis=1, keepdims=True)
        others = jnp.max(jnp.where(hits, -jnp.inf, summed), axis=1, keepdims=True)
        second = jnp.where(repeats > 1.0, first, others)
        fcol[pl.ds(i0, chunk), :] = jnp.broadcast_to(first, (chunk, 128))
        scol[pl.ds(i0, chunk), :] = jnp.broadcast_to(second, (chunk, 128))

    colb_all = colb_ref[...].reshape(cols, -1)
    rowb_all = rowb_ref[...].reshape(rows, -1)
    cb = 128 if cols % 128 == 0 else cols
    for j in range(cols // cb):
        xc = colb_all[j * cb:(j + 1) * cb, :].astype(jnp.float32)
        qc = jnp.sum(xc * xc, axis=1, keepdims=True)
        cq[0:1, pl.ds(j * cb, cb)] = jnp.broadcast_to(qc, (cb, 128)).T[0:1, :]
    xr = rowb_all.astype(jnp.float32)
    rq_s = fcol
    rq_s[...] = jnp.broadcast_to(jnp.sum(xr * xr, axis=1, keepdims=True), (rows, 128))
    rb = 128 if rows % 128 == 0 else rows
    for j in range(rows // rb):
        sim_s[pl.ds(j * rb, rb), :] = lax.dot_general(
            rowb_all[j * rb:(j + 1) * rb, :], colb_all, (((1,), (1,)), ((), ())),
            preferred_element_type=jnp.float32)

    def sim_body(i, carry):
        i0 = pl.multiple_of(i * chunk, chunk)
        rq = rq_s[pl.ds(i0, chunk), 0:1]
        dist = 2.0 * sim_s[pl.ds(i0, chunk), :] - rq - cq[...]
        s = jnp.where(diag_at(i0), prefc[pl.ds(i0, chunk), 0:1], dist)
        sim_s[pl.ds(i0, chunk), :] = s
        record_top(i0, s)
        return carry

    lax.fori_loop(0, n_chunks, sim_body, 0)
    for step in range(iters):
        first_step = step == 0
        last_step = step == iters - 1
        resp_prev, avail_prev = resp_s, avail_s
        resp_new, avail_new = (resp_out, avail_out) if last_step else (resp_s, avail_s)
        pk = pack.at[step]
        pk[0:1, :] = fcol[...].T[0:1, :]
        pk[1:2, :] = scol[...].T[0:1, :]
        for k, dst in enumerate((buf_f.at[step], buf_s.at[step])):
            src = pk.at[pl.ds(k, 1)]
            pltpu.make_async_copy(src, dst.at[pl.ds(c, 1)], recv_t.at[step, k, c]).start()
            for i, p in enumerate(cpeers):
                cp = pltpu.make_async_remote_copy(
                    src_ref=src, dst_ref=dst.at[pl.ds(c, 1)], send_sem=send_t.at[step, k, i],
                    recv_sem=recv_t.at[step, k, c], device_id={"col": p}, device_id_type=MESH)
                cp.start()
                copies.append(cp)
        for k, dst in enumerate((buf_f.at[step], buf_s.at[step])):
            for s in range(n_col):
                pltpu.make_async_copy(pk.at[pl.ds(0, 1)], dst.at[pl.ds(s, 1)], recv_t.at[step, k, s]).wait()
        firsts = buf_f[step]
        seconds = buf_s[step]
        first = jnp.max(firsts, axis=0, keepdims=True)
        at_top = firsts == first
        repeats = jnp.sum(at_top.astype(jnp.float32), axis=0, keepdims=True)
        others = jnp.max(jnp.where(at_top, -jnp.inf, firsts), axis=0, keepdims=True)
        second = jnp.where(repeats > 1.0, first, jnp.maximum(jnp.max(seconds, axis=0, keepdims=True), others))
        fcol[...] = jnp.broadcast_to(first, (128, rows)).T
        scol[...] = jnp.broadcast_to(second, (128, rows)).T

        def resp_body(i, acc):
            i0 = pl.multiple_of(i * chunk, chunk)
            s = sim_s[pl.ds(i0, chunk), :]
            summed = s if first_step else avail_prev[pl.ds(i0, chunk), :] + s
            f = fcol[pl.ds(i0, chunk), 0:1]
            sc = scol[pl.ds(i0, chunk), 0:1]
            fresh = s - jnp.where(summed == f, sc, f)
            if first_step:
                resp = (1.0 - DAMPING) * fresh
            else:
                resp = DAMPING * resp_prev[pl.ds(i0, chunk), :] + (1.0 - DAMPING) * fresh
            resp_new[pl.ds(i0, chunk), :] = resp
            positive = jnp.where(diag_at(i0), resp, jnp.maximum(resp, 0.0))
            return acc + jnp.sum(positive, axis=0, keepdims=True)

        zp = zpart.at[step]
        zp[...] = lax.fori_loop(0, n_chunks, resp_body, jnp.zeros((1, cols), jnp.float32))

        b1 = buf1.at[step]
        pltpu.make_async_copy(zp, b1.at[pl.ds(z, 1)], recv_z.at[step, z]).start()
        for i, p in enumerate(zpeers):
            cp = pltpu.make_async_remote_copy(
                src_ref=zp, dst_ref=b1.at[pl.ds(z, 1)], send_sem=send_z.at[step, i],
                recv_sem=recv_z.at[step, z], device_id={"row": p}, device_id_type=MESH)
            cp.start()
            copies.append(cp)
        for s in range(inner):
            pltpu.make_async_copy(zp, b1.at[pl.ds(s, 1)], recv_z.at[step, s]).wait()
        zs = zsum.at[step]
        zs[...] = jnp.sum(b1[...], axis=0, keepdims=True)
        b2 = buf2.at[step]
        pltpu.make_async_copy(zs, b2.at[pl.ds(y, 1)], recv_y.at[step, y]).start()
        for i, p in enumerate(ypeers):
            cp = pltpu.make_async_remote_copy(
                src_ref=zs, dst_ref=b2.at[pl.ds(y, 1)], send_sem=send_y.at[step, i],
                recv_sem=recv_y.at[step, y], device_id={"row": p}, device_id_type=MESH)
            cp.start()
            copies.append(cp)
        for s in range(outer):
            pltpu.make_async_copy(zs, b2.at[pl.ds(s, 1)], recv_y.at[step, s]).wait()
        colsum = jnp.sum(b2[...], axis=0, keepdims=True)

        def avail_body(i, carry):
            i0 = pl.multiple_of(i * chunk, chunk)
            resp = resp_new[pl.ds(i0, chunk), :]
            diag = diag_at(i0)
            positive = jnp.where(diag, resp, jnp.maximum(resp, 0.0))
            renew = colsum - positive
            renew = jnp.where(diag, renew, jnp.minimum(renew, 0.0))
            if first_step:
                avail = (1.0 - DAMPING) * renew
            else:
                avail = DAMPING * avail_prev[pl.ds(i0, chunk), :] + (1.0 - DAMPING) * renew
            avail_new[pl.ds(i0, chunk), :] = avail
            if not last_step:
                record_top(i0, avail + sim_s[pl.ds(i0, chunk), :])
            return carry

        lax.fori_loop(0, n_chunks, avail_body, 0)
    for cp in copies:
        cp.wait_send()
    for j, dev in enumerate(targets):
        @pl.when(differs(dev))
        def _():
            row_copies[j].wait_send()


def propagate(chunk, pref_row, n_row, n_col, inner, iters, cid):
    mol, width = chunk.shape
    rows, cols = mol * n_col, mol * n_row
    outer = n_row // inner
    f32 = jnp.float32
    return pl.pallas_call(
        functools.partial(ap_kernel, n_row, n_col, inner, 32, iters),
        out_shape=(jax.ShapeDtypeStruct((rows, cols), f32), jax.ShapeDtypeStruct((rows, cols), f32)),
        in_specs=[VMEM] * 2,
        out_specs=(VMEM, VMEM),
        scratch_shapes=[
            pltpu.VMEM((n_row, mol, width), chunk.dtype),
            pltpu.VMEM((n_col, mol, width), chunk.dtype),
            pltpu.VMEM((rows, 128), f32),
            pltpu.VMEM((rows, cols), f32),
            pltpu.VMEM((rows, cols), f32),
            pltpu.VMEM((rows, cols), f32),
            pltpu.VMEM((rows, 128), f32),
            pltpu.VMEM((rows, 128), f32),
            pltpu.VMEM((1, cols), f32),
            pltpu.VMEM((iters, 2, rows), f32),
            pltpu.VMEM((iters, n_col, rows), f32),
            pltpu.VMEM((iters, n_col, rows), f32),
            pltpu.VMEM((iters, 1, cols), f32),
            pltpu.VMEM((iters, inner, cols), f32),
            pltpu.VMEM((iters, 1, cols), f32),
            pltpu.VMEM((iters, outer, cols), f32),
            pltpu.SemaphoreType.DMA((inner - 1,)),
            pltpu.SemaphoreType.DMA((inner, outer - 1)),
            pltpu.SemaphoreType.DMA((n_col,)),
            pltpu.SemaphoreType.DMA((inner,)),
            pltpu.SemaphoreType.DMA((outer, inner)),
            pltpu.SemaphoreType.DMA((n_col,)),
            pltpu.SemaphoreType.DMA((iters, 2, n_col - 1)),
            pltpu.SemaphoreType.DMA((iters, 2, n_col)),
            pltpu.SemaphoreType.DMA((iters, inner - 1)),
            pltpu.SemaphoreType.DMA((iters, outer - 1)),
            pltpu.SemaphoreType.DMA((iters, inner)),
            pltpu.SemaphoreType.DMA((iters, outer)),
        ],
        compiler_params=pltpu.CompilerParams(
            collective_id=cid, has_side_effects=True, vmem_limit_bytes=60 * 1024 * 1024),
    )(chunk, pref_row)


def similarity(row_emb, col_emb, row_start, col_start, pref_rows):
    cross = lax.dot_general(
        row_emb, col_emb, (((1,), (1,)), ((), ())), preferred_element_type=jnp.float32
    )
    row_vals = row_emb.astype(jnp.float32)
    col_vals = col_emb.astype(jnp.float32)
    row_sq = jnp.sum(row_vals * row_vals, axis=1)
    col_sq = jnp.sum(col_vals * col_vals, axis=1)
    dist = 2.0 * cross - row_sq[:, None] - col_sq[None, :]
    row_ids = row_start + jnp.arange(row_emb.shape[0], dtype=jnp.int32)
    col_ids = col_start + jnp.arange(col_emb.shape[0], dtype=jnp.int32)
    diagonal = row_ids[:, None] == col_ids[None, :]
    return (jnp.where(diagonal, pref_rows[:, None], dist), diagonal)


def top_two(summed):
    first = jnp.max(summed, axis=1)
    hits = summed == first[:, None]
    repeats = jnp.sum(hits.astype(jnp.int32), axis=1)
    others = jnp.max(jnp.where(hits, -jnp.inf, summed), axis=1)
    second = jnp.where(repeats > 1, first, others)
    return (first, second)


def local(embedding, preference):
    rows_n = lax.axis_size("row")
    cols_n = lax.axis_size("col")
    row_idx = lax.axis_index("row")
    col_idx = lax.axis_index("col")
    mol = embedding.shape[2]
    width = embedding.shape[3]
    row_count = mol * cols_n
    col_count = mol * rows_n
    resp, avail = propagate(embedding.reshape(mol, width), preference.reshape(1, row_count), rows_n, cols_n, INNER, ITERS, 0)
    return (resp, avail)


def solution(mesh):
    placed = (P("col", "row", None, None), P("row"))
    return jax.shard_map(
        local,
        mesh=mesh,
        in_specs=placed,
        out_specs=(P("row", "col"), P("row", "col")),
        check_vma=False,
    )
```

```python
import functools

import jax
import jax.numpy as jnp
from jax import lax
from jax.experimental import pallas as pl
from jax.experimental.pallas import tpu as pltpu
from jax.sharding import PartitionSpec as P

ITERS = 2


DAMPING = 0.5

INNER = 8

MESH = pl.DeviceIdType.MESH
VMEM = pl.BlockSpec(memory_space=pltpu.VMEM)


def params(cid):
    return pltpu.CompilerParams(collective_id=cid, has_side_effects=True)


def embed_kernel(n_row, n_col, inner, chunk_ref, colb_ref, rowb_ref, send_z, send_y, send_r, recv_c, recv_b, recv_r):
    r = lax.axis_index("row")
    c = lax.axis_index("col")
    outer = n_row // inner
    y = r // inner
    z = r % inner
    g = c * n_row + r
    target_row = g // n_col
    my_slot = g % n_col
    zpeers = [(y * inner + lax.rem(z + d, inner), c) for d in range(1, inner)]
    ypeers = [(lax.rem(y + d, outer) * inner + z, c) for d in range(1, outer)]
    parity = c % 2
    sibling = c + 1 - 2 * parity
    targets = [(target_row, 2 * x + my_slot % 2) for x in range(n_col // 2)]
    sources = []
    for t in range(n_col // 2):
        gs = r * n_col + 2 * t + parity
        sources.append((gs % n_row, gs // n_row))

    def differs(dev):
        return jnp.logical_or(dev[0] != r, dev[1] != c)

    barrier = pltpu.get_barrier_semaphore()
    for dev in zpeers + ypeers:
        pl.semaphore_signal(barrier, inc=1, device_id=dev, device_id_type=MESH)
    for dev in targets + sources:
        @pl.when(differs(dev))
        def _():
            pl.semaphore_signal(barrier, inc=1, device_id=dev, device_id_type=MESH)
    self_in = (target_row == r).astype(jnp.int32)
    pl.semaphore_wait(barrier, (inner - 1) + (outer - 1) + 2 * (n_col - self_in))

    pltpu.make_async_copy(chunk_ref, colb_ref.at[r], recv_c.at[z]).start()
    zcopies = []
    for i, dev in enumerate(zpeers):
        cp = pltpu.make_async_remote_copy(
            src_ref=chunk_ref, dst_ref=colb_ref.at[r], send_sem=send_z.at[i],
            recv_sem=recv_c.at[z], device_id=dev, device_id_type=MESH)
        cp.start()
        zcopies.append(cp)
    row_copies = []
    for j, dev in enumerate(targets):
        cp = pltpu.make_async_remote_copy(
            src_ref=chunk_ref, dst_ref=rowb_ref.at[my_slot], send_sem=send_r.at[j],
            recv_sem=recv_r.at[my_slot], device_id=dev, device_id_type=MESH)
        row_copies.append(cp)

        @pl.when(differs(dev))
        def _():
            cp.start()

        @pl.when(jnp.logical_not(differs(dev)))
        def _():
            pltpu.make_async_copy(chunk_ref, rowb_ref.at[my_slot], recv_r.at[my_slot]).start()

    for s in range(inner):
        pltpu.make_async_copy(chunk_ref, colb_ref.at[y * inner + s], recv_c.at[s]).wait()
    block = colb_ref.at[pl.ds(y * inner, inner)]
    ycopies = []
    for i, dev in enumerate(ypeers):
        cp = pltpu.make_async_remote_copy(
            src_ref=block, dst_ref=block, send_sem=send_y.at[i],
            recv_sem=recv_b.at[y], device_id=dev, device_id_type=MESH)
        cp.start()
        ycopies.append(cp)

    for cp in zcopies + ycopies:
        cp.wait_send()
    for j, dev in enumerate(targets):
        @pl.when(differs(dev))
        def _():
            row_copies[j].wait_send()
    for d in range(1, outer):
        yo = lax.rem(y + d, outer)
        other = colb_ref.at[pl.ds(yo * inner, inner)]
        pltpu.make_async_copy(other, other, recv_b.at[yo]).wait()
    for s in range(n_col):
        pltpu.make_async_copy(chunk_ref, rowb_ref.at[s], recv_r.at[s]).wait()


def distribute(chunk, n_row, n_col, inner):
    mol, width = chunk.shape
    outer = n_row // inner
    return pl.pallas_call(
        functools.partial(embed_kernel, n_row, n_col, inner),
        out_shape=(jax.ShapeDtypeStruct((n_row, mol, width), chunk.dtype),
                   jax.ShapeDtypeStruct((n_col, mol, width), chunk.dtype)),
        in_specs=[VMEM],
        out_specs=(VMEM, VMEM),
        scratch_shapes=[
            pltpu.SemaphoreType.DMA((inner - 1,)),
            pltpu.SemaphoreType.DMA((inner, outer - 1)),
            pltpu.SemaphoreType.DMA((n_col // 2,)),
            pltpu.SemaphoreType.DMA((n_col // 2,)),
            pltpu.SemaphoreType.DMA((inner,)),
            pltpu.SemaphoreType.DMA((outer, inner)),
            pltpu.SemaphoreType.DMA((n_col,)),
        ],
        compiler_params=params(0),
    )(chunk)


def colsum_kernel(n, inner, part_ref, out_ref, buf1, zsum, buf2, send_z, send_y, recv_z, recv_y):
    r = lax.axis_index("row")
    outer = n // inner
    y = r // inner
    z = r % inner
    zpeers = [y * inner + lax.rem(z + d, inner) for d in range(1, inner)]
    ypeers = [lax.rem(y + d, outer) * inner + z for d in range(1, outer)]
    barrier = pltpu.get_barrier_semaphore()
    for p in zpeers + ypeers:
        pl.semaphore_signal(barrier, inc=1, device_id={"row": p}, device_id_type=MESH)
    pl.semaphore_wait(barrier, (inner - 1) + (outer - 1))
    pltpu.make_async_copy(part_ref, buf1.at[pl.ds(z, 1)], recv_z.at[z]).start()
    zcopies = []
    for i, p in enumerate(zpeers):
        cp = pltpu.make_async_remote_copy(
            src_ref=part_ref, dst_ref=buf1.at[pl.ds(z, 1)], send_sem=send_z.at[i],
            recv_sem=recv_z.at[z], device_id={"row": p}, device_id_type=MESH)
        cp.start()
        zcopies.append(cp)
    for s in range(inner):
        pltpu.make_async_copy(part_ref, buf1.at[pl.ds(s, 1)], recv_z.at[s]).wait()
    zsum[...] = jnp.sum(buf1[...], axis=0, keepdims=True)
    pltpu.make_async_copy(zsum, buf2.at[pl.ds(y, 1)], recv_y.at[y]).start()
    ycopies = []
    for i, p in enumerate(ypeers):
        cp = pltpu.make_async_remote_copy(
            src_ref=zsum, dst_ref=buf2.at[pl.ds(y, 1)], send_sem=send_y.at[i],
            recv_sem=recv_y.at[y], device_id={"row": p}, device_id_type=MESH)
        cp.start()
        ycopies.append(cp)
    for cp in zcopies + ycopies:
        cp.wait_send()
    for s in range(outer):
        pltpu.make_async_copy(zsum, buf2.at[pl.ds(s, 1)], recv_y.at[s]).wait()
    out_ref[...] = jnp.sum(buf2[...], axis=0, keepdims=True)


def row_sum(part, n, inner, cid):
    outer = n // inner
    width = part.shape[1]
    return pl.pallas_call(
        functools.partial(colsum_kernel, n, inner),
        out_shape=jax.ShapeDtypeStruct((1, width), part.dtype),
        in_specs=[VMEM],
        out_specs=VMEM,
        scratch_shapes=[
            pltpu.VMEM((inner, width), part.dtype),
            pltpu.VMEM((1, width), part.dtype),
            pltpu.VMEM((outer, width), part.dtype),
            pltpu.SemaphoreType.DMA((inner - 1,)),
            pltpu.SemaphoreType.DMA((outer - 1,)),
            pltpu.SemaphoreType.DMA((inner,)),
            pltpu.SemaphoreType.DMA((outer,)),
        ],
        compiler_params=params(cid),
    )(part)


def gather_kernel(axis, n, src_ref, out_ref, send_sem, recv_sem):
    me = lax.axis_index(axis)
    peers = [lax.rem(me + d, n) for d in range(1, n)]
    barrier = pltpu.get_barrier_semaphore()
    for p in peers:
        pl.semaphore_signal(barrier, inc=1, device_id={axis: p}, device_id_type=MESH)
    pl.semaphore_wait(barrier, n - 1)
    pltpu.make_async_copy(src_ref, out_ref.at[me], recv_sem.at[me]).start()
    copies = []
    for i, p in enumerate(peers):
        cp = pltpu.make_async_remote_copy(
            src_ref=src_ref, dst_ref=out_ref.at[me], send_sem=send_sem.at[i],
            recv_sem=recv_sem.at[me], device_id={axis: p}, device_id_type=MESH)
        cp.start()
        copies.append(cp)
    for cp in copies:
        cp.wait_send()
    for s in range(n):
        pltpu.make_async_copy(src_ref, out_ref.at[s], recv_sem.at[s]).wait()


def gather(x, axis, n, cid):
    return pl.pallas_call(
        functools.partial(gather_kernel, axis, n),
        out_shape=jax.ShapeDtypeStruct((n,) + x.shape, x.dtype),
        in_specs=[VMEM],
        out_specs=VMEM,
        scratch_shapes=[
            pltpu.SemaphoreType.DMA((n - 1,)),
            pltpu.SemaphoreType.DMA((n,)),
        ],
        compiler_params=params(cid),
    )(x)


def ap_kernel(n_row, n_col, inner, chunk, iters, chunk_ref, prefr_ref, resp_out, avail_out,
              colb3, rowb3, prefc, sim_s, resp_s, avail_s, fcol, scol, cq, pack, buf_f, buf_s, zpart, buf1,
              zsum, buf2, e_send_z, e_send_y, e_send_r, e_send_f, e_recv_c, e_recv_b, e_recv_r,
              send_t, recv_t, send_z, send_y, recv_z, recv_y):
    rows, cols = sim_s.shape
    r = lax.axis_index("row")
    c = lax.axis_index("col")
    outer = n_row // inner
    y = r // inner
    z = r % inner
    cpeers = [lax.rem(c + d, n_col) for d in range(1, n_col)]
    zpeers = [y * inner + lax.rem(z + d, inner) for d in range(1, inner)]
    ypeers = [lax.rem(y + d, outer) * inner + z for d in range(1, outer)]
    g = c * n_row + r
    target_row = g // n_col
    my_slot = g % n_col
    parity = c % 2
    sibling = c + 1 - 2 * parity
    targets = [(target_row, 2 * x + my_slot % 2) for x in range(n_col // 2)]
    sources = []
    for t in range(n_col // 2):
        gs = r * n_col + 2 * t + parity
        sources.append((gs % n_row, gs // n_row))

    def differs(dev):
        return jnp.logical_or(dev[0] != r, dev[1] != c)

    barrier = pltpu.get_barrier_semaphore()
    for p in cpeers:
        pl.semaphore_signal(barrier, inc=1, device_id={"col": p}, device_id_type=MESH)
    for p in zpeers + ypeers:
        pl.semaphore_signal(barrier, inc=1, device_id={"row": p}, device_id_type=MESH)
    for dev in targets + sources:
        @pl.when(differs(dev))
        def _():
            pl.semaphore_signal(barrier, inc=1, device_id=dev, device_id_type=MESH)
    self_in = jnp.logical_and(target_row == r, my_slot % 2 == parity).astype(jnp.int32)
    pl.semaphore_wait(barrier, (n_col - 1) + (inner - 1) + (outer - 1) + 2 * (n_col // 2 - self_in))

    copies = []
    pltpu.make_async_copy(chunk_ref, colb3.at[r], e_recv_c.at[z]).start()
    for i, p in enumerate(zpeers):
        cp = pltpu.make_async_remote_copy(
            src_ref=chunk_ref, dst_ref=colb3.at[r], send_sem=e_send_z.at[i],
            recv_sem=e_recv_c.at[z], device_id={"row": p}, device_id_type=MESH)
        cp.start()
        copies.append(cp)
    row_copies = []
    for j, dev in enumerate(targets):
        cp = pltpu.make_async_remote_copy(
            src_ref=chunk_ref, dst_ref=rowb3.at[my_slot], send_sem=e_send_r.at[j],
            recv_sem=e_recv_r.at[my_slot], device_id=dev, device_id_type=MESH)
        row_copies.append(cp)

        @pl.when(differs(dev))
        def _():
            cp.start()

        @pl.when(jnp.logical_not(differs(dev)))
        def _():
            pltpu.make_async_copy(chunk_ref, rowb3.at[my_slot], e_recv_r.at[my_slot]).start()

    prefc[...] = jnp.broadcast_to(prefr_ref[...], (128, rows)).T
    for d in range(inner):
        zs = lax.rem(z + d, inner)
        slot = colb3.at[y * inner + zs]
        pltpu.make_async_copy(chunk_ref, slot, e_recv_c.at[zs]).wait()
        for i, p in enumerate(ypeers):
            cp = pltpu.make_async_remote_copy(
                src_ref=slot, dst_ref=slot, send_sem=e_send_y.at[d, i],
                recv_sem=e_recv_b.at[y, zs], device_id={"row": p}, device_id_type=MESH)
            cp.start()
            copies.append(cp)
    for d in range(1, outer):
        yo = lax.rem(y + d, outer)
        for s in range(inner):
            other = colb3.at[yo * inner + s]
            pltpu.make_async_copy(other, other, e_recv_b.at[yo, s]).wait()
    for t in range(n_col // 2):
        s = 2 * t + parity
        pltpu.make_async_copy(chunk_ref, rowb3.at[s], e_recv_r.at[s]).wait()
        cp = pltpu.make_async_remote_copy(
            src_ref=rowb3.at[s], dst_ref=rowb3.at[s], send_sem=e_send_f.at[t],
            recv_sem=e_recv_r.at[s], device_id={"col": sibling}, device_id_type=MESH)
        cp.start()
        copies.append(cp)
    for t in range(n_col // 2):
        s = 2 * t + 1 - parity
        pltpu.make_async_copy(chunk_ref, rowb3.at[s], e_recv_r.at[s]).wait()
    mol = chunk_ref.shape[0]
    colb_ref = colb3
    rowb_ref = rowb3

    def colb_rows(start, size):
        return colb_ref[pl.ds(start // mol, size // mol)].reshape(size, -1)

    def rowb_rows(start, size):
        return rowb_ref[pl.ds(start // mol, size // mol)].reshape(size, -1)

    row_start = r * rows
    col_start = c * cols
    n_chunks = rows // chunk
    col_ids = col_start + lax.broadcasted_iota(jnp.int32, (chunk, cols), 1)

    def diag_at(i0):
        row_ids = row_start + i0 + lax.broadcasted_iota(jnp.int32, (chunk, cols), 0)
        return row_ids == col_ids

    def record_top(i0, summed):
        first = jnp.max(summed, axis=1, keepdims=True)
        hits = summed == first
        repeats = jnp.sum(hits.astype(jnp.float32), axis=1, keepdims=True)
        others = jnp.max(jnp.where(hits, -jnp.inf, summed), axis=1, keepdims=True)
        second = jnp.where(repeats > 1.0, first, others)
        fcol[pl.ds(i0, chunk), :] = jnp.broadcast_to(first, (chunk, 128))
        scol[pl.ds(i0, chunk), :] = jnp.broadcast_to(second, (chunk, 128))

    colb_all = colb_ref[...].reshape(cols, -1)
    rowb_all = rowb_ref[...].reshape(rows, -1)
    cb = 128 if cols % 128 == 0 else cols
    for j in range(cols // cb):
        xc = colb_all[j * cb:(j + 1) * cb, :].astype(jnp.float32)
        qc = jnp.sum(xc * xc, axis=1, keepdims=True)
        cq[0:1, pl.ds(j * cb, cb)] = jnp.broadcast_to(qc, (cb, 128)).T[0:1, :]
    xr = rowb_all.astype(jnp.float32)
    rq_s = fcol
    rq_s[...] = jnp.broadcast_to(jnp.sum(xr * xr, axis=1, keepdims=True), (rows, 128))
    rb = 128 if rows % 128 == 0 else rows
    for j in range(rows // rb):
        sim_s[pl.ds(j * rb, rb), :] = lax.dot_general(
            rowb_all[j * rb:(j + 1) * rb, :], colb_all, (((1,), (1,)), ((), ())),
            preferred_element_type=jnp.float32)

    def sim_body(i, carry):
        i0 = pl.multiple_of(i * chunk, chunk)
        rq = rq_s[pl.ds(i0, chunk), 0:1]
        dist = 2.0 * sim_s[pl.ds(i0, chunk), :] - rq - cq[...]
        s = jnp.where(diag_at(i0), prefc[pl.ds(i0, chunk), 0:1], dist)
        sim_s[pl.ds(i0, chunk), :] = s
        record_top(i0, s)
        return carry

    lax.fori_loop(0, n_chunks, sim_body, 0)
    for step in range(iters):
        first_step = step == 0
        last_step = step == iters - 1
        resp_prev, avail_prev = resp_s, avail_s
        resp_new, avail_new = (resp_out, avail_out) if last_step else (resp_s, avail_s)
        pk = pack.at[step]
        pk[0:1, :] = fcol[...].T[0:1, :]
        pk[1:2, :] = scol[...].T[0:1, :]
        for k, dst in enumerate((buf_f.at[step], buf_s.at[step])):
            src = pk.at[pl.ds(k, 1)]
            pltpu.make_async_copy(src, dst.at[pl.ds(c, 1)], recv_t.at[step, k, c]).start()
            for i, p in enumerate(cpeers):
                cp = pltpu.make_async_remote_copy(
                    src_ref=src, dst_ref=dst.at[pl.ds(c, 1)], send_sem=send_t.at[step, k, i],
                    recv_sem=recv_t.at[step, k, c], device_id={"col": p}, device_id_type=MESH)
                cp.start()
                copies.append(cp)
        for k, dst in enumerate((buf_f.at[step], buf_s.at[step])):
            for s in range(n_col):
                pltpu.make_async_copy(pk.at[pl.ds(0, 1)], dst.at[pl.ds(s, 1)], recv_t.at[step, k, s]).wait()
        firsts = buf_f[step]
        seconds = buf_s[step]
        first = jnp.max(firsts, axis=0, keepdims=True)
        at_top = firsts == first
        repeats = jnp.sum(at_top.astype(jnp.float32), axis=0, keepdims=True)
        others = jnp.max(jnp.where(at_top, -jnp.inf, firsts), axis=0, keepdims=True)
        second = jnp.where(repeats > 1.0, first, jnp.maximum(jnp.max(seconds, axis=0, keepdims=True), others))
        fcol[...] = jnp.broadcast_to(first, (128, rows)).T
        scol[...] = jnp.broadcast_to(second, (128, rows)).T

        def resp_body(i, acc):
            i0 = pl.multiple_of(i * chunk, chunk)
            s = sim_s[pl.ds(i0, chunk), :]
            summed = s if first_step else avail_prev[pl.ds(i0, chunk), :] + s
            f = fcol[pl.ds(i0, chunk), 0:1]
            sc = scol[pl.ds(i0, chunk), 0:1]
            fresh = s - jnp.where(summed == f, sc, f)
            if first_step:
                resp = (1.0 - DAMPING) * fresh
            else:
                resp = DAMPING * resp_prev[pl.ds(i0, chunk), :] + (1.0 - DAMPING) * fresh
            resp_new[pl.ds(i0, chunk), :] = resp
            positive = jnp.where(diag_at(i0), resp, jnp.maximum(resp, 0.0))
            return acc + jnp.sum(positive, axis=0, keepdims=True)

        zp = zpart.at[step]
        zp[...] = lax.fori_loop(0, n_chunks, resp_body, jnp.zeros((1, cols), jnp.float32))

        b1 = buf1.at[step]
        pltpu.make_async_copy(zp, b1.at[pl.ds(z, 1)], recv_z.at[step, z]).start()
        for i, p in enumerate(zpeers):
            cp = pltpu.make_async_remote_copy(
                src_ref=zp, dst_ref=b1.at[pl.ds(z, 1)], send_sem=send_z.at[step, i],
                recv_sem=recv_z.at[step, z], device_id={"row": p}, device_id_type=MESH)
            cp.start()
            copies.append(cp)
        for s in range(inner):
            pltpu.make_async_copy(zp, b1.at[pl.ds(s, 1)], recv_z.at[step, s]).wait()
        zs = zsum.at[step]
        zs[...] = jnp.sum(b1[...], axis=0, keepdims=True)
        b2 = buf2.at[step]
        pltpu.make_async_copy(zs, b2.at[pl.ds(y, 1)], recv_y.at[step, y]).start()
        for i, p in enumerate(ypeers):
            cp = pltpu.make_async_remote_copy(
                src_ref=zs, dst_ref=b2.at[pl.ds(y, 1)], send_sem=send_y.at[step, i],
                recv_sem=recv_y.at[step, y], device_id={"row": p}, device_id_type=MESH)
            cp.start()
            copies.append(cp)
        for s in range(outer):
            pltpu.make_async_copy(zs, b2.at[pl.ds(s, 1)], recv_y.at[step, s]).wait()
        colsum = jnp.sum(b2[...], axis=0, keepdims=True)

        def avail_body(i, carry):
            i0 = pl.multiple_of(i * chunk, chunk)
            resp = resp_new[pl.ds(i0, chunk), :]
            diag = diag_at(i0)
            positive = jnp.where(diag, resp, jnp.maximum(resp, 0.0))
            renew = colsum - positive
            renew = jnp.where(diag, renew, jnp.minimum(renew, 0.0))
            if first_step:
                avail = (1.0 - DAMPING) * renew
            else:
                avail = DAMPING * avail_prev[pl.ds(i0, chunk), :] + (1.0 - DAMPING) * renew
            avail_new[pl.ds(i0, chunk), :] = avail
            if not last_step:
                record_top(i0, avail + sim_s[pl.ds(i0, chunk), :])
            return carry

        lax.fori_loop(0, n_chunks, avail_body, 0)
    for cp in copies:
        cp.wait_send()
    for j, dev in enumerate(targets):
        @pl.when(differs(dev))
        def _():
            row_copies[j].wait_send()


def propagate(chunk, pref_row, n_row, n_col, inner, iters, cid):
    mol, width = chunk.shape
    rows, cols = mol * n_col, mol * n_row
    outer = n_row // inner
    f32 = jnp.float32
    return pl.pallas_call(
        functools.partial(ap_kernel, n_row, n_col, inner, 32, iters),
        out_shape=(jax.ShapeDtypeStruct((rows, cols), f32), jax.ShapeDtypeStruct((rows, cols), f32)),
        in_specs=[VMEM] * 2,
        out_specs=(VMEM, VMEM),
        scratch_shapes=[
            pltpu.VMEM((n_row, mol, width), chunk.dtype),
            pltpu.VMEM((n_col, mol, width), chunk.dtype),
            pltpu.VMEM((rows, 128), f32),
            pltpu.VMEM((rows, cols), f32),
            pltpu.VMEM((rows, cols), f32),
            pltpu.VMEM((rows, cols), f32),
            pltpu.VMEM((rows, 128), f32),
            pltpu.VMEM((rows, 128), f32),
            pltpu.VMEM((1, cols), f32),
            pltpu.VMEM((iters, 2, rows), f32),
            pltpu.VMEM((iters, n_col, rows), f32),
            pltpu.VMEM((iters, n_col, rows), f32),
            pltpu.VMEM((iters, 1, cols), f32),
            pltpu.VMEM((iters, inner, cols), f32),
            pltpu.VMEM((iters, 1, cols), f32),
            pltpu.VMEM((iters, outer, cols), f32),
            pltpu.SemaphoreType.DMA((inner - 1,)),
            pltpu.SemaphoreType.DMA((inner, outer - 1)),
            pltpu.SemaphoreType.DMA((n_col // 2,)),
            pltpu.SemaphoreType.DMA((n_col // 2,)),
            pltpu.SemaphoreType.DMA((inner,)),
            pltpu.SemaphoreType.DMA((outer, inner)),
            pltpu.SemaphoreType.DMA((n_col,)),
            pltpu.SemaphoreType.DMA((iters, 2, n_col - 1)),
            pltpu.SemaphoreType.DMA((iters, 2, n_col)),
            pltpu.SemaphoreType.DMA((iters, inner - 1)),
            pltpu.SemaphoreType.DMA((iters, outer - 1)),
            pltpu.SemaphoreType.DMA((iters, inner)),
            pltpu.SemaphoreType.DMA((iters, outer)),
        ],
        compiler_params=pltpu.CompilerParams(
            collective_id=cid, has_side_effects=True, vmem_limit_bytes=60 * 1024 * 1024),
    )(chunk, pref_row)


def similarity(row_emb, col_emb, row_start, col_start, pref_rows):
    cross = lax.dot_general(
        row_emb, col_emb, (((1,), (1,)), ((), ())), preferred_element_type=jnp.float32
    )
    row_vals = row_emb.astype(jnp.float32)
    col_vals = col_emb.astype(jnp.float32)
    row_sq = jnp.sum(row_vals * row_vals, axis=1)
    col_sq = jnp.sum(col_vals * col_vals, axis=1)
    dist = 2.0 * cross - row_sq[:, None] - col_sq[None, :]
    row_ids = row_start + jnp.arange(row_emb.shape[0], dtype=jnp.int32)
    col_ids = col_start + jnp.arange(col_emb.shape[0], dtype=jnp.int32)
    diagonal = row_ids[:, None] == col_ids[None, :]
    return (jnp.where(diagonal, pref_rows[:, None], dist), diagonal)


def top_two(summed):
    first = jnp.max(summed, axis=1)
    hits = summed == first[:, None]
    repeats = jnp.sum(hits.astype(jnp.int32), axis=1)
    others = jnp.max(jnp.where(hits, -jnp.inf, summed), axis=1)
    second = jnp.where(repeats > 1, first, others)
    return (first, second)


def local(embedding, preference):
    rows_n = lax.axis_size("row")
    cols_n = lax.axis_size("col")
    row_idx = lax.axis_index("row")
    col_idx = lax.axis_index("col")
    mol = embedding.shape[2]
    width = embedding.shape[3]
    row_count = mol * cols_n
    col_count = mol * rows_n
    resp, avail = propagate(embedding.reshape(mol, width), preference.reshape(1, row_count), rows_n, cols_n, INNER, ITERS, 0)
    return (resp, avail)


def solution(mesh):
    placed = (P("col", "row", None, None), P("row"))
    return jax.shard_map(
        local,
        mesh=mesh,
        in_specs=placed,
        out_specs=(P("row", "col"), P("row", "col")),
        check_vma=False,
    )
```

```python
import functools

import jax
import jax.numpy as jnp
from jax import lax
from jax.experimental import pallas as pl
from jax.experimental.pallas import tpu as pltpu
from jax.sharding import PartitionSpec as P

ITERS = 2


DAMPING = 0.5

INNER = 8

MESH = pl.DeviceIdType.MESH
VMEM = pl.BlockSpec(memory_space=pltpu.VMEM)


def ap_kernel(n_row, n_col, inner, chunk, iters, chunk_ref, prefr_ref, resp_out, avail_out,
              colb3, rowb3, prefc, sim_s, resp_s, avail_s, fcol, scol, cq, pack, buf_f, buf_s, zpart, buf1,
              zsum, buf2, e_send_z, e_send_y, e_send_r, e_send_f, e_recv_c, e_recv_b, e_recv_r,
              send_t, recv_t, send_z, send_y, recv_z, recv_y):
    rows, cols = sim_s.shape
    r = lax.axis_index("row")
    c = lax.axis_index("col")
    outer = n_row // inner
    y = r // inner
    z = r % inner
    cpeers = [lax.rem(c + d, n_col) for d in range(1, n_col)]
    zpeers = [y * inner + lax.rem(z + d, inner) for d in range(1, inner)]
    ypeers = [lax.rem(y + d, outer) * inner + z for d in range(1, outer)]
    g = c * n_row + r
    target_row = g // n_col
    my_slot = g % n_col
    parity = c % 2
    sibling = c + 1 - 2 * parity
    targets = [(target_row, 2 * x + my_slot % 2) for x in range(n_col // 2)]
    sources = []
    for t in range(n_col // 2):
        gs = r * n_col + 2 * t + parity
        sources.append((gs % n_row, gs // n_row))

    def differs(dev):
        return jnp.logical_or(dev[0] != r, dev[1] != c)

    barrier = pltpu.get_barrier_semaphore()
    for p in cpeers:
        pl.semaphore_signal(barrier, inc=1, device_id={"col": p}, device_id_type=MESH)
    for p in zpeers + ypeers:
        pl.semaphore_signal(barrier, inc=1, device_id={"row": p}, device_id_type=MESH)
    for dev in targets + sources:
        @pl.when(differs(dev))
        def _():
            pl.semaphore_signal(barrier, inc=1, device_id=dev, device_id_type=MESH)
    self_in = jnp.logical_and(target_row == r, my_slot % 2 == parity).astype(jnp.int32)
    pl.semaphore_wait(barrier, (n_col - 1) + (inner - 1) + (outer - 1) + 2 * (n_col // 2 - self_in))

    copies = []
    pltpu.make_async_copy(chunk_ref, colb3.at[r], e_recv_c.at[z]).start()
    for i, p in enumerate(zpeers):
        cp = pltpu.make_async_remote_copy(
            src_ref=chunk_ref, dst_ref=colb3.at[r], send_sem=e_send_z.at[i],
            recv_sem=e_recv_c.at[z], device_id={"row": p}, device_id_type=MESH)
        cp.start()
        copies.append(cp)
    row_copies = []
    for j, dev in enumerate(targets):
        cp = pltpu.make_async_remote_copy(
            src_ref=chunk_ref, dst_ref=rowb3.at[my_slot], send_sem=e_send_r.at[j],
            recv_sem=e_recv_r.at[my_slot], device_id=dev, device_id_type=MESH)
        row_copies.append(cp)

        @pl.when(differs(dev))
        def _():
            cp.start()

        @pl.when(jnp.logical_not(differs(dev)))
        def _():
            pltpu.make_async_copy(chunk_ref, rowb3.at[my_slot], e_recv_r.at[my_slot]).start()

    prefc[...] = jnp.broadcast_to(prefr_ref[...], (128, rows)).T
    for d in range(inner):
        zs = lax.rem(z + d, inner)
        slot = colb3.at[y * inner + zs]
        pltpu.make_async_copy(chunk_ref, slot, e_recv_c.at[zs]).wait()
        for i, p in enumerate(ypeers):
            cp = pltpu.make_async_remote_copy(
                src_ref=slot, dst_ref=slot, send_sem=e_send_y.at[d, i],
                recv_sem=e_recv_b.at[y, zs], device_id={"row": p}, device_id_type=MESH)
            cp.start()
            copies.append(cp)
    for d in range(1, outer):
        yo = lax.rem(y + d, outer)
        for s in range(inner):
            other = colb3.at[yo * inner + s]
            pltpu.make_async_copy(other, other, e_recv_b.at[yo, s]).wait()
    for t in range(n_col // 2):
        s = 2 * t + parity
        pltpu.make_async_copy(chunk_ref, rowb3.at[s], e_recv_r.at[s]).wait()
        cp = pltpu.make_async_remote_copy(
            src_ref=rowb3.at[s], dst_ref=rowb3.at[s], send_sem=e_send_f.at[t],
            recv_sem=e_recv_r.at[s], device_id={"col": sibling}, device_id_type=MESH)
        cp.start()
        copies.append(cp)
    for t in range(n_col // 2):
        s = 2 * t + 1 - parity
        pltpu.make_async_copy(chunk_ref, rowb3.at[s], e_recv_r.at[s]).wait()
    mol = chunk_ref.shape[0]
    colb_ref = colb3
    rowb_ref = rowb3


    row_start = r * rows
    col_start = c * cols
    n_chunks = rows // chunk
    col_ids = col_start + lax.broadcasted_iota(jnp.int32, (chunk, cols), 1)

    def diag_at(i0):
        row_ids = row_start + i0 + lax.broadcasted_iota(jnp.int32, (chunk, cols), 0)
        return row_ids == col_ids

    def record_top(i0, summed):
        first = jnp.max(summed, axis=1, keepdims=True)
        hits = summed == first
        repeats = jnp.sum(hits.astype(jnp.float32), axis=1, keepdims=True)
        others = jnp.max(jnp.where(hits, -jnp.inf, summed), axis=1, keepdims=True)
        second = jnp.where(repeats > 1.0, first, others)
        fcol[pl.ds(i0, chunk), :] = jnp.broadcast_to(first, (chunk, 128))
        scol[pl.ds(i0, chunk), :] = jnp.broadcast_to(second, (chunk, 128))

    colb_all = colb_ref[...].reshape(cols, -1)
    rowb_all = rowb_ref[...].reshape(rows, -1)
    cb = 128 if cols % 128 == 0 else cols
    for j in range(cols // cb):
        xc = colb_all[j * cb:(j + 1) * cb, :].astype(jnp.float32)
        qc = jnp.sum(xc * xc, axis=1, keepdims=True)
        cq[0:1, pl.ds(j * cb, cb)] = jnp.broadcast_to(qc, (cb, 128)).T[0:1, :]
    xr = rowb_all.astype(jnp.float32)
    rq_s = fcol
    rq_s[...] = jnp.broadcast_to(jnp.sum(xr * xr, axis=1, keepdims=True), (rows, 128))
    rb = 128 if rows % 128 == 0 else rows
    for j in range(rows // rb):
        sim_s[pl.ds(j * rb, rb), :] = lax.dot_general(
            rowb_all[j * rb:(j + 1) * rb, :], colb_all, (((1,), (1,)), ((), ())),
            preferred_element_type=jnp.float32)

    def sim_body(i, carry):
        i0 = pl.multiple_of(i * chunk, chunk)
        rq = rq_s[pl.ds(i0, chunk), 0:1]
        dist = 2.0 * sim_s[pl.ds(i0, chunk), :] - rq - cq[...]
        s = jnp.where(diag_at(i0), prefc[pl.ds(i0, chunk), 0:1], dist)
        sim_s[pl.ds(i0, chunk), :] = s
        record_top(i0, s)
        return carry

    lax.fori_loop(0, n_chunks, sim_body, 0)
    for step in range(iters):
        first_step = step == 0
        last_step = step == iters - 1
        resp_prev, avail_prev = resp_s, avail_s
        resp_new, avail_new = (resp_out, avail_out) if last_step else (resp_s, avail_s)
        pk = pack.at[step]
        pk[0:1, :] = fcol[...].T[0:1, :]
        pk[1:2, :] = scol[...].T[0:1, :]
        for k, dst in enumerate((buf_f.at[step], buf_s.at[step])):
            src = pk.at[pl.ds(k, 1)]
            pltpu.make_async_copy(src, dst.at[pl.ds(c, 1)], recv_t.at[step, k, c]).start()
            for i, p in enumerate(cpeers):
                cp = pltpu.make_async_remote_copy(
                    src_ref=src, dst_ref=dst.at[pl.ds(c, 1)], send_sem=send_t.at[step, k, i],
                    recv_sem=recv_t.at[step, k, c], device_id={"col": p}, device_id_type=MESH)
                cp.start()
                copies.append(cp)
        for k, dst in enumerate((buf_f.at[step], buf_s.at[step])):
            for s in range(n_col):
                pltpu.make_async_copy(pk.at[pl.ds(0, 1)], dst.at[pl.ds(s, 1)], recv_t.at[step, k, s]).wait()
        firsts = buf_f[step]
        seconds = buf_s[step]
        first = jnp.max(firsts, axis=0, keepdims=True)
        at_top = firsts == first
        repeats = jnp.sum(at_top.astype(jnp.float32), axis=0, keepdims=True)
        others = jnp.max(jnp.where(at_top, -jnp.inf, firsts), axis=0, keepdims=True)
        second = jnp.where(repeats > 1.0, first, jnp.maximum(jnp.max(seconds, axis=0, keepdims=True), others))
        fcol[...] = jnp.broadcast_to(first, (128, rows)).T
        scol[...] = jnp.broadcast_to(second, (128, rows)).T

        def resp_body(i, acc):
            i0 = pl.multiple_of(i * chunk, chunk)
            s = sim_s[pl.ds(i0, chunk), :]
            summed = s if first_step else avail_prev[pl.ds(i0, chunk), :] + s
            f = fcol[pl.ds(i0, chunk), 0:1]
            sc = scol[pl.ds(i0, chunk), 0:1]
            fresh = s - jnp.where(summed == f, sc, f)
            if first_step:
                resp = (1.0 - DAMPING) * fresh
            else:
                resp = DAMPING * resp_prev[pl.ds(i0, chunk), :] + (1.0 - DAMPING) * fresh
            resp_new[pl.ds(i0, chunk), :] = resp
            positive = jnp.where(diag_at(i0), resp, jnp.maximum(resp, 0.0))
            return acc + jnp.sum(positive, axis=0, keepdims=True)

        zp = zpart.at[step]
        zp[...] = lax.fori_loop(0, n_chunks, resp_body, jnp.zeros((1, cols), jnp.float32))

        b1 = buf1.at[step]
        pltpu.make_async_copy(zp, b1.at[pl.ds(z, 1)], recv_z.at[step, z]).start()
        for i, p in enumerate(zpeers):
            cp = pltpu.make_async_remote_copy(
                src_ref=zp, dst_ref=b1.at[pl.ds(z, 1)], send_sem=send_z.at[step, i],
                recv_sem=recv_z.at[step, z], device_id={"row": p}, device_id_type=MESH)
            cp.start()
            copies.append(cp)
        for s in range(inner):
            pltpu.make_async_copy(zp, b1.at[pl.ds(s, 1)], recv_z.at[step, s]).wait()
        zs = zsum.at[step]
        zs[...] = jnp.sum(b1[...], axis=0, keepdims=True)
        b2 = buf2.at[step]
        pltpu.make_async_copy(zs, b2.at[pl.ds(y, 1)], recv_y.at[step, y]).start()
        for i, p in enumerate(ypeers):
            cp = pltpu.make_async_remote_copy(
                src_ref=zs, dst_ref=b2.at[pl.ds(y, 1)], send_sem=send_y.at[step, i],
                recv_sem=recv_y.at[step, y], device_id={"row": p}, device_id_type=MESH)
            cp.start()
            copies.append(cp)
        for s in range(outer):
            pltpu.make_async_copy(zs, b2.at[pl.ds(s, 1)], recv_y.at[step, s]).wait()
        colsum = jnp.sum(b2[...], axis=0, keepdims=True)

        def avail_body(i, carry):
            i0 = pl.multiple_of(i * chunk, chunk)
            resp = resp_new[pl.ds(i0, chunk), :]
            diag = diag_at(i0)
            positive = jnp.where(diag, resp, jnp.maximum(resp, 0.0))
            renew = colsum - positive
            renew = jnp.where(diag, renew, jnp.minimum(renew, 0.0))
            if first_step:
                avail = (1.0 - DAMPING) * renew
            else:
                avail = DAMPING * avail_prev[pl.ds(i0, chunk), :] + (1.0 - DAMPING) * renew
            avail_new[pl.ds(i0, chunk), :] = avail
            if not last_step:
                record_top(i0, avail + sim_s[pl.ds(i0, chunk), :])
            return carry

        lax.fori_loop(0, n_chunks, avail_body, 0)
    for cp in copies:
        cp.wait_send()
    for j, dev in enumerate(targets):
        @pl.when(differs(dev))
        def _():
            row_copies[j].wait_send()


def propagate(chunk, pref_row, n_row, n_col, inner, iters, cid):
    mol, width = chunk.shape
    rows, cols = mol * n_col, mol * n_row
    outer = n_row // inner
    f32 = jnp.float32
    return pl.pallas_call(
        functools.partial(ap_kernel, n_row, n_col, inner, rows, iters),
        out_shape=(jax.ShapeDtypeStruct((rows, cols), f32), jax.ShapeDtypeStruct((rows, cols), f32)),
        in_specs=[VMEM] * 2,
        out_specs=(VMEM, VMEM),
        scratch_shapes=[
            pltpu.VMEM((n_row, mol, width), chunk.dtype),
            pltpu.VMEM((n_col, mol, width), chunk.dtype),
            pltpu.VMEM((rows, 128), f32),
            pltpu.VMEM((rows, cols), f32),
            pltpu.VMEM((rows, cols), f32),
            pltpu.VMEM((rows, cols), f32),
            pltpu.VMEM((rows, 128), f32),
            pltpu.VMEM((rows, 128), f32),
            pltpu.VMEM((1, cols), f32),
            pltpu.VMEM((iters, 2, rows), f32),
            pltpu.VMEM((iters, n_col, rows), f32),
            pltpu.VMEM((iters, n_col, rows), f32),
            pltpu.VMEM((iters, 1, cols), f32),
            pltpu.VMEM((iters, inner, cols), f32),
            pltpu.VMEM((iters, 1, cols), f32),
            pltpu.VMEM((iters, outer, cols), f32),
            pltpu.SemaphoreType.DMA((inner - 1,)),
            pltpu.SemaphoreType.DMA((inner, outer - 1)),
            pltpu.SemaphoreType.DMA((n_col // 2,)),
            pltpu.SemaphoreType.DMA((n_col // 2,)),
            pltpu.SemaphoreType.DMA((inner,)),
            pltpu.SemaphoreType.DMA((outer, inner)),
            pltpu.SemaphoreType.DMA((n_col,)),
            pltpu.SemaphoreType.DMA((iters, 2, n_col - 1)),
            pltpu.SemaphoreType.DMA((iters, 2, n_col)),
            pltpu.SemaphoreType.DMA((iters, inner - 1)),
            pltpu.SemaphoreType.DMA((iters, outer - 1)),
            pltpu.SemaphoreType.DMA((iters, inner)),
            pltpu.SemaphoreType.DMA((iters, outer)),
        ],
        compiler_params=pltpu.CompilerParams(
            collective_id=cid, has_side_effects=True, vmem_limit_bytes=60 * 1024 * 1024),
    )(chunk, pref_row)


def local(embedding, preference):
    rows_n = lax.axis_size("row")
    cols_n = lax.axis_size("col")
    row_idx = lax.axis_index("row")
    col_idx = lax.axis_index("col")
    mol = embedding.shape[2]
    width = embedding.shape[3]
    row_count = mol * cols_n
    col_count = mol * rows_n
    resp, avail = propagate(embedding.reshape(mol, width), preference.reshape(1, row_count), rows_n, cols_n, INNER, ITERS, 0)
    return (resp, avail)


def solution(mesh):
    placed = (P("col", "row", None, None), P("row"))
    return jax.shard_map(
        local,
        mesh=mesh,
        in_specs=placed,
        out_specs=(P("row", "col"), P("row", "col")),
        check_vma=False,
    )
```

```python
import functools

import jax
import jax.numpy as jnp
from jax import lax
from jax.experimental import pallas as pl
from jax.experimental.pallas import tpu as pltpu
from jax.sharding import PartitionSpec as P

ITERS = 2


DAMPING = 0.5

INNER = 8

MESH = pl.DeviceIdType.MESH
VMEM = pl.BlockSpec(memory_space=pltpu.VMEM)


def ap_kernel(n_row, n_col, inner, chunk, iters, chunk_ref, prefr_ref, resp_out, avail_out,
              colb3, rowb3, prefc, sim_s, resp_s, avail_s, fcol, scol, cq, pack, buf_f, buf_s, zpart, buf1,
              zsum, buf2, e_send_z, e_send_y, e_send_r, e_send_f, e_recv_c, e_recv_b, e_recv_r,
              send_t, recv_t, send_z, send_y, recv_z, recv_y):
    rows, cols = sim_s.shape
    r = lax.axis_index("row")
    c = lax.axis_index("col")
    outer = n_row // inner
    y = r // inner
    z = r % inner
    cpeers = [lax.rem(c + d, n_col) for d in range(1, n_col)]
    zpeers = [y * inner + lax.rem(z + d, inner) for d in range(1, inner)]
    ypeers = [lax.rem(y + d, outer) * inner + z for d in range(1, outer)]
    g = c * n_row + r
    target_row = g // n_col
    my_slot = g % n_col
    parity = c % 2
    sibling = c + 1 - 2 * parity
    targets = [(target_row, 2 * x + my_slot % 2) for x in range(n_col // 2)]
    sources = []
    for t in range(n_col // 2):
        gs = r * n_col + 2 * t + parity
        sources.append((gs % n_row, gs // n_row))

    def differs(dev):
        return jnp.logical_or(dev[0] != r, dev[1] != c)

    barrier = pltpu.get_barrier_semaphore()
    for p in cpeers:
        pl.semaphore_signal(barrier, inc=1, device_id={"col": p}, device_id_type=MESH)
    for p in zpeers + ypeers:
        pl.semaphore_signal(barrier, inc=1, device_id={"row": p}, device_id_type=MESH)
    for dev in targets + sources:
        @pl.when(differs(dev))
        def _():
            pl.semaphore_signal(barrier, inc=1, device_id=dev, device_id_type=MESH)
    self_in = jnp.logical_and(target_row == r, my_slot % 2 == parity).astype(jnp.int32)
    pl.semaphore_wait(barrier, (n_col - 1) + (inner - 1) + (outer - 1) + 2 * (n_col // 2 - self_in))

    copies = []
    pltpu.make_async_copy(chunk_ref, colb3.at[r], e_recv_c.at[z]).start()
    for i, p in enumerate(zpeers):
        cp = pltpu.make_async_remote_copy(
            src_ref=chunk_ref, dst_ref=colb3.at[r], send_sem=e_send_z.at[i],
            recv_sem=e_recv_c.at[z], device_id={"row": p}, device_id_type=MESH)
        cp.start()
        copies.append(cp)
    row_copies = []
    for j, dev in enumerate(targets):
        cp = pltpu.make_async_remote_copy(
            src_ref=chunk_ref, dst_ref=rowb3.at[my_slot], send_sem=e_send_r.at[j],
            recv_sem=e_recv_r.at[my_slot], device_id=dev, device_id_type=MESH)
        row_copies.append(cp)

        @pl.when(differs(dev))
        def _():
            cp.start()

        @pl.when(jnp.logical_not(differs(dev)))
        def _():
            pltpu.make_async_copy(chunk_ref, rowb3.at[my_slot], e_recv_r.at[my_slot]).start()

    prefc[...] = jnp.broadcast_to(prefr_ref[...].reshape(1, rows), (128, rows)).T
    for d in range(inner):
        zs = lax.rem(z + d, inner)
        slot = colb3.at[y * inner + zs]
        pltpu.make_async_copy(chunk_ref, slot, e_recv_c.at[zs]).wait()
        for i, p in enumerate(ypeers):
            cp = pltpu.make_async_remote_copy(
                src_ref=slot, dst_ref=slot, send_sem=e_send_y.at[d, i],
                recv_sem=e_recv_b.at[y, zs], device_id={"row": p}, device_id_type=MESH)
            cp.start()
            copies.append(cp)
    for d in range(1, outer):
        yo = lax.rem(y + d, outer)
        for s in range(inner):
            other = colb3.at[yo * inner + s]
            pltpu.make_async_copy(other, other, e_recv_b.at[yo, s]).wait()
    for t in range(n_col // 2):
        s = 2 * t + parity
        pltpu.make_async_copy(chunk_ref, rowb3.at[s], e_recv_r.at[s]).wait()
        cp = pltpu.make_async_remote_copy(
            src_ref=rowb3.at[s], dst_ref=rowb3.at[s], send_sem=e_send_f.at[t],
            recv_sem=e_recv_r.at[s], device_id={"col": sibling}, device_id_type=MESH)
        cp.start()
        copies.append(cp)
    for t in range(n_col // 2):
        s = 2 * t + 1 - parity
        pltpu.make_async_copy(chunk_ref, rowb3.at[s], e_recv_r.at[s]).wait()
    mol = chunk_ref.shape[0]
    colb_ref = colb3
    rowb_ref = rowb3


    row_start = r * rows
    col_start = c * cols
    n_chunks = rows // chunk
    col_ids = col_start + lax.broadcasted_iota(jnp.int32, (chunk, cols), 1)

    def diag_at(i0):
        row_ids = row_start + i0 + lax.broadcasted_iota(jnp.int32, (chunk, cols), 0)
        return row_ids == col_ids

    def record_top(i0, summed):
        first = jnp.max(summed, axis=1, keepdims=True)
        hits = summed == first
        repeats = jnp.sum(hits.astype(jnp.float32), axis=1, keepdims=True)
        others = jnp.max(jnp.where(hits, -jnp.inf, summed), axis=1, keepdims=True)
        second = jnp.where(repeats > 1.0, first, others)
        fcol[pl.ds(i0, chunk), :] = jnp.broadcast_to(first, (chunk, 128))
        scol[pl.ds(i0, chunk), :] = jnp.broadcast_to(second, (chunk, 128))

    colb_all = colb_ref[...].reshape(cols, -1)
    rowb_all = rowb_ref[...].reshape(rows, -1)
    cb = 128 if cols % 128 == 0 else cols
    for j in range(cols // cb):
        xc = colb_all[j * cb:(j + 1) * cb, :].astype(jnp.float32)
        qc = jnp.sum(xc * xc, axis=1, keepdims=True)
        cq[0:1, pl.ds(j * cb, cb)] = jnp.broadcast_to(qc, (cb, 128)).T[0:1, :]
    xr = rowb_all.astype(jnp.float32)
    rq_s = fcol
    rq_s[...] = jnp.broadcast_to(jnp.sum(xr * xr, axis=1, keepdims=True), (rows, 128))
    rb = 128 if rows % 128 == 0 else rows
    for j in range(rows // rb):
        sim_s[pl.ds(j * rb, rb), :] = lax.dot_general(
            rowb_all[j * rb:(j + 1) * rb, :], colb_all, (((1,), (1,)), ((), ())),
            preferred_element_type=jnp.float32)

    def sim_body(i, carry):
        i0 = pl.multiple_of(i * chunk, chunk)
        rq = rq_s[pl.ds(i0, chunk), 0:1]
        dist = 2.0 * sim_s[pl.ds(i0, chunk), :] - rq - cq[...]
        s = jnp.where(diag_at(i0), prefc[pl.ds(i0, chunk), 0:1], dist)
        sim_s[pl.ds(i0, chunk), :] = s
        record_top(i0, s)
        return carry

    lax.fori_loop(0, n_chunks, sim_body, 0)
    for step in range(iters):
        first_step = step == 0
        last_step = step == iters - 1
        resp_prev, avail_prev = resp_s, avail_s
        resp_new, avail_new = (resp_out, avail_out) if last_step else (resp_s, avail_s)
        pk = pack.at[step]
        pk[0:1, :] = fcol[...].T[0:1, :]
        pk[1:2, :] = scol[...].T[0:1, :]
        for k, dst in enumerate((buf_f.at[step], buf_s.at[step])):
            src = pk.at[pl.ds(k, 1)]
            pltpu.make_async_copy(src, dst.at[pl.ds(c, 1)], recv_t.at[step, k, c]).start()
            for i, p in enumerate(cpeers):
                cp = pltpu.make_async_remote_copy(
                    src_ref=src, dst_ref=dst.at[pl.ds(c, 1)], send_sem=send_t.at[step, k, i],
                    recv_sem=recv_t.at[step, k, c], device_id={"col": p}, device_id_type=MESH)
                cp.start()
                copies.append(cp)
        for k, dst in enumerate((buf_f.at[step], buf_s.at[step])):
            for s in range(n_col):
                pltpu.make_async_copy(pk.at[pl.ds(0, 1)], dst.at[pl.ds(s, 1)], recv_t.at[step, k, s]).wait()
        firsts = buf_f[step]
        seconds = buf_s[step]
        first = jnp.max(firsts, axis=0, keepdims=True)
        at_top = firsts == first
        repeats = jnp.sum(at_top.astype(jnp.float32), axis=0, keepdims=True)
        others = jnp.max(jnp.where(at_top, -jnp.inf, firsts), axis=0, keepdims=True)
        second = jnp.where(repeats > 1.0, first, jnp.maximum(jnp.max(seconds, axis=0, keepdims=True), others))
        fcol[...] = jnp.broadcast_to(first, (128, rows)).T
        scol[...] = jnp.broadcast_to(second, (128, rows)).T

        def resp_body(i, acc):
            i0 = pl.multiple_of(i * chunk, chunk)
            s = sim_s[pl.ds(i0, chunk), :]
            summed = s if first_step else avail_prev[pl.ds(i0, chunk), :] + s
            f = fcol[pl.ds(i0, chunk), 0:1]
            sc = scol[pl.ds(i0, chunk), 0:1]
            fresh = s - jnp.where(summed == f, sc, f)
            if first_step:
                resp = (1.0 - DAMPING) * fresh
            else:
                resp = DAMPING * resp_prev[pl.ds(i0, chunk), :] + (1.0 - DAMPING) * fresh
            resp_new[pl.ds(i0, chunk), :] = resp
            positive = jnp.where(diag_at(i0), resp, jnp.maximum(resp, 0.0))
            return acc + jnp.sum(positive, axis=0, keepdims=True)

        zp = zpart.at[step]
        zp[...] = lax.fori_loop(0, n_chunks, resp_body, jnp.zeros((1, cols), jnp.float32))

        b1 = buf1.at[step]
        pltpu.make_async_copy(zp, b1.at[pl.ds(z, 1)], recv_z.at[step, z]).start()
        for i, p in enumerate(zpeers):
            cp = pltpu.make_async_remote_copy(
                src_ref=zp, dst_ref=b1.at[pl.ds(z, 1)], send_sem=send_z.at[step, i],
                recv_sem=recv_z.at[step, z], device_id={"row": p}, device_id_type=MESH)
            cp.start()
            copies.append(cp)
        for s in range(inner):
            pltpu.make_async_copy(zp, b1.at[pl.ds(s, 1)], recv_z.at[step, s]).wait()
        zs = zsum.at[step]
        zs[...] = jnp.sum(b1[...], axis=0, keepdims=True)
        b2 = buf2.at[step]
        pltpu.make_async_copy(zs, b2.at[pl.ds(y, 1)], recv_y.at[step, y]).start()
        for i, p in enumerate(ypeers):
            cp = pltpu.make_async_remote_copy(
                src_ref=zs, dst_ref=b2.at[pl.ds(y, 1)], send_sem=send_y.at[step, i],
                recv_sem=recv_y.at[step, y], device_id={"row": p}, device_id_type=MESH)
            cp.start()
            copies.append(cp)
        for s in range(outer):
            pltpu.make_async_copy(zs, b2.at[pl.ds(s, 1)], recv_y.at[step, s]).wait()
        colsum = jnp.sum(b2[...], axis=0, keepdims=True)

        def avail_body(i, carry):
            i0 = pl.multiple_of(i * chunk, chunk)
            resp = resp_new[pl.ds(i0, chunk), :]
            diag = diag_at(i0)
            positive = jnp.where(diag, resp, jnp.maximum(resp, 0.0))
            renew = colsum - positive
            renew = jnp.where(diag, renew, jnp.minimum(renew, 0.0))
            if first_step:
                avail = (1.0 - DAMPING) * renew
            else:
                avail = DAMPING * avail_prev[pl.ds(i0, chunk), :] + (1.0 - DAMPING) * renew
            avail_new[pl.ds(i0, chunk), :] = avail
            if not last_step:
                record_top(i0, avail + sim_s[pl.ds(i0, chunk), :])
            return carry

        lax.fori_loop(0, n_chunks, avail_body, 0)
    for cp in copies:
        cp.wait_send()
    for j, dev in enumerate(targets):
        @pl.when(differs(dev))
        def _():
            row_copies[j].wait_send()


def propagate(chunk, pref_row, n_row, n_col, inner, iters, cid):
    mol, width = chunk.shape
    rows, cols = mol * n_col, mol * n_row
    outer = n_row // inner
    f32 = jnp.float32
    return pl.pallas_call(
        functools.partial(ap_kernel, n_row, n_col, inner, rows, iters),
        out_shape=(jax.ShapeDtypeStruct((rows, cols), f32), jax.ShapeDtypeStruct((rows, cols), f32)),
        in_specs=[VMEM] * 2,
        out_specs=(VMEM, VMEM),
        scratch_shapes=[
            pltpu.VMEM((n_row, mol, width), chunk.dtype),
            pltpu.VMEM((n_col, mol, width), chunk.dtype),
            pltpu.VMEM((rows, 128), f32),
            pltpu.VMEM((rows, cols), f32),
            pltpu.VMEM((rows, cols), f32),
            pltpu.VMEM((rows, cols), f32),
            pltpu.VMEM((rows, 128), f32),
            pltpu.VMEM((rows, 128), f32),
            pltpu.VMEM((1, cols), f32),
            pltpu.VMEM((iters, 2, rows), f32),
            pltpu.VMEM((iters, n_col, rows), f32),
            pltpu.VMEM((iters, n_col, rows), f32),
            pltpu.VMEM((iters, 1, cols), f32),
            pltpu.VMEM((iters, inner, cols), f32),
            pltpu.VMEM((iters, 1, cols), f32),
            pltpu.VMEM((iters, outer, cols), f32),
            pltpu.SemaphoreType.DMA((inner - 1,)),
            pltpu.SemaphoreType.DMA((inner, outer - 1)),
            pltpu.SemaphoreType.DMA((n_col // 2,)),
            pltpu.SemaphoreType.DMA((n_col // 2,)),
            pltpu.SemaphoreType.DMA((inner,)),
            pltpu.SemaphoreType.DMA((outer, inner)),
            pltpu.SemaphoreType.DMA((n_col,)),
            pltpu.SemaphoreType.DMA((iters, 2, n_col - 1)),
            pltpu.SemaphoreType.DMA((iters, 2, n_col)),
            pltpu.SemaphoreType.DMA((iters, inner - 1)),
            pltpu.SemaphoreType.DMA((iters, outer - 1)),
            pltpu.SemaphoreType.DMA((iters, inner)),
            pltpu.SemaphoreType.DMA((iters, outer)),
        ],
        compiler_params=pltpu.CompilerParams(
            collective_id=cid, has_side_effects=True, vmem_limit_bytes=60 * 1024 * 1024),
    )(chunk, pref_row)


def local(embedding, preference):
    rows_n = lax.axis_size("row")
    cols_n = lax.axis_size("col")
    row_idx = lax.axis_index("row")
    col_idx = lax.axis_index("col")
    mol = embedding.shape[2]
    width = embedding.shape[3]
    row_count = mol * cols_n
    col_count = mol * rows_n
    resp, avail = propagate(embedding.reshape(mol, width), preference, rows_n, cols_n, INNER, ITERS, 0)
    return (resp, avail)


def solution(mesh):
    placed = (P("col", "row", None, None), P("row"))
    return jax.shard_map(
        local,
        mesh=mesh,
        in_specs=placed,
        out_specs=(P("row", "col"), P("row", "col")),
        check_vma=False,
    )
```

```python
import functools

import jax
import jax.numpy as jnp
from jax import lax
from jax.experimental import pallas as pl
from jax.experimental.pallas import tpu as pltpu
from jax.sharding import PartitionSpec as P

ITERS = 2


DAMPING = 0.5

INNER = 8

MESH = pl.DeviceIdType.MESH
VMEM = pl.BlockSpec(memory_space=pltpu.VMEM)


def ap_kernel(n_row, n_col, inner, chunk, iters, chunk_ref, prefr_ref, resp_out, avail_out,
              colb3, rowb3, prefc, sim_s, resp_s, avail_s, fcol, scol, cq, pack, buf_f, buf_s, zpart, buf1,
              zsum, buf2, e_send_z, e_send_y, e_send_r, e_send_f, e_recv_c, e_recv_b, e_recv_r,
              send_t, recv_t, send_z, send_y, recv_z, recv_y):
    rows, cols = sim_s.shape
    r = lax.axis_index("row")
    c = lax.axis_index("col")
    outer = n_row // inner
    y = r // inner
    z = r % inner
    cpeers = [lax.rem(c + d, n_col) for d in range(1, n_col)]
    zpeers = [y * inner + lax.rem(z + d, inner) for d in range(1, inner)]
    ypeers = [lax.rem(y + d, outer) * inner + z for d in range(1, outer)]
    g = c * n_row + r
    target_row = g // n_col
    my_slot = g % n_col
    parity = c % 2
    sibling = c + 1 - 2 * parity
    targets = [(target_row, 2 * x + my_slot % 2) for x in range(n_col // 2)]
    sources = []
    for t in range(n_col // 2):
        gs = r * n_col + 2 * t + parity
        sources.append((gs % n_row, gs // n_row))

    def differs(dev):
        return jnp.logical_or(dev[0] != r, dev[1] != c)

    barrier = pltpu.get_barrier_semaphore()
    for p in cpeers:
        pl.semaphore_signal(barrier, inc=1, device_id={"col": p}, device_id_type=MESH)
    for p in zpeers + ypeers:
        pl.semaphore_signal(barrier, inc=1, device_id={"row": p}, device_id_type=MESH)
    for dev in targets + sources:
        @pl.when(differs(dev))
        def _():
            pl.semaphore_signal(barrier, inc=1, device_id=dev, device_id_type=MESH)
    self_in = jnp.logical_and(target_row == r, my_slot % 2 == parity).astype(jnp.int32)
    pl.semaphore_wait(barrier, (n_col - 1) + (inner - 1) + (outer - 1) + 2 * (n_col // 2 - self_in))

    copies = []
    pltpu.make_async_copy(chunk_ref, colb3.at[r], e_recv_c.at[z]).start()
    for i, p in enumerate(zpeers):
        cp = pltpu.make_async_remote_copy(
            src_ref=chunk_ref, dst_ref=colb3.at[r], send_sem=e_send_z.at[i],
            recv_sem=e_recv_c.at[z], device_id={"row": p}, device_id_type=MESH)
        cp.start()
        copies.append(cp)
    row_copies = []
    for j, dev in enumerate(targets):
        cp = pltpu.make_async_remote_copy(
            src_ref=chunk_ref, dst_ref=rowb3.at[my_slot], send_sem=e_send_r.at[j],
            recv_sem=e_recv_r.at[my_slot], device_id=dev, device_id_type=MESH)
        row_copies.append(cp)

        @pl.when(differs(dev))
        def _():
            cp.start()

        @pl.when(jnp.logical_not(differs(dev)))
        def _():
            pltpu.make_async_copy(chunk_ref, rowb3.at[my_slot], e_recv_r.at[my_slot]).start()

    prefc[...] = jnp.broadcast_to(prefr_ref[...].reshape(1, rows), (128, rows)).T
    for d in range(inner):
        zs = lax.rem(z + d, inner)
        slot = colb3.at[y * inner + zs]
        pltpu.make_async_copy(chunk_ref, slot, e_recv_c.at[zs]).wait()
        for i, p in enumerate(ypeers):
            cp = pltpu.make_async_remote_copy(
                src_ref=slot, dst_ref=slot, send_sem=e_send_y.at[d, i],
                recv_sem=e_recv_b.at[y, zs], device_id={"row": p}, device_id_type=MESH)
            cp.start()
            copies.append(cp)
    for d in range(1, outer):
        yo = lax.rem(y + d, outer)
        for s in range(inner):
            other = colb3.at[yo * inner + s]
            pltpu.make_async_copy(other, other, e_recv_b.at[yo, s]).wait()
    for t in range(n_col // 2):
        s = 2 * t + parity
        pltpu.make_async_copy(chunk_ref, rowb3.at[s], e_recv_r.at[s]).wait()
        cp = pltpu.make_async_remote_copy(
            src_ref=rowb3.at[s], dst_ref=rowb3.at[s], send_sem=e_send_f.at[t],
            recv_sem=e_recv_r.at[s], device_id={"col": sibling}, device_id_type=MESH)
        cp.start()
        copies.append(cp)
    for t in range(n_col // 2):
        s = 2 * t + 1 - parity
        pltpu.make_async_copy(chunk_ref, rowb3.at[s], e_recv_r.at[s]).wait()
    mol = chunk_ref.shape[0]
    colb_ref = colb3
    rowb_ref = rowb3


    row_start = r * rows
    col_start = c * cols
    n_chunks = rows // chunk

    def record_top(i0, summed):
        first = jnp.max(summed, axis=1, keepdims=True)
        hits = summed == first
        repeats = jnp.sum(hits.astype(jnp.float32), axis=1, keepdims=True)
        others = jnp.max(jnp.where(hits, -jnp.inf, summed), axis=1, keepdims=True)
        second = jnp.where(repeats > 1.0, first, others)
        fcol[pl.ds(i0, chunk), :] = jnp.broadcast_to(first, (chunk, 128))
        scol[pl.ds(i0, chunk), :] = jnp.broadcast_to(second, (chunk, 128))

    colb_all = colb_ref[...].reshape(cols, -1)
    rowb_all = rowb_ref[...].reshape(rows, -1)
    cb = 128 if cols % 128 == 0 else cols
    for j in range(cols // cb):
        xc = colb_all[j * cb:(j + 1) * cb, :].astype(jnp.float32)
        qc = jnp.sum(xc * xc, axis=1, keepdims=True)
        cq[0:1, pl.ds(j * cb, cb)] = jnp.broadcast_to(qc, (cb, 128)).T[0:1, :]
    xr = rowb_all.astype(jnp.float32)
    rq_s = fcol
    rq_s[...] = jnp.broadcast_to(jnp.sum(xr * xr, axis=1, keepdims=True), (rows, 128))
    rb = 128 if rows % 128 == 0 else rows
    for j in range(rows // rb):
        sim_s[pl.ds(j * rb, rb), :] = lax.dot_general(
            rowb_all[j * rb:(j + 1) * rb, :], colb_all, (((1,), (1,)), ((), ())),
            preferred_element_type=jnp.float32)

    has_diag = row_start // cols == c
    band = pl.ds(pl.multiple_of(row_start % cols, rows), rows)

    def eye():
        return lax.broadcasted_iota(jnp.int32, (rows, rows), 0) == lax.broadcasted_iota(jnp.int32, (rows, rows), 1)

    sim_s[...] = 2.0 * sim_s[...] - rq_s[:, 0:1] - cq[...]

    @pl.when(has_diag)
    def _():
        sim_s[:, band] = jnp.where(eye(), prefc[:, 0:1], sim_s[:, band])

    record_top(0, sim_s[...])
    for step in range(iters):
        first_step = step == 0
        last_step = step == iters - 1
        resp_prev, avail_prev = resp_s, avail_s
        resp_new, avail_new = (resp_out, avail_out) if last_step else (resp_s, avail_s)
        pk = pack.at[step]
        pk[0:1, :] = fcol[...].T[0:1, :]
        pk[1:2, :] = scol[...].T[0:1, :]
        for k, dst in enumerate((buf_f.at[step], buf_s.at[step])):
            src = pk.at[pl.ds(k, 1)]
            pltpu.make_async_copy(src, dst.at[pl.ds(c, 1)], recv_t.at[step, k, c]).start()
            for i, p in enumerate(cpeers):
                cp = pltpu.make_async_remote_copy(
                    src_ref=src, dst_ref=dst.at[pl.ds(c, 1)], send_sem=send_t.at[step, k, i],
                    recv_sem=recv_t.at[step, k, c], device_id={"col": p}, device_id_type=MESH)
                cp.start()
                copies.append(cp)
        for k, dst in enumerate((buf_f.at[step], buf_s.at[step])):
            for s in range(n_col):
                pltpu.make_async_copy(pk.at[pl.ds(0, 1)], dst.at[pl.ds(s, 1)], recv_t.at[step, k, s]).wait()
        firsts = buf_f[step]
        seconds = buf_s[step]
        first = jnp.max(firsts, axis=0, keepdims=True)
        at_top = firsts == first
        repeats = jnp.sum(at_top.astype(jnp.float32), axis=0, keepdims=True)
        others = jnp.max(jnp.where(at_top, -jnp.inf, firsts), axis=0, keepdims=True)
        second = jnp.where(repeats > 1.0, first, jnp.maximum(jnp.max(seconds, axis=0, keepdims=True), others))
        fcol[...] = jnp.broadcast_to(first, (128, rows)).T
        scol[...] = jnp.broadcast_to(second, (128, rows)).T

        s = sim_s[...]
        summed = s if first_step else avail_prev[...] + s
        f = fcol[:, 0:1]
        sc = scol[:, 0:1]
        fresh = s - jnp.where(summed == f, sc, f)
        if first_step:
            resp = (1.0 - DAMPING) * fresh
        else:
            resp = DAMPING * resp_prev[...] + (1.0 - DAMPING) * fresh
        resp_new[...] = resp
        zp = zpart.at[step]
        zp[...] = jnp.sum(jnp.maximum(resp, 0.0), axis=0, keepdims=True)

        @pl.when(has_diag)
        def _():
            rb_ = resp_new[:, band]
            zp[:, band] = jnp.sum(jnp.where(eye(), rb_, jnp.maximum(rb_, 0.0)), axis=0, keepdims=True)

        b1 = buf1.at[step]
        pltpu.make_async_copy(zp, b1.at[pl.ds(z, 1)], recv_z.at[step, z]).start()
        for i, p in enumerate(zpeers):
            cp = pltpu.make_async_remote_copy(
                src_ref=zp, dst_ref=b1.at[pl.ds(z, 1)], send_sem=send_z.at[step, i],
                recv_sem=recv_z.at[step, z], device_id={"row": p}, device_id_type=MESH)
            cp.start()
            copies.append(cp)
        for s in range(inner):
            pltpu.make_async_copy(zp, b1.at[pl.ds(s, 1)], recv_z.at[step, s]).wait()
        zs = zsum.at[step]
        zs[...] = jnp.sum(b1[...], axis=0, keepdims=True)
        b2 = buf2.at[step]
        pltpu.make_async_copy(zs, b2.at[pl.ds(y, 1)], recv_y.at[step, y]).start()
        for i, p in enumerate(ypeers):
            cp = pltpu.make_async_remote_copy(
                src_ref=zs, dst_ref=b2.at[pl.ds(y, 1)], send_sem=send_y.at[step, i],
                recv_sem=recv_y.at[step, y], device_id={"row": p}, device_id_type=MESH)
            cp.start()
            copies.append(cp)
        for s in range(outer):
            pltpu.make_async_copy(zs, b2.at[pl.ds(s, 1)], recv_y.at[step, s]).wait()
        colsum = jnp.sum(b2[...], axis=0, keepdims=True)

        cq[...] = colsum
        renew = jnp.minimum(colsum - jnp.maximum(resp_new[...], 0.0), 0.0)
        if first_step:
            avail_new[...] = (1.0 - DAMPING) * renew
        else:
            avail_new[...] = DAMPING * avail_prev[...] + (1.0 - DAMPING) * renew

        @pl.when(has_diag)
        def _():
            rb_ = resp_new[:, band]
            e = eye()
            positive = jnp.where(e, rb_, jnp.maximum(rb_, 0.0))
            renew_b = cq[:, band] - positive
            renew_b = jnp.where(e, renew_b, jnp.minimum(renew_b, 0.0))
            if first_step:
                avail_new[:, band] = (1.0 - DAMPING) * renew_b
            else:
                avail_new[:, band] = DAMPING * avail_prev[:, band] + (1.0 - DAMPING) * renew_b

        if not last_step:
            record_top(0, avail_new[...] + sim_s[...])
    for cp in copies:
        cp.wait_send()
    for j, dev in enumerate(targets):
        @pl.when(differs(dev))
        def _():
            row_copies[j].wait_send()


def propagate(chunk, pref_row, n_row, n_col, inner, iters, cid):
    mol, width = chunk.shape
    rows, cols = mol * n_col, mol * n_row
    outer = n_row // inner
    f32 = jnp.float32
    return pl.pallas_call(
        functools.partial(ap_kernel, n_row, n_col, inner, rows, iters),
        out_shape=(jax.ShapeDtypeStruct((rows, cols), f32), jax.ShapeDtypeStruct((rows, cols), f32)),
        in_specs=[VMEM] * 2,
        out_specs=(VMEM, VMEM),
        scratch_shapes=[
            pltpu.VMEM((n_row, mol, width), chunk.dtype),
            pltpu.VMEM((n_col, mol, width), chunk.dtype),
            pltpu.VMEM((rows, 128), f32),
            pltpu.VMEM((rows, cols), f32),
            pltpu.VMEM((rows, cols), f32),
            pltpu.VMEM((rows, cols), f32),
            pltpu.VMEM((rows, 128), f32),
            pltpu.VMEM((rows, 128), f32),
            pltpu.VMEM((1, cols), f32),
            pltpu.VMEM((iters, 2, rows), f32),
            pltpu.VMEM((iters, n_col, rows), f32),
            pltpu.VMEM((iters, n_col, rows), f32),
            pltpu.VMEM((iters, 1, cols), f32),
            pltpu.VMEM((iters, inner, cols), f32),
            pltpu.VMEM((iters, 1, cols), f32),
            pltpu.VMEM((iters, outer, cols), f32),
            pltpu.SemaphoreType.DMA((inner - 1,)),
            pltpu.SemaphoreType.DMA((inner, outer - 1)),
            pltpu.SemaphoreType.DMA((n_col // 2,)),
            pltpu.SemaphoreType.DMA((n_col // 2,)),
            pltpu.SemaphoreType.DMA((inner,)),
            pltpu.SemaphoreType.DMA((outer, inner)),
            pltpu.SemaphoreType.DMA((n_col,)),
            pltpu.SemaphoreType.DMA((iters, 2, n_col - 1)),
            pltpu.SemaphoreType.DMA((iters, 2, n_col)),
            pltpu.SemaphoreType.DMA((iters, inner - 1)),
            pltpu.SemaphoreType.DMA((iters, outer - 1)),
            pltpu.SemaphoreType.DMA((iters, inner)),
            pltpu.SemaphoreType.DMA((iters, outer)),
        ],
        compiler_params=pltpu.CompilerParams(
            collective_id=cid, has_side_effects=True, vmem_limit_bytes=60 * 1024 * 1024),
    )(chunk, pref_row)


def local(embedding, preference):
    rows_n = lax.axis_size("row")
    cols_n = lax.axis_size("col")
    row_idx = lax.axis_index("row")
    col_idx = lax.axis_index("col")
    mol = embedding.shape[2]
    width = embedding.shape[3]
    row_count = mol * cols_n
    col_count = mol * rows_n
    resp, avail = propagate(embedding.reshape(mol, width), preference, rows_n, cols_n, INNER, ITERS, 0)
    return (resp, avail)


def solution(mesh):
    placed = (P("col", "row", None, None), P("row"))
    return jax.shard_map(
        local,
        mesh=mesh,
        in_specs=placed,
        out_specs=(P("row", "col"), P("row", "col")),
        check_vma=False,
    )
```

```python
import functools

import jax
import jax.numpy as jnp
from jax import lax
from jax.experimental import pallas as pl
from jax.experimental.pallas import tpu as pltpu
from jax.sharding import PartitionSpec as P

ITERS = 2


DAMPING = 0.5

INNER = 8

MESH = pl.DeviceIdType.MESH
VMEM = pl.BlockSpec(memory_space=pltpu.VMEM)


def ap_kernel(n_row, n_col, inner, chunk, iters, chunk_ref, prefr_ref, resp_out, avail_out,
              colb3, rowb3, prefc, sim_s, resp_s, avail_s, fcol, scol, cq, pack, buf_f, buf_s, zpart, buf1,
              zsum, buf2, e_send_z, e_send_y, e_send_r, e_send_f, e_recv_c, e_recv_b, e_recv_r,
              send_t, recv_t, send_z, send_y, recv_z, recv_y):
    rows, cols = sim_s.shape
    r = lax.axis_index("row")
    c = lax.axis_index("col")
    outer = n_row // inner
    y = r // inner
    z = r % inner
    cpeers = [lax.rem(c + d, n_col) for d in range(1, n_col)]
    zpeers = [y * inner + lax.rem(z + d, inner) for d in range(1, inner)]
    ypeers = [lax.rem(y + d, outer) * inner + z for d in range(1, outer)]
    g = c * n_row + r
    target_row = g // n_col
    my_slot = g % n_col
    parity = c % 2
    sibling = c + 1 - 2 * parity
    targets = [(target_row, 2 * x + my_slot % 2) for x in range(n_col // 2)]
    sources = []
    for t in range(n_col // 2):
        gs = r * n_col + 2 * t + parity
        sources.append((gs % n_row, gs // n_row))

    def differs(dev):
        return jnp.logical_or(dev[0] != r, dev[1] != c)

    barrier = pltpu.get_barrier_semaphore()
    for p in cpeers:
        pl.semaphore_signal(barrier, inc=1, device_id={"col": p}, device_id_type=MESH)
    for p in zpeers + ypeers:
        pl.semaphore_signal(barrier, inc=1, device_id={"row": p}, device_id_type=MESH)
    for dev in targets + sources:
        @pl.when(differs(dev))
        def _():
            pl.semaphore_signal(barrier, inc=1, device_id=dev, device_id_type=MESH)
    self_in = jnp.logical_and(target_row == r, my_slot % 2 == parity).astype(jnp.int32)
    pl.semaphore_wait(barrier, (n_col - 1) + (inner - 1) + (outer - 1) + 2 * (n_col // 2 - self_in))

    copies = []
    pltpu.make_async_copy(chunk_ref, colb3.at[r], e_recv_c.at[z]).start()
    for i, p in enumerate(zpeers):
        cp = pltpu.make_async_remote_copy(
            src_ref=chunk_ref, dst_ref=colb3.at[r], send_sem=e_send_z.at[i],
            recv_sem=e_recv_c.at[z], device_id={"row": p}, device_id_type=MESH)
        cp.start()
        copies.append(cp)
    row_copies = []
    for j, dev in enumerate(targets):
        cp = pltpu.make_async_remote_copy(
            src_ref=chunk_ref, dst_ref=rowb3.at[my_slot], send_sem=e_send_r.at[j],
            recv_sem=e_recv_r.at[my_slot], device_id=dev, device_id_type=MESH)
        row_copies.append(cp)

        @pl.when(differs(dev))
        def _():
            cp.start()

        @pl.when(jnp.logical_not(differs(dev)))
        def _():
            pltpu.make_async_copy(chunk_ref, rowb3.at[my_slot], e_recv_r.at[my_slot]).start()

    prefc[...] = jnp.broadcast_to(prefr_ref[...].reshape(1, rows), (128, rows)).T
    for d in range(inner):
        zs = lax.rem(z + d, inner)
        slot = colb3.at[y * inner + zs]
        pltpu.make_async_copy(chunk_ref, slot, e_recv_c.at[zs]).wait()
        for i, p in enumerate(ypeers):
            cp = pltpu.make_async_remote_copy(
                src_ref=slot, dst_ref=slot, send_sem=e_send_y.at[d, i],
                recv_sem=e_recv_b.at[y, zs], device_id={"row": p}, device_id_type=MESH)
            cp.start()
            copies.append(cp)
    for d in range(1, outer):
        yo = lax.rem(y + d, outer)
        for s in range(inner):
            other = colb3.at[yo * inner + s]
            pltpu.make_async_copy(other, other, e_recv_b.at[yo, s]).wait()
    for t in range(n_col // 2):
        s = 2 * t + parity
        pltpu.make_async_copy(chunk_ref, rowb3.at[s], e_recv_r.at[s]).wait()
        cp = pltpu.make_async_remote_copy(
            src_ref=rowb3.at[s], dst_ref=rowb3.at[s], send_sem=e_send_f.at[t],
            recv_sem=e_recv_r.at[s], device_id={"col": sibling}, device_id_type=MESH)
        cp.start()
        copies.append(cp)
    for t in range(n_col // 2):
        s = 2 * t + 1 - parity
        pltpu.make_async_copy(chunk_ref, rowb3.at[s], e_recv_r.at[s]).wait()
    mol = chunk_ref.shape[0]
    colb_ref = colb3
    rowb_ref = rowb3


    row_start = r * rows
    col_start = c * cols
    n_chunks = rows // chunk

    def record_top(i0, summed):
        first = jnp.max(summed, axis=1, keepdims=True)
        hits = summed == first
        repeats = jnp.sum(hits.astype(jnp.float32), axis=1, keepdims=True)
        others = jnp.max(jnp.where(hits, -jnp.inf, summed), axis=1, keepdims=True)
        second = jnp.where(repeats > 1.0, first, others)
        fcol[pl.ds(i0, chunk), :] = jnp.broadcast_to(first, (chunk, 128))
        scol[pl.ds(i0, chunk), :] = jnp.broadcast_to(second, (chunk, 128))

    colb_all = colb_ref[...].reshape(cols, -1)
    rowb_all = rowb_ref[...].reshape(rows, -1)
    cb = 128 if cols % 128 == 0 else cols
    for j in range(cols // cb):
        xc = colb_all[j * cb:(j + 1) * cb, :].astype(jnp.float32)
        qc = jnp.sum(xc * xc, axis=1, keepdims=True)
        cq[0:1, pl.ds(j * cb, cb)] = jnp.broadcast_to(qc, (cb, 128)).T[0:1, :]
    xr = rowb_all.astype(jnp.float32)
    rq_s = fcol
    rq_s[...] = jnp.broadcast_to(jnp.sum(xr * xr, axis=1, keepdims=True), (rows, 128))
    rb = 128 if rows % 128 == 0 else rows
    for j in range(rows // rb):
        sim_s[pl.ds(j * rb, rb), :] = lax.dot_general(
            rowb_all[j * rb:(j + 1) * rb, :], colb_all, (((1,), (1,)), ((), ())),
            preferred_element_type=jnp.float32)

    has_diag = row_start // cols == c
    band = pl.ds(pl.multiple_of(row_start % cols, rows), rows)

    def eye():
        return lax.broadcasted_iota(jnp.int32, (rows, rows), 0) == lax.broadcasted_iota(jnp.int32, (rows, rows), 1)

    sim_s[...] = 2.0 * sim_s[...] - rq_s[:, 0:1] - cq[...]

    @pl.when(has_diag)
    def _():
        sim_s[:, band] = jnp.where(eye(), prefc[:, 0:1], sim_s[:, band])

    record_top(0, sim_s[...])
    for step in range(iters):
        first_step = step == 0
        last_step = step == iters - 1
        resp_prev, avail_prev = resp_s, avail_s
        resp_new, avail_new = (resp_out, avail_out) if last_step else (resp_s, avail_s)
        pk = pack.at[step]
        pk[0:1, :] = fcol[...].T[0:1, :]
        pk[1:2, :] = scol[...].T[0:1, :]
        for k, dst in enumerate((buf_f.at[step], buf_s.at[step])):
            src = pk.at[pl.ds(k, 1)]
            pltpu.make_async_copy(src, dst.at[pl.ds(c, 1)], recv_t.at[step, k, c]).start()
            for i, p in enumerate(cpeers):
                cp = pltpu.make_async_remote_copy(
                    src_ref=src, dst_ref=dst.at[pl.ds(c, 1)], send_sem=send_t.at[step, k, i],
                    recv_sem=recv_t.at[step, k, c], device_id={"col": p}, device_id_type=MESH)
                cp.start()
                copies.append(cp)
        for k, dst in enumerate((buf_f.at[step], buf_s.at[step])):
            for s in range(n_col):
                pltpu.make_async_copy(pk.at[pl.ds(0, 1)], dst.at[pl.ds(s, 1)], recv_t.at[step, k, s]).wait()
        firsts = buf_f[step]
        seconds = buf_s[step]
        first = jnp.max(firsts, axis=0, keepdims=True)
        at_top = firsts == first
        repeats = jnp.sum(at_top.astype(jnp.float32), axis=0, keepdims=True)
        others = jnp.max(jnp.where(at_top, -jnp.inf, firsts), axis=0, keepdims=True)
        second = jnp.where(repeats > 1.0, first, jnp.maximum(jnp.max(seconds, axis=0, keepdims=True), others))
        fcol[...] = jnp.broadcast_to(first, (128, rows)).T
        scol[...] = jnp.broadcast_to(second, (128, rows)).T

        s = sim_s[...]
        summed = s if first_step else avail_prev[...] + s
        f = fcol[:, 0:1]
        sc = scol[:, 0:1]
        fresh = s - jnp.where(summed == f, sc, f)
        if first_step:
            resp = (1.0 - DAMPING) * fresh
        else:
            resp = DAMPING * resp_prev[...] + (1.0 - DAMPING) * fresh
        resp_new[...] = resp
        zp = zpart.at[step]
        zp[...] = jnp.sum(jnp.maximum(resp, 0.0), axis=0, keepdims=True)

        @pl.when(has_diag)
        def _():
            rb_ = resp_new[:, band]
            zp[:, band] = jnp.sum(jnp.where(eye(), rb_, jnp.maximum(rb_, 0.0)), axis=0, keepdims=True)

        b1 = buf1.at[step]
        pltpu.make_async_copy(zp, b1.at[pl.ds(z, 1)], recv_z.at[step, z]).start()
        for i, p in enumerate(zpeers):
            cp = pltpu.make_async_remote_copy(
                src_ref=zp, dst_ref=b1.at[pl.ds(z, 1)], send_sem=send_z.at[step, i],
                recv_sem=recv_z.at[step, z], device_id={"row": p}, device_id_type=MESH)
            cp.start()
            copies.append(cp)
        for s in range(inner):
            pltpu.make_async_copy(zp, b1.at[pl.ds(s, 1)], recv_z.at[step, s]).wait()
        zs = zsum.at[step]
        zs[...] = jnp.sum(b1[...], axis=0, keepdims=True)
        b2 = buf2.at[step]
        pltpu.make_async_copy(zs, b2.at[pl.ds(y, 1)], recv_y.at[step, y]).start()
        for i, p in enumerate(ypeers):
            cp = pltpu.make_async_remote_copy(
                src_ref=zs, dst_ref=b2.at[pl.ds(y, 1)], send_sem=send_y.at[step, i],
                recv_sem=recv_y.at[step, y], device_id={"row": p}, device_id_type=MESH)
            cp.start()
            copies.append(cp)
        for s in range(outer):
            pltpu.make_async_copy(zs, b2.at[pl.ds(s, 1)], recv_y.at[step, s]).wait()
        colsum = jnp.sum(b2[...], axis=0, keepdims=True)

        cq[...] = colsum
        renew = jnp.minimum(colsum - jnp.maximum(resp_new[...], 0.0), 0.0)
        if first_step:
            avail_new[...] = (1.0 - DAMPING) * renew
        else:
            avail_new[...] = DAMPING * avail_prev[...] + (1.0 - DAMPING) * renew

        @pl.when(has_diag)
        def _():
            rb_ = resp_new[:, band]
            e = eye()
            positive = jnp.where(e, rb_, jnp.maximum(rb_, 0.0))
            renew_b = cq[:, band] - positive
            renew_b = jnp.where(e, renew_b, jnp.minimum(renew_b, 0.0))
            if first_step:
                avail_new[:, band] = (1.0 - DAMPING) * renew_b
            else:
                avail_new[:, band] = DAMPING * avail_prev[:, band] + (1.0 - DAMPING) * renew_b

        if not last_step:
            record_top(0, avail_new[...] + sim_s[...])
    for cp in copies:
        cp.wait_send()
    for j, dev in enumerate(targets):
        @pl.when(differs(dev))
        def _():
            row_copies[j].wait_send()


def propagate(chunk, pref_row, n_row, n_col, inner, iters, cid):
    mol, width = chunk.shape
    rows, cols = mol * n_col, mol * n_row
    outer = n_row // inner
    f32 = jnp.float32
    return pl.pallas_call(
        functools.partial(ap_kernel, n_row, n_col, inner, rows, iters),
        out_shape=(pltpu.VMEM((rows, cols), f32), pltpu.VMEM((rows, cols), f32)),
        in_specs=[VMEM] * 2,
        out_specs=(VMEM, VMEM),
        scratch_shapes=[
            pltpu.VMEM((n_row, mol, width), chunk.dtype),
            pltpu.VMEM((n_col, mol, width), chunk.dtype),
            pltpu.VMEM((rows, 128), f32),
            pltpu.VMEM((rows, cols), f32),
            pltpu.VMEM((rows, cols), f32),
            pltpu.VMEM((rows, cols), f32),
            pltpu.VMEM((rows, 128), f32),
            pltpu.VMEM((rows, 128), f32),
            pltpu.VMEM((1, cols), f32),
            pltpu.VMEM((iters, 2, rows), f32),
            pltpu.VMEM((iters, n_col, rows), f32),
            pltpu.VMEM((iters, n_col, rows), f32),
            pltpu.VMEM((iters, 1, cols), f32),
            pltpu.VMEM((iters, inner, cols), f32),
            pltpu.VMEM((iters, 1, cols), f32),
            pltpu.VMEM((iters, outer, cols), f32),
            pltpu.SemaphoreType.DMA((inner - 1,)),
            pltpu.SemaphoreType.DMA((inner, outer - 1)),
            pltpu.SemaphoreType.DMA((n_col // 2,)),
            pltpu.SemaphoreType.DMA((n_col // 2,)),
            pltpu.SemaphoreType.DMA((inner,)),
            pltpu.SemaphoreType.DMA((outer, inner)),
            pltpu.SemaphoreType.DMA((n_col,)),
            pltpu.SemaphoreType.DMA((iters, 2, n_col - 1)),
            pltpu.SemaphoreType.DMA((iters, 2, n_col)),
            pltpu.SemaphoreType.DMA((iters, inner - 1)),
            pltpu.SemaphoreType.DMA((iters, outer - 1)),
            pltpu.SemaphoreType.DMA((iters, inner)),
            pltpu.SemaphoreType.DMA((iters, outer)),
        ],
        compiler_params=pltpu.CompilerParams(
            collective_id=cid, has_side_effects=True, vmem_limit_bytes=32 * 1024 * 1024),
    )(chunk, pref_row)


def local(embedding, preference):
    rows_n = lax.axis_size("row")
    cols_n = lax.axis_size("col")
    row_idx = lax.axis_index("row")
    col_idx = lax.axis_index("col")
    mol = embedding.shape[2]
    width = embedding.shape[3]
    row_count = mol * cols_n
    col_count = mol * rows_n
    resp, avail = propagate(embedding.reshape(mol, width), preference, rows_n, cols_n, INNER, ITERS, 0)
    return (resp, avail)


def solution(mesh):
    placed = (P("col", "row", None, None), P("row"))
    return jax.shard_map(
        local,
        mesh=mesh,
        in_specs=placed,
        out_specs=(P("row", "col"), P("row", "col")),
        check_vma=False,
    )
```

```python
import functools

import jax
import jax.numpy as jnp
from jax import lax
from jax.experimental import pallas as pl
from jax.experimental.pallas import tpu as pltpu
from jax.sharding import PartitionSpec as P

ITERS = 2


DAMPING = 0.5

INNER = 8

MESH = pl.DeviceIdType.MESH
VMEM = pl.BlockSpec(memory_space=pltpu.VMEM)


def ap_kernel(n_row, n_col, inner, chunk, iters, chunk_ref, prefr_ref, resp_out, avail_out,
              colb3, rowb3, prefc, sim_s, resp_s, avail_s, fcol, scol, cq, pack, buf_f, buf_s, zpart, buf1,
              zsum, buf2, e_send_z, e_send_y, e_send_r, e_send_f, e_recv_c, e_recv_b, e_recv_r,
              send_t, recv_t, send_z, send_y, recv_z, recv_y):
    rows, cols = sim_s.shape
    r = lax.axis_index("row")
    c = lax.axis_index("col")
    outer = n_row // inner
    y = r // inner
    z = r % inner
    cpeers = [lax.rem(c + d, n_col) for d in range(1, n_col)]
    zpeers = [y * inner + lax.rem(z + d, inner) for d in range(1, inner)]
    ypeers = [lax.rem(y + d, outer) * inner + z for d in range(1, outer)]
    g = c * n_row + r
    target_row = g // n_col
    my_slot = g % n_col
    parity = c % 2
    sibling = c + 1 - 2 * parity
    targets = [(target_row, 2 * x + my_slot % 2) for x in range(n_col // 2)]
    sources = []
    for t in range(n_col // 2):
        gs = r * n_col + 2 * t + parity
        sources.append((gs % n_row, gs // n_row))

    def differs(dev):
        return jnp.logical_or(dev[0] != r, dev[1] != c)

    barrier = pltpu.get_barrier_semaphore()
    for p in cpeers:
        pl.semaphore_signal(barrier, inc=1, device_id={"col": p}, device_id_type=MESH)
    for p in zpeers + ypeers:
        pl.semaphore_signal(barrier, inc=1, device_id={"row": p}, device_id_type=MESH)
    for dev in targets + sources:
        @pl.when(differs(dev))
        def _():
            pl.semaphore_signal(barrier, inc=1, device_id=dev, device_id_type=MESH)
    self_in = jnp.logical_and(target_row == r, my_slot % 2 == parity).astype(jnp.int32)
    pl.semaphore_wait(barrier, (n_col - 1) + (inner - 1) + (outer - 1) + 2 * (n_col // 2 - self_in))

    copies = []
    pltpu.make_async_copy(chunk_ref, colb3.at[r], e_recv_c.at[z]).start()
    for i, p in enumerate(zpeers):
        cp = pltpu.make_async_remote_copy(
            src_ref=chunk_ref, dst_ref=colb3.at[r], send_sem=e_send_z.at[i],
            recv_sem=e_recv_c.at[z], device_id={"row": p}, device_id_type=MESH)
        cp.start()
        copies.append(cp)
    row_copies = []
    for j, dev in enumerate(targets):
        cp = pltpu.make_async_remote_copy(
            src_ref=chunk_ref, dst_ref=rowb3.at[my_slot], send_sem=e_send_r.at[j],
            recv_sem=e_recv_r.at[my_slot], device_id=dev, device_id_type=MESH)
        row_copies.append(cp)

        @pl.when(differs(dev))
        def _():
            cp.start()

        @pl.when(jnp.logical_not(differs(dev)))
        def _():
            pltpu.make_async_copy(chunk_ref, rowb3.at[my_slot], e_recv_r.at[my_slot]).start()

    prefc[...] = jnp.broadcast_to(prefr_ref[...].reshape(1, rows), (128, rows)).T
    for d in range(inner):
        zs = lax.rem(z + d, inner)
        slot = colb3.at[y * inner + zs]
        pltpu.make_async_copy(chunk_ref, slot, e_recv_c.at[zs]).wait()
        for i, p in enumerate(ypeers):
            cp = pltpu.make_async_remote_copy(
                src_ref=slot, dst_ref=slot, send_sem=e_send_y.at[d, i],
                recv_sem=e_recv_b.at[y, zs], device_id={"row": p}, device_id_type=MESH)
            cp.start()
            copies.append(cp)
    for d in range(1, outer):
        yo = lax.rem(y + d, outer)
        for s in range(inner):
            other = colb3.at[yo * inner + s]
            pltpu.make_async_copy(other, other, e_recv_b.at[yo, s]).wait()
    for t in range(n_col // 2):
        s = 2 * t + parity
        pltpu.make_async_copy(chunk_ref, rowb3.at[s], e_recv_r.at[s]).wait()
        cp = pltpu.make_async_remote_copy(
            src_ref=rowb3.at[s], dst_ref=rowb3.at[s], send_sem=e_send_f.at[t],
            recv_sem=e_recv_r.at[s], device_id={"col": sibling}, device_id_type=MESH)
        cp.start()
        copies.append(cp)
    for t in range(n_col // 2):
        s = 2 * t + 1 - parity
        pltpu.make_async_copy(chunk_ref, rowb3.at[s], e_recv_r.at[s]).wait()
    mol = chunk_ref.shape[0]
    colb_ref = colb3
    rowb_ref = rowb3


    row_start = r * rows
    col_start = c * cols
    n_chunks = rows // chunk

    def record_top(i0, summed):
        first = jnp.max(summed, axis=1, keepdims=True)
        hits = summed == first
        repeats = jnp.sum(hits.astype(jnp.float32), axis=1, keepdims=True)
        others = jnp.max(jnp.where(hits, -jnp.inf, summed), axis=1, keepdims=True)
        second = jnp.where(repeats > 1.0, first, others)
        fcol[pl.ds(i0, chunk), :] = jnp.broadcast_to(first, (chunk, 128))
        scol[pl.ds(i0, chunk), :] = jnp.broadcast_to(second, (chunk, 128))

    colb_all = colb_ref[...].reshape(cols, -1)
    rowb_all = rowb_ref[...].reshape(rows, -1)
    cb = 128 if cols % 128 == 0 else cols
    for j in range(cols // cb):
        xc = colb_all[j * cb:(j + 1) * cb, :].astype(jnp.float32)
        qc = jnp.sum(xc * xc, axis=1, keepdims=True)
        cq[0:1, pl.ds(j * cb, cb)] = jnp.broadcast_to(qc, (cb, 128)).T[0:1, :]
    xr = rowb_all.astype(jnp.float32)
    rq_s = fcol
    rq_s[...] = jnp.broadcast_to(jnp.sum(xr * xr, axis=1, keepdims=True), (rows, 128))
    rb = 128 if rows % 128 == 0 else rows
    for j in range(rows // rb):
        sim_s[pl.ds(j * rb, rb), :] = lax.dot_general(
            rowb_all[j * rb:(j + 1) * rb, :], colb_all, (((1,), (1,)), ((), ())),
            preferred_element_type=jnp.float32)

    has_diag = row_start // cols == c
    band = pl.ds(pl.multiple_of(row_start % cols, rows), rows)

    def eye():
        return lax.broadcasted_iota(jnp.int32, (rows, rows), 0) == lax.broadcasted_iota(jnp.int32, (rows, rows), 1)

    sim_s[...] = 2.0 * sim_s[...] - rq_s[:, 0:1] - cq[...]

    @pl.when(has_diag)
    def _():
        sim_s[:, band] = jnp.where(eye(), prefc[:, 0:1], sim_s[:, band])

    record_top(0, sim_s[...])
    for step in range(iters):
        first_step = step == 0
        last_step = step == iters - 1
        resp_prev, avail_prev = resp_s, avail_s
        resp_new, avail_new = (resp_out, avail_out) if last_step else (resp_s, avail_s)
        pk = pack.at[step]
        pk[0:1, :] = fcol[...].T[0:1, :]
        pk[1:2, :] = scol[...].T[0:1, :]
        dst = buf_f.at[step]
        pltpu.make_async_copy(pk, dst.at[c], recv_t.at[step, 0, c]).start()
        for i, p in enumerate(cpeers):
            cp = pltpu.make_async_remote_copy(
                src_ref=pk, dst_ref=dst.at[c], send_sem=send_t.at[step, 0, i],
                recv_sem=recv_t.at[step, 0, c], device_id={"col": p}, device_id_type=MESH)
            cp.start()
            copies.append(cp)
        for s in range(n_col):
            pltpu.make_async_copy(pk, dst.at[s], recv_t.at[step, 0, s]).wait()
        firsts = dst[:, 0, :]
        seconds = dst[:, 1, :]
        first = jnp.max(firsts, axis=0, keepdims=True)
        at_top = firsts == first
        repeats = jnp.sum(at_top.astype(jnp.float32), axis=0, keepdims=True)
        others = jnp.max(jnp.where(at_top, -jnp.inf, firsts), axis=0, keepdims=True)
        second = jnp.where(repeats > 1.0, first, jnp.maximum(jnp.max(seconds, axis=0, keepdims=True), others))
        fcol[...] = jnp.broadcast_to(first, (128, rows)).T
        scol[...] = jnp.broadcast_to(second, (128, rows)).T

        s = sim_s[...]
        summed = s if first_step else avail_prev[...] + s
        f = fcol[:, 0:1]
        sc = scol[:, 0:1]
        fresh = s - jnp.where(summed == f, sc, f)
        if first_step:
            resp = (1.0 - DAMPING) * fresh
        else:
            resp = DAMPING * resp_prev[...] + (1.0 - DAMPING) * fresh
        resp_new[...] = resp
        zp = zpart.at[step]
        zp[...] = jnp.sum(jnp.maximum(resp, 0.0), axis=0, keepdims=True)

        @pl.when(has_diag)
        def _():
            rb_ = resp_new[:, band]
            zp[:, band] = jnp.sum(jnp.where(eye(), rb_, jnp.maximum(rb_, 0.0)), axis=0, keepdims=True)

        b1 = buf1.at[step]
        pltpu.make_async_copy(zp, b1.at[pl.ds(z, 1)], recv_z.at[step, z]).start()
        for i, p in enumerate(zpeers):
            cp = pltpu.make_async_remote_copy(
                src_ref=zp, dst_ref=b1.at[pl.ds(z, 1)], send_sem=send_z.at[step, i],
                recv_sem=recv_z.at[step, z], device_id={"row": p}, device_id_type=MESH)
            cp.start()
            copies.append(cp)
        for s in range(inner):
            pltpu.make_async_copy(zp, b1.at[pl.ds(s, 1)], recv_z.at[step, s]).wait()
        zs = zsum.at[step]
        zs[...] = jnp.sum(b1[...], axis=0, keepdims=True)
        b2 = buf2.at[step]
        pltpu.make_async_copy(zs, b2.at[pl.ds(y, 1)], recv_y.at[step, y]).start()
        for i, p in enumerate(ypeers):
            cp = pltpu.make_async_remote_copy(
                src_ref=zs, dst_ref=b2.at[pl.ds(y, 1)], send_sem=send_y.at[step, i],
                recv_sem=recv_y.at[step, y], device_id={"row": p}, device_id_type=MESH)
            cp.start()
            copies.append(cp)
        for s in range(outer):
            pltpu.make_async_copy(zs, b2.at[pl.ds(s, 1)], recv_y.at[step, s]).wait()
        colsum = jnp.sum(b2[...], axis=0, keepdims=True)

        cq[...] = colsum
        renew = jnp.minimum(colsum - jnp.maximum(resp_new[...], 0.0), 0.0)
        if first_step:
            avail_new[...] = (1.0 - DAMPING) * renew
        else:
            avail_new[...] = DAMPING * avail_prev[...] + (1.0 - DAMPING) * renew

        @pl.when(has_diag)
        def _():
            rb_ = resp_new[:, band]
            e = eye()
            positive = jnp.where(e, rb_, jnp.maximum(rb_, 0.0))
            renew_b = cq[:, band] - positive
            renew_b = jnp.where(e, renew_b, jnp.minimum(renew_b, 0.0))
            if first_step:
                avail_new[:, band] = (1.0 - DAMPING) * renew_b
            else:
                avail_new[:, band] = DAMPING * avail_prev[:, band] + (1.0 - DAMPING) * renew_b

        if not last_step:
            record_top(0, avail_new[...] + sim_s[...])
    for cp in copies:
        cp.wait_send()
    for j, dev in enumerate(targets):
        @pl.when(differs(dev))
        def _():
            row_copies[j].wait_send()


def propagate(chunk, pref_row, n_row, n_col, inner, iters, cid):
    mol, width = chunk.shape
    rows, cols = mol * n_col, mol * n_row
    outer = n_row // inner
    f32 = jnp.float32
    return pl.pallas_call(
        functools.partial(ap_kernel, n_row, n_col, inner, rows, iters),
        out_shape=(pltpu.VMEM((rows, cols), f32), pltpu.VMEM((rows, cols), f32)),
        in_specs=[VMEM] * 2,
        out_specs=(VMEM, VMEM),
        scratch_shapes=[
            pltpu.VMEM((n_row, mol, width), chunk.dtype),
            pltpu.VMEM((n_col, mol, width), chunk.dtype),
            pltpu.VMEM((rows, 128), f32),
            pltpu.VMEM((rows, cols), f32),
            pltpu.VMEM((rows, cols), f32),
            pltpu.VMEM((rows, cols), f32),
            pltpu.VMEM((rows, 128), f32),
            pltpu.VMEM((rows, 128), f32),
            pltpu.VMEM((1, cols), f32),
            pltpu.VMEM((iters, 2, rows), f32),
            pltpu.VMEM((iters, n_col, 2, rows), f32),
            pltpu.VMEM((iters, n_col, rows), f32),
            pltpu.VMEM((iters, 1, cols), f32),
            pltpu.VMEM((iters, inner, cols), f32),
            pltpu.VMEM((iters, 1, cols), f32),
            pltpu.VMEM((iters, outer, cols), f32),
            pltpu.SemaphoreType.DMA((inner - 1,)),
            pltpu.SemaphoreType.DMA((inner, outer - 1)),
            pltpu.SemaphoreType.DMA((n_col // 2,)),
            pltpu.SemaphoreType.DMA((n_col // 2,)),
            pltpu.SemaphoreType.DMA((inner,)),
            pltpu.SemaphoreType.DMA((outer, inner)),
            pltpu.SemaphoreType.DMA((n_col,)),
            pltpu.SemaphoreType.DMA((iters, 2, n_col - 1)),
            pltpu.SemaphoreType.DMA((iters, 2, n_col)),
            pltpu.SemaphoreType.DMA((iters, inner - 1)),
            pltpu.SemaphoreType.DMA((iters, outer - 1)),
            pltpu.SemaphoreType.DMA((iters, inner)),
            pltpu.SemaphoreType.DMA((iters, outer)),
        ],
        compiler_params=pltpu.CompilerParams(
            collective_id=cid, has_side_effects=True, vmem_limit_bytes=32 * 1024 * 1024),
    )(chunk, pref_row)


def local(embedding, preference):
    rows_n = lax.axis_size("row")
    cols_n = lax.axis_size("col")
    row_idx = lax.axis_index("row")
    col_idx = lax.axis_index("col")
    mol = embedding.shape[2]
    width = embedding.shape[3]
    row_count = mol * cols_n
    col_count = mol * rows_n
    resp, avail = propagate(embedding.reshape(mol, width), preference, rows_n, cols_n, INNER, ITERS, 0)
    return (resp, avail)


def solution(mesh):
    placed = (P("col", "row", None, None), P("row"))
    return jax.shard_map(
        local,
        mesh=mesh,
        in_specs=placed,
        out_specs=(P("row", "col"), P("row", "col")),
        check_vma=False,
    )
```

```python
import functools

import jax
import jax.numpy as jnp
from jax import lax
from jax.experimental import pallas as pl
from jax.experimental.pallas import tpu as pltpu
from jax.sharding import PartitionSpec as P

ITERS = 2


DAMPING = 0.5

INNER = 8

MESH = pl.DeviceIdType.MESH
VMEM = pl.BlockSpec(memory_space=pltpu.VMEM)


def ap_kernel(n_row, n_col, inner, chunk, iters, chunk_ref, prefr_ref, resp_out, avail_out,
              colb3, rowb3, prefc, sim_s, resp_s, avail_s, fcol, scol, cq, pack, buf_f, buf_s, zpart, buf1,
              zsum, buf2, e_send_z, e_send_y, e_send_r, e_send_f, e_recv_c, e_recv_b, e_recv_r,
              send_t, recv_t, send_z, send_y, recv_z, recv_y):
    rows, cols = sim_s.shape
    r = lax.axis_index("row")
    c = lax.axis_index("col")
    outer = n_row // inner
    y = r // inner
    z = r % inner
    cpeers = [lax.rem(c + d, n_col) for d in range(1, n_col)]
    zpeers = [y * inner + lax.rem(z + d, inner) for d in range(1, inner)]
    ypeers = [lax.rem(y + d, outer) * inner + z for d in range(1, outer)]
    g = c * n_row + r
    target_row = g // n_col
    my_slot = g % n_col
    parity = c % 2
    sibling = c + 1 - 2 * parity
    targets = [(target_row, 2 * x + my_slot % 2) for x in range(n_col // 2)]
    sources = []
    for t in range(n_col // 2):
        gs = r * n_col + 2 * t + parity
        sources.append((gs % n_row, gs // n_row))

    def differs(dev):
        return jnp.logical_or(dev[0] != r, dev[1] != c)

    barrier = pltpu.get_barrier_semaphore()
    for p in cpeers:
        pl.semaphore_signal(barrier, inc=1, device_id={"col": p}, device_id_type=MESH)
    for p in zpeers + ypeers:
        pl.semaphore_signal(barrier, inc=1, device_id={"row": p}, device_id_type=MESH)
    for dev in targets + sources:
        @pl.when(differs(dev))
        def _():
            pl.semaphore_signal(barrier, inc=1, device_id=dev, device_id_type=MESH)
    self_in = jnp.logical_and(target_row == r, my_slot % 2 == parity).astype(jnp.int32)
    pl.semaphore_wait(barrier, (n_col - 1) + (inner - 1) + (outer - 1) + 2 * (n_col // 2 - self_in))

    copies = []
    pltpu.make_async_copy(chunk_ref, colb3.at[r], e_recv_c.at[z]).start()
    for i, p in enumerate(zpeers):
        cp = pltpu.make_async_remote_copy(
            src_ref=chunk_ref, dst_ref=colb3.at[r], send_sem=e_send_z.at[i],
            recv_sem=e_recv_c.at[z], device_id={"row": p}, device_id_type=MESH)
        cp.start()
        copies.append(cp)
    row_copies = []
    for j, dev in enumerate(targets):
        cp = pltpu.make_async_remote_copy(
            src_ref=chunk_ref, dst_ref=rowb3.at[my_slot], send_sem=e_send_r.at[j],
            recv_sem=e_recv_r.at[my_slot], device_id=dev, device_id_type=MESH)
        row_copies.append(cp)

        @pl.when(differs(dev))
        def _():
            cp.start()

        @pl.when(jnp.logical_not(differs(dev)))
        def _():
            pltpu.make_async_copy(chunk_ref, rowb3.at[my_slot], e_recv_r.at[my_slot]).start()

    prefc[...] = jnp.broadcast_to(prefr_ref[...].reshape(1, rows), (128, rows)).T
    for d in range(inner):
        zs = lax.rem(z + d, inner)
        slot = colb3.at[y * inner + zs]
        pltpu.make_async_copy(chunk_ref, slot, e_recv_c.at[zs]).wait()
        for i, p in enumerate(ypeers):
            cp = pltpu.make_async_remote_copy(
                src_ref=slot, dst_ref=slot, send_sem=e_send_y.at[d, i],
                recv_sem=e_recv_b.at[y, zs], device_id={"row": p}, device_id_type=MESH)
            cp.start()
            copies.append(cp)
    for t in range(n_col // 2):
        s = 2 * t + parity
        pltpu.make_async_copy(chunk_ref, rowb3.at[s], e_recv_r.at[s]).wait()
        cp = pltpu.make_async_remote_copy(
            src_ref=rowb3.at[s], dst_ref=rowb3.at[s], send_sem=e_send_f.at[t],
            recv_sem=e_recv_r.at[s], device_id={"col": sibling}, device_id_type=MESH)
        cp.start()
        copies.append(cp)
    for t in range(n_col // 2):
        s = 2 * t + 1 - parity
        pltpu.make_async_copy(chunk_ref, rowb3.at[s], e_recv_r.at[s]).wait()
    mol = chunk_ref.shape[0]
    colb_ref = colb3
    rowb_ref = rowb3


    row_start = r * rows
    col_start = c * cols
    n_chunks = rows // chunk

    def record_top(i0, summed):
        first = jnp.max(summed, axis=1, keepdims=True)
        hits = summed == first
        repeats = jnp.sum(hits.astype(jnp.float32), axis=1, keepdims=True)
        others = jnp.max(jnp.where(hits, -jnp.inf, summed), axis=1, keepdims=True)
        second = jnp.where(repeats > 1.0, first, others)
        fcol[pl.ds(i0, chunk), :] = jnp.broadcast_to(first, (chunk, 128))
        scol[pl.ds(i0, chunk), :] = jnp.broadcast_to(second, (chunk, 128))

    rowb_all = rowb_ref[...].reshape(rows, -1)
    xr = rowb_all.astype(jnp.float32)
    rq_s = fcol
    rq_s[...] = jnp.broadcast_to(jnp.sum(xr * xr, axis=1, keepdims=True), (rows, 128))
    blk = inner * mol
    for d in range(outer):
        yo = lax.rem(y + d, outer)
        if d > 0:
            for s in range(inner):
                other = colb3.at[yo * inner + s]
                pltpu.make_async_copy(other, other, e_recv_b.at[yo, s]).wait()
        xb = colb_ref[pl.ds(yo * inner, inner)].reshape(blk, -1)
        xc = xb.astype(jnp.float32)
        qc = jnp.sum(xc * xc, axis=1, keepdims=True)
        cols_at = pl.ds(pl.multiple_of(yo * blk, blk), blk)
        cq[:, cols_at] = jnp.broadcast_to(qc, (blk, 128)).T[0:1, :]
        sim_s[:, cols_at] = lax.dot_general(
            rowb_all, xb, (((1,), (1,)), ((), ())), preferred_element_type=jnp.float32)

    has_diag = row_start // cols == c
    band = pl.ds(pl.multiple_of(row_start % cols, rows), rows)

    def eye():
        return lax.broadcasted_iota(jnp.int32, (rows, rows), 0) == lax.broadcasted_iota(jnp.int32, (rows, rows), 1)

    sim_s[...] = 2.0 * sim_s[...] - rq_s[:, 0:1] - cq[...]

    @pl.when(has_diag)
    def _():
        sim_s[:, band] = jnp.where(eye(), prefc[:, 0:1], sim_s[:, band])

    record_top(0, sim_s[...])
    for step in range(iters):
        first_step = step == 0
        last_step = step == iters - 1
        resp_prev, avail_prev = resp_s, avail_s
        resp_new, avail_new = (resp_out, avail_out) if last_step else (resp_s, avail_s)
        pk = pack.at[step]
        pk[0:1, :] = fcol[...].T[0:1, :]
        pk[1:2, :] = scol[...].T[0:1, :]
        for k, dst in enumerate((buf_f.at[step], buf_s.at[step])):
            src = pk.at[pl.ds(k, 1)]
            pltpu.make_async_copy(src, dst.at[pl.ds(c, 1)], recv_t.at[step, k, c]).start()
            for i, p in enumerate(cpeers):
                cp = pltpu.make_async_remote_copy(
                    src_ref=src, dst_ref=dst.at[pl.ds(c, 1)], send_sem=send_t.at[step, k, i],
                    recv_sem=recv_t.at[step, k, c], device_id={"col": p}, device_id_type=MESH)
                cp.start()
                copies.append(cp)
        for k, dst in enumerate((buf_f.at[step], buf_s.at[step])):
            for s in range(n_col):
                pltpu.make_async_copy(pk.at[pl.ds(0, 1)], dst.at[pl.ds(s, 1)], recv_t.at[step, k, s]).wait()
        firsts = buf_f[step]
        seconds = buf_s[step]
        first = jnp.max(firsts, axis=0, keepdims=True)
        at_top = firsts == first
        repeats = jnp.sum(at_top.astype(jnp.float32), axis=0, keepdims=True)
        others = jnp.max(jnp.where(at_top, -jnp.inf, firsts), axis=0, keepdims=True)
        second = jnp.where(repeats > 1.0, first, jnp.maximum(jnp.max(seconds, axis=0, keepdims=True), others))
        fcol[...] = jnp.broadcast_to(first, (128, rows)).T
        scol[...] = jnp.broadcast_to(second, (128, rows)).T

        s = sim_s[...]
        summed = s if first_step else avail_prev[...] + s
        f = fcol[:, 0:1]
        sc = scol[:, 0:1]
        fresh = s - jnp.where(summed == f, sc, f)
        if first_step:
            resp = (1.0 - DAMPING) * fresh
        else:
            resp = DAMPING * resp_prev[...] + (1.0 - DAMPING) * fresh
        resp_new[...] = resp
        zp = zpart.at[step]
        zp[...] = jnp.sum(jnp.maximum(resp, 0.0), axis=0, keepdims=True)

        @pl.when(has_diag)
        def _():
            rb_ = resp_new[:, band]
            zp[:, band] = jnp.sum(jnp.where(eye(), rb_, jnp.maximum(rb_, 0.0)), axis=0, keepdims=True)

        b1 = buf1.at[step]
        pltpu.make_async_copy(zp, b1.at[pl.ds(z, 1)], recv_z.at[step, z]).start()
        for i, p in enumerate(zpeers):
            cp = pltpu.make_async_remote_copy(
                src_ref=zp, dst_ref=b1.at[pl.ds(z, 1)], send_sem=send_z.at[step, i],
                recv_sem=recv_z.at[step, z], device_id={"row": p}, device_id_type=MESH)
            cp.start()
            copies.append(cp)
        for s in range(inner):
            pltpu.make_async_copy(zp, b1.at[pl.ds(s, 1)], recv_z.at[step, s]).wait()
        zs = zsum.at[step]
        zs[...] = jnp.sum(b1[...], axis=0, keepdims=True)
        b2 = buf2.at[step]
        pltpu.make_async_copy(zs, b2.at[pl.ds(y, 1)], recv_y.at[step, y]).start()
        for i, p in enumerate(ypeers):
            cp = pltpu.make_async_remote_copy(
                src_ref=zs, dst_ref=b2.at[pl.ds(y, 1)], send_sem=send_y.at[step, i],
                recv_sem=recv_y.at[step, y], device_id={"row": p}, device_id_type=MESH)
            cp.start()
            copies.append(cp)
        for s in range(outer):
            pltpu.make_async_copy(zs, b2.at[pl.ds(s, 1)], recv_y.at[step, s]).wait()
        colsum = jnp.sum(b2[...], axis=0, keepdims=True)

        cq[...] = colsum
        renew = jnp.minimum(colsum - jnp.maximum(resp_new[...], 0.0), 0.0)
        if first_step:
            avail_new[...] = (1.0 - DAMPING) * renew
        else:
            avail_new[...] = DAMPING * avail_prev[...] + (1.0 - DAMPING) * renew

        @pl.when(has_diag)
        def _():
            rb_ = resp_new[:, band]
            e = eye()
            positive = jnp.where(e, rb_, jnp.maximum(rb_, 0.0))
            renew_b = cq[:, band] - positive
            renew_b = jnp.where(e, renew_b, jnp.minimum(renew_b, 0.0))
            if first_step:
                avail_new[:, band] = (1.0 - DAMPING) * renew_b
            else:
                avail_new[:, band] = DAMPING * avail_prev[:, band] + (1.0 - DAMPING) * renew_b

        if not last_step:
            record_top(0, avail_new[...] + sim_s[...])
    for cp in copies:
        cp.wait_send()
    for j, dev in enumerate(targets):
        @pl.when(differs(dev))
        def _():
            row_copies[j].wait_send()


def propagate(chunk, pref_row, n_row, n_col, inner, iters, cid):
    mol, width = chunk.shape
    rows, cols = mol * n_col, mol * n_row
    outer = n_row // inner
    f32 = jnp.float32
    return pl.pallas_call(
        functools.partial(ap_kernel, n_row, n_col, inner, rows, iters),
        out_shape=(pltpu.VMEM((rows, cols), f32), pltpu.VMEM((rows, cols), f32)),
        in_specs=[VMEM] * 2,
        out_specs=(VMEM, VMEM),
        scratch_shapes=[
            pltpu.VMEM((n_row, mol, width), chunk.dtype),
            pltpu.VMEM((n_col, mol, width), chunk.dtype),
            pltpu.VMEM((rows, 128), f32),
            pltpu.VMEM((rows, cols), f32),
            pltpu.VMEM((rows, cols), f32),
            pltpu.VMEM((rows, cols), f32),
            pltpu.VMEM((rows, 128), f32),
            pltpu.VMEM((rows, 128), f32),
            pltpu.VMEM((1, cols), f32),
            pltpu.VMEM((iters, 2, rows), f32),
            pltpu.VMEM((iters, n_col, rows), f32),
            pltpu.VMEM((iters, n_col, rows), f32),
            pltpu.VMEM((iters, 1, cols), f32),
            pltpu.VMEM((iters, inner, cols), f32),
            pltpu.VMEM((iters, 1, cols), f32),
            pltpu.VMEM((iters, outer, cols), f32),
            pltpu.SemaphoreType.DMA((inner - 1,)),
            pltpu.SemaphoreType.DMA((inner, outer - 1)),
            pltpu.SemaphoreType.DMA((n_col // 2,)),
            pltpu.SemaphoreType.DMA((n_col // 2,)),
            pltpu.SemaphoreType.DMA((inner,)),
            pltpu.SemaphoreType.DMA((outer, inner)),
            pltpu.SemaphoreType.DMA((n_col,)),
            pltpu.SemaphoreType.DMA((iters, 2, n_col - 1)),
            pltpu.SemaphoreType.DMA((iters, 2, n_col)),
            pltpu.SemaphoreType.DMA((iters, inner - 1)),
            pltpu.SemaphoreType.DMA((iters, outer - 1)),
            pltpu.SemaphoreType.DMA((iters, inner)),
            pltpu.SemaphoreType.DMA((iters, outer)),
        ],
        compiler_params=pltpu.CompilerParams(
            collective_id=cid, has_side_effects=True, vmem_limit_bytes=32 * 1024 * 1024),
    )(chunk, pref_row)


def local(embedding, preference):
    rows_n = lax.axis_size("row")
    cols_n = lax.axis_size("col")
    row_idx = lax.axis_index("row")
    col_idx = lax.axis_index("col")
    mol = embedding.shape[2]
    width = embedding.shape[3]
    row_count = mol * cols_n
    col_count = mol * rows_n
    resp, avail = propagate(embedding.reshape(mol, width), preference, rows_n, cols_n, INNER, ITERS, 0)
    return (resp, avail)


def solution(mesh):
    placed = (P("col", "row", None, None), P("row"))
    return jax.shard_map(
        local,
        mesh=mesh,
        in_specs=placed,
        out_specs=(P("row", "col"), P("row", "col")),
        check_vma=False,
    )
```

```python
import functools

import jax
import jax.numpy as jnp
from jax import lax
from jax.experimental import pallas as pl
from jax.experimental.pallas import tpu as pltpu
from jax.sharding import PartitionSpec as P

ITERS = 2


DAMPING = 0.5

INNER = 8

MESH = pl.DeviceIdType.MESH
VMEM = pl.BlockSpec(memory_space=pltpu.VMEM)


def ap_kernel(n_row, n_col, inner, chunk, iters, chunk_ref, prefr_ref, resp_out, avail_out,
              colb3, rowb3, prefc, sim_s, resp_s, avail_s, fcol, scol, cq, pack, buf_f, buf_s, zpart, buf1,
              zsum, buf2, e_send_z, e_send_y, e_send_r, e_send_f, e_recv_c, e_recv_b, e_recv_r,
              send_t, recv_t, send_z, send_y, recv_z, recv_y):
    rows, cols = sim_s.shape
    r = lax.axis_index("row")
    c = lax.axis_index("col")
    outer = n_row // inner
    y = r // inner
    z = r % inner
    cpeers = [lax.rem(c + d, n_col) for d in range(1, n_col)]
    zpeers = [y * inner + lax.rem(z + d, inner) for d in range(1, inner)]
    ypeers = [lax.rem(y + d, outer) * inner + z for d in range(1, outer)]
    g = c * n_row + r
    target_row = g // n_col
    my_slot = g % n_col
    parity = c % 2
    sibling = c + 1 - 2 * parity
    targets = [(target_row, 2 * x + my_slot % 2) for x in range(n_col // 2)]
    sources = []
    for t in range(n_col // 2):
        gs = r * n_col + 2 * t + parity
        sources.append((gs % n_row, gs // n_row))

    def differs(dev):
        return jnp.logical_or(dev[0] != r, dev[1] != c)

    barrier = pltpu.get_barrier_semaphore()
    for p in cpeers:
        pl.semaphore_signal(barrier, inc=1, device_id={"col": p}, device_id_type=MESH)
    for p in zpeers + ypeers:
        pl.semaphore_signal(barrier, inc=1, device_id={"row": p}, device_id_type=MESH)
    for dev in targets + sources:
        @pl.when(differs(dev))
        def _():
            pl.semaphore_signal(barrier, inc=1, device_id=dev, device_id_type=MESH)
    self_in = jnp.logical_and(target_row == r, my_slot % 2 == parity).astype(jnp.int32)
    pl.semaphore_wait(barrier, (n_col - 1) + (inner - 1) + (outer - 1) + 2 * (n_col // 2 - self_in))

    copies = []
    pltpu.make_async_copy(chunk_ref, colb3.at[r], e_recv_c.at[z]).start()
    for i, p in enumerate(zpeers):
        cp = pltpu.make_async_remote_copy(
            src_ref=chunk_ref, dst_ref=colb3.at[r], send_sem=e_send_z.at[i],
            recv_sem=e_recv_c.at[z], device_id={"row": p}, device_id_type=MESH)
        cp.start()
        copies.append(cp)
    row_copies = []
    for j, dev in enumerate(targets):
        cp = pltpu.make_async_remote_copy(
            src_ref=chunk_ref, dst_ref=rowb3.at[my_slot], send_sem=e_send_r.at[j],
            recv_sem=e_recv_r.at[my_slot], device_id=dev, device_id_type=MESH)
        row_copies.append(cp)

        @pl.when(differs(dev))
        def _():
            cp.start()

        @pl.when(jnp.logical_not(differs(dev)))
        def _():
            pltpu.make_async_copy(chunk_ref, rowb3.at[my_slot], e_recv_r.at[my_slot]).start()

    prefc[...] = jnp.broadcast_to(prefr_ref[...].reshape(1, rows), (128, rows)).T
    for d in range(inner):
        zs = lax.rem(z + d, inner)
        slot = colb3.at[y * inner + zs]
        pltpu.make_async_copy(chunk_ref, slot, e_recv_c.at[zs]).wait()
        for i, p in enumerate(ypeers):
            cp = pltpu.make_async_remote_copy(
                src_ref=slot, dst_ref=slot, send_sem=e_send_y.at[d, i],
                recv_sem=e_recv_b.at[y, zs], device_id={"row": p}, device_id_type=MESH)
            cp.start()
            copies.append(cp)
    for t in range(n_col // 2):
        s = 2 * t + parity
        pltpu.make_async_copy(chunk_ref, rowb3.at[s], e_recv_r.at[s]).wait()
        cp = pltpu.make_async_remote_copy(
            src_ref=rowb3.at[s], dst_ref=rowb3.at[s], send_sem=e_send_f.at[t],
            recv_sem=e_recv_r.at[s], device_id={"col": sibling}, device_id_type=MESH)
        cp.start()
        copies.append(cp)
    for t in range(n_col // 2):
        s = 2 * t + 1 - parity
        pltpu.make_async_copy(chunk_ref, rowb3.at[s], e_recv_r.at[s]).wait()
    mol = chunk_ref.shape[0]
    row_start = r * rows
    col_start = c * cols
    colb_ref = colb3
    rowb_ref = rowb3


    def record_top(i0, summed):
        first = jnp.max(summed, axis=1, keepdims=True)
        hits = summed == first
        repeats = jnp.sum(hits.astype(jnp.float32), axis=1, keepdims=True)
        others = jnp.max(jnp.where(hits, -jnp.inf, summed), axis=1, keepdims=True)
        second = jnp.where(repeats > 1.0, first, others)
        fcol[pl.ds(i0, chunk), :] = jnp.broadcast_to(first, (chunk, 128))
        scol[pl.ds(i0, chunk), :] = jnp.broadcast_to(second, (chunk, 128))

    rowb_all = rowb_ref[...].reshape(rows, -1)
    xr = rowb_all.astype(jnp.float32)
    rq_s = fcol
    rq_s[...] = jnp.broadcast_to(jnp.sum(xr * xr, axis=1, keepdims=True), (rows, 128))
    blk = inner * mol
    block_firsts, block_seconds = [], []
    for d in range(outer):
        yo = lax.rem(y + d, outer)
        if d > 0:
            for s in range(inner):
                other = colb3.at[yo * inner + s]
                pltpu.make_async_copy(other, other, e_recv_b.at[yo, s]).wait()
        xb = colb_ref[pl.ds(yo * inner, inner)].reshape(blk, -1)
        xc = xb.astype(jnp.float32)
        qc = jnp.sum(xc * xc, axis=1, keepdims=True)
        cols_at = pl.ds(pl.multiple_of(yo * blk, blk), blk)
        cq[:, cols_at] = jnp.broadcast_to(qc, (blk, 128)).T[0:1, :]
        cross = lax.dot_general(
            rowb_all, xb, (((1,), (1,)), ((), ())), preferred_element_type=jnp.float32)
        sim_s[:, cols_at] = 2.0 * cross - rq_s[:, 0:1] - cq[:, cols_at]
        block_start = col_start + yo * blk

        @pl.when(jnp.logical_and(row_start < block_start + blk, block_start < row_start + rows))
        def _():
            row_ids = row_start + lax.broadcasted_iota(jnp.int32, (rows, blk), 0)
            col_ids = block_start + lax.broadcasted_iota(jnp.int32, (rows, blk), 1)
            sim_s[:, cols_at] = jnp.where(row_ids == col_ids, prefc[:, 0:1], sim_s[:, cols_at])

        summed = sim_s[:, cols_at]
        first = jnp.max(summed, axis=1, keepdims=True)
        hits = summed == first
        repeats = jnp.sum(hits.astype(jnp.float32), axis=1, keepdims=True)
        others = jnp.max(jnp.where(hits, -jnp.inf, summed), axis=1, keepdims=True)
        block_firsts.append(first)
        block_seconds.append(jnp.where(repeats > 1.0, first, others))

    first = functools.reduce(jnp.maximum, block_firsts)
    repeats = functools.reduce(jnp.add, [(f == first).astype(jnp.float32) for f in block_firsts])
    others = functools.reduce(jnp.maximum, [jnp.where(f == first, -jnp.inf, f) for f in block_firsts])
    second = jnp.where(repeats > 1.0, first, jnp.maximum(functools.reduce(jnp.maximum, block_seconds), others))
    fcol[...] = jnp.broadcast_to(first, (rows, 128))
    scol[...] = jnp.broadcast_to(second, (rows, 128))

    has_diag = row_start // cols == c
    band = pl.ds(pl.multiple_of(row_start % cols, rows), rows)

    def eye():
        return lax.broadcasted_iota(jnp.int32, (rows, rows), 0) == lax.broadcasted_iota(jnp.int32, (rows, rows), 1)
    for step in range(iters):
        first_step = step == 0
        last_step = step == iters - 1
        resp_prev, avail_prev = resp_s, avail_s
        resp_new, avail_new = (resp_out, avail_out) if last_step else (resp_s, avail_s)
        pk = pack.at[step]
        pk[0:1, :] = fcol[...].T[0:1, :]
        pk[1:2, :] = scol[...].T[0:1, :]
        for k, dst in enumerate((buf_f.at[step], buf_s.at[step])):
            src = pk.at[pl.ds(k, 1)]
            pltpu.make_async_copy(src, dst.at[pl.ds(c, 1)], recv_t.at[step, k, c]).start()
            for i, p in enumerate(cpeers):
                cp = pltpu.make_async_remote_copy(
                    src_ref=src, dst_ref=dst.at[pl.ds(c, 1)], send_sem=send_t.at[step, k, i],
                    recv_sem=recv_t.at[step, k, c], device_id={"col": p}, device_id_type=MESH)
                cp.start()
                copies.append(cp)
        for k, dst in enumerate((buf_f.at[step], buf_s.at[step])):
            for s in range(n_col):
                pltpu.make_async_copy(pk.at[pl.ds(0, 1)], dst.at[pl.ds(s, 1)], recv_t.at[step, k, s]).wait()
        firsts = buf_f[step]
        seconds = buf_s[step]
        first = jnp.max(firsts, axis=0, keepdims=True)
        at_top = firsts == first
        repeats = jnp.sum(at_top.astype(jnp.float32), axis=0, keepdims=True)
        others = jnp.max(jnp.where(at_top, -jnp.inf, firsts), axis=0, keepdims=True)
        second = jnp.where(repeats > 1.0, first, jnp.maximum(jnp.max(seconds, axis=0, keepdims=True), others))
        fcol[...] = jnp.broadcast_to(first, (128, rows)).T
        scol[...] = jnp.broadcast_to(second, (128, rows)).T

        s = sim_s[...]
        summed = s if first_step else avail_prev[...] + s
        f = fcol[:, 0:1]
        sc = scol[:, 0:1]
        fresh = s - jnp.where(summed == f, sc, f)
        if first_step:
            resp = (1.0 - DAMPING) * fresh
        else:
            resp = DAMPING * resp_prev[...] + (1.0 - DAMPING) * fresh
        resp_new[...] = resp
        zp = zpart.at[step]
        zp[...] = jnp.sum(jnp.maximum(resp, 0.0), axis=0, keepdims=True)

        @pl.when(has_diag)
        def _():
            rb_ = resp_new[:, band]
            zp[:, band] = jnp.sum(jnp.where(eye(), rb_, jnp.maximum(rb_, 0.0)), axis=0, keepdims=True)

        b1 = buf1.at[step]
        pltpu.make_async_copy(zp, b1.at[pl.ds(z, 1)], recv_z.at[step, z]).start()
        for i, p in enumerate(zpeers):
            cp = pltpu.make_async_remote_copy(
                src_ref=zp, dst_ref=b1.at[pl.ds(z, 1)], send_sem=send_z.at[step, i],
                recv_sem=recv_z.at[step, z], device_id={"row": p}, device_id_type=MESH)
            cp.start()
            copies.append(cp)
        for s in range(inner):
            pltpu.make_async_copy(zp, b1.at[pl.ds(s, 1)], recv_z.at[step, s]).wait()
        zs = zsum.at[step]
        zs[...] = jnp.sum(b1[...], axis=0, keepdims=True)
        b2 = buf2.at[step]
        pltpu.make_async_copy(zs, b2.at[pl.ds(y, 1)], recv_y.at[step, y]).start()
        for i, p in enumerate(ypeers):
            cp = pltpu.make_async_remote_copy(
                src_ref=zs, dst_ref=b2.at[pl.ds(y, 1)], send_sem=send_y.at[step, i],
                recv_sem=recv_y.at[step, y], device_id={"row": p}, device_id_type=MESH)
            cp.start()
            copies.append(cp)
        for s in range(outer):
            pltpu.make_async_copy(zs, b2.at[pl.ds(s, 1)], recv_y.at[step, s]).wait()
        colsum = jnp.sum(b2[...], axis=0, keepdims=True)

        cq[...] = colsum
        renew = jnp.minimum(colsum - jnp.maximum(resp_new[...], 0.0), 0.0)
        if first_step:
            avail_new[...] = (1.0 - DAMPING) * renew
        else:
            avail_new[...] = DAMPING * avail_prev[...] + (1.0 - DAMPING) * renew

        @pl.when(has_diag)
        def _():
            rb_ = resp_new[:, band]
            e = eye()
            positive = jnp.where(e, rb_, jnp.maximum(rb_, 0.0))
            renew_b = cq[:, band] - positive
            renew_b = jnp.where(e, renew_b, jnp.minimum(renew_b, 0.0))
            if first_step:
                avail_new[:, band] = (1.0 - DAMPING) * renew_b
            else:
                avail_new[:, band] = DAMPING * avail_prev[:, band] + (1.0 - DAMPING) * renew_b

        if not last_step:
            record_top(0, avail_new[...] + sim_s[...])
    for cp in copies:
        cp.wait_send()
    for j, dev in enumerate(targets):
        @pl.when(differs(dev))
        def _():
            row_copies[j].wait_send()


def propagate(chunk, pref_row, n_row, n_col, inner, iters, cid):
    mol, width = chunk.shape
    rows, cols = mol * n_col, mol * n_row
    outer = n_row // inner
    f32 = jnp.float32
    return pl.pallas_call(
        functools.partial(ap_kernel, n_row, n_col, inner, rows, iters),
        out_shape=(pltpu.VMEM((rows, cols), f32), pltpu.VMEM((rows, cols), f32)),
        in_specs=[VMEM] * 2,
        out_specs=(VMEM, VMEM),
        scratch_shapes=[
            pltpu.VMEM((n_row, mol, width), chunk.dtype),
            pltpu.VMEM((n_col, mol, width), chunk.dtype),
            pltpu.VMEM((rows, 128), f32),
            pltpu.VMEM((rows, cols), f32),
            pltpu.VMEM((rows, cols), f32),
            pltpu.VMEM((rows, cols), f32),
            pltpu.VMEM((rows, 128), f32),
            pltpu.VMEM((rows, 128), f32),
            pltpu.VMEM((1, cols), f32),
            pltpu.VMEM((iters, 2, rows), f32),
            pltpu.VMEM((iters, n_col, rows), f32),
            pltpu.VMEM((iters, n_col, rows), f32),
            pltpu.VMEM((iters, 1, cols), f32),
            pltpu.VMEM((iters, inner, cols), f32),
            pltpu.VMEM((iters, 1, cols), f32),
            pltpu.VMEM((iters, outer, cols), f32),
            pltpu.SemaphoreType.DMA((inner - 1,)),
            pltpu.SemaphoreType.DMA((inner, outer - 1)),
            pltpu.SemaphoreType.DMA((n_col // 2,)),
            pltpu.SemaphoreType.DMA((n_col // 2,)),
            pltpu.SemaphoreType.DMA((inner,)),
            pltpu.SemaphoreType.DMA((outer, inner)),
            pltpu.SemaphoreType.DMA((n_col,)),
            pltpu.SemaphoreType.DMA((iters, 2, n_col - 1)),
            pltpu.SemaphoreType.DMA((iters, 2, n_col)),
            pltpu.SemaphoreType.DMA((iters, inner - 1)),
            pltpu.SemaphoreType.DMA((iters, outer - 1)),
            pltpu.SemaphoreType.DMA((iters, inner)),
            pltpu.SemaphoreType.DMA((iters, outer)),
        ],
        compiler_params=pltpu.CompilerParams(
            collective_id=cid, has_side_effects=True, vmem_limit_bytes=32 * 1024 * 1024),
    )(chunk, pref_row)


def local(embedding, preference):
    rows_n = lax.axis_size("row")
    cols_n = lax.axis_size("col")
    row_idx = lax.axis_index("row")
    col_idx = lax.axis_index("col")
    mol = embedding.shape[2]
    width = embedding.shape[3]
    row_count = mol * cols_n
    col_count = mol * rows_n
    resp, avail = propagate(embedding.reshape(mol, width), preference, rows_n, cols_n, INNER, ITERS, 0)
    return (resp, avail)


def solution(mesh):
    placed = (P("col", "row", None, None), P("row"))
    return jax.shard_map(
        local,
        mesh=mesh,
        in_specs=placed,
        out_specs=(P("row", "col"), P("row", "col")),
        check_vma=False,
    )
```

```python
import functools

import jax
import jax.numpy as jnp
from jax import lax
from jax.experimental import pallas as pl
from jax.experimental.pallas import tpu as pltpu
from jax.sharding import PartitionSpec as P

ITERS = 2


DAMPING = 0.5

INNER = 8

MESH = pl.DeviceIdType.MESH
VMEM = pl.BlockSpec(memory_space=pltpu.VMEM)


def ap_kernel(n_row, n_col, inner, chunk, iters, chunk_ref, prefr_ref, resp_out, avail_out,
              colb3, rowb3, prefc, sim_s, resp_s, avail_s, fcol, scol, cq, pack, buf_f, buf_s, zpart, buf1,
              zsum, buf2, e_send_z, e_send_y, e_send_r, e_send_f, e_recv_c, e_recv_b, e_recv_r,
              send_t, recv_t, send_z, send_y, recv_z, recv_y):
    rows, cols = sim_s.shape
    r = lax.axis_index("row")
    c = lax.axis_index("col")
    outer = n_row // inner
    y = r // inner
    z = r % inner
    cpeers = [lax.rem(c + d, n_col) for d in range(1, n_col)]
    zpeers = [y * inner + lax.rem(z + d, inner) for d in range(1, inner)]
    ypeers = [lax.rem(y + d, outer) * inner + z for d in range(1, outer)]
    g = c * n_row + r
    target_row = g // n_col
    my_slot = g % n_col
    parity = c % 2
    sibling = c + 1 - 2 * parity
    targets = [(target_row, 2 * x + my_slot % 2) for x in range(n_col // 2)]
    sources = []
    for t in range(n_col // 2):
        gs = r * n_col + 2 * t + parity
        sources.append((gs % n_row, gs // n_row))

    def differs(dev):
        return jnp.logical_or(dev[0] != r, dev[1] != c)

    barrier = pltpu.get_barrier_semaphore()
    for p in cpeers:
        pl.semaphore_signal(barrier, inc=1, device_id={"col": p}, device_id_type=MESH)
    for p in zpeers + ypeers:
        pl.semaphore_signal(barrier, inc=1, device_id={"row": p}, device_id_type=MESH)
    for dev in targets + sources:
        @pl.when(differs(dev))
        def _():
            pl.semaphore_signal(barrier, inc=1, device_id=dev, device_id_type=MESH)
    self_in = jnp.logical_and(target_row == r, my_slot % 2 == parity).astype(jnp.int32)
    pl.semaphore_wait(barrier, (n_col - 1) + (inner - 1) + (outer - 1) + 2 * (n_col // 2 - self_in))

    copies = []
    pltpu.make_async_copy(chunk_ref, colb3.at[r], e_recv_c.at[z]).start()
    for i, p in enumerate(zpeers):
        cp = pltpu.make_async_remote_copy(
            src_ref=chunk_ref, dst_ref=colb3.at[r], send_sem=e_send_z.at[i],
            recv_sem=e_recv_c.at[z], device_id={"row": p}, device_id_type=MESH)
        cp.start()
        copies.append(cp)
    row_copies = []
    for j, dev in enumerate(targets):
        cp = pltpu.make_async_remote_copy(
            src_ref=chunk_ref, dst_ref=rowb3.at[my_slot], send_sem=e_send_r.at[j],
            recv_sem=e_recv_r.at[my_slot], device_id=dev, device_id_type=MESH)
        row_copies.append(cp)

        @pl.when(differs(dev))
        def _():
            cp.start()

        @pl.when(jnp.logical_not(differs(dev)))
        def _():
            pltpu.make_async_copy(chunk_ref, rowb3.at[my_slot], e_recv_r.at[my_slot]).start()

    prefc[...] = jnp.broadcast_to(prefr_ref[...].reshape(1, rows), (128, rows)).T
    for d in range(inner):
        zs = lax.rem(z + d, inner)
        slot = colb3.at[y * inner + zs]
        pltpu.make_async_copy(chunk_ref, slot, e_recv_c.at[zs]).wait()
        for i, p in enumerate(ypeers):
            cp = pltpu.make_async_remote_copy(
                src_ref=slot, dst_ref=slot, send_sem=e_send_y.at[d, i],
                recv_sem=e_recv_b.at[y, zs], device_id={"row": p}, device_id_type=MESH)
            cp.start()
            copies.append(cp)
    for t in range(n_col // 2):
        s = 2 * t + parity
        pltpu.make_async_copy(chunk_ref, rowb3.at[s], e_recv_r.at[s]).wait()
        cp = pltpu.make_async_remote_copy(
            src_ref=rowb3.at[s], dst_ref=rowb3.at[s], send_sem=e_send_f.at[t],
            recv_sem=e_recv_r.at[s], device_id={"col": sibling}, device_id_type=MESH)
        cp.start()
        copies.append(cp)
    for t in range(n_col // 2):
        s = 2 * t + 1 - parity
        pltpu.make_async_copy(chunk_ref, rowb3.at[s], e_recv_r.at[s]).wait()
    mol = chunk_ref.shape[0]
    row_start = r * rows
    col_start = c * cols
    colb_ref = colb3
    rowb_ref = rowb3


    def record_top(i0, summed):
        first = jnp.max(summed, axis=1, keepdims=True)
        hits = summed == first
        repeats = jnp.sum(hits.astype(jnp.float32), axis=1, keepdims=True)
        others = jnp.max(jnp.where(hits, -jnp.inf, summed), axis=1, keepdims=True)
        second = jnp.where(repeats > 1.0, first, others)
        fcol[pl.ds(i0, chunk), :] = jnp.broadcast_to(first, (chunk, 128))
        scol[pl.ds(i0, chunk), :] = jnp.broadcast_to(second, (chunk, 128))

    rowb_all = rowb_ref[...].reshape(rows, -1)
    xr = rowb_all.astype(jnp.float32)
    rq_s = fcol
    rq_s[...] = jnp.broadcast_to(jnp.sum(xr * xr, axis=1, keepdims=True), (rows, 128))
    blk = inner * mol
    block_firsts, block_seconds = [], []
    for d in range(outer):
        yo = lax.rem(y + d, outer)
        if d > 0:
            for s in range(inner):
                other = colb3.at[yo * inner + s]
                pltpu.make_async_copy(other, other, e_recv_b.at[yo, s]).wait()
        xb = colb_ref[pl.ds(yo * inner, inner)].reshape(blk, -1)
        xc = xb.astype(jnp.float32)
        qc = jnp.sum(xc * xc, axis=1, keepdims=True)
        cols_at = pl.ds(pl.multiple_of(yo * blk, blk), blk)
        cq[:, cols_at] = jnp.broadcast_to(qc, (blk, 128)).T[0:1, :]
        cross = lax.dot_general(
            rowb_all, xb, (((1,), (1,)), ((), ())), preferred_element_type=jnp.float32)
        sim_s[:, cols_at] = 2.0 * cross - rq_s[:, 0:1] - cq[:, cols_at]
        block_start = col_start + yo * blk

        @pl.when(jnp.logical_and(row_start < block_start + blk, block_start < row_start + rows))
        def _():
            row_ids = row_start + lax.broadcasted_iota(jnp.int32, (rows, blk), 0)
            col_ids = block_start + lax.broadcasted_iota(jnp.int32, (rows, blk), 1)
            sim_s[:, cols_at] = jnp.where(row_ids == col_ids, prefc[:, 0:1], sim_s[:, cols_at])

        summed = sim_s[:, cols_at]
        first = jnp.max(summed, axis=1, keepdims=True)
        hits = summed == first
        repeats = jnp.sum(hits.astype(jnp.float32), axis=1, keepdims=True)
        others = jnp.max(jnp.where(hits, -jnp.inf, summed), axis=1, keepdims=True)
        block_firsts.append(first)
        block_seconds.append(jnp.where(repeats > 1.0, first, others))

    first = functools.reduce(jnp.maximum, block_firsts)
    repeats = functools.reduce(jnp.add, [(f == first).astype(jnp.float32) for f in block_firsts])
    others = functools.reduce(jnp.maximum, [jnp.where(f == first, -jnp.inf, f) for f in block_firsts])
    second = jnp.where(repeats > 1.0, first, jnp.maximum(functools.reduce(jnp.maximum, block_seconds), others))
    fcol[...] = jnp.broadcast_to(first, (rows, 128))
    scol[...] = jnp.broadcast_to(second, (rows, 128))

    has_diag = row_start // cols == c
    band = pl.ds(pl.multiple_of(row_start % cols, rows), rows)

    def eye():
        return lax.broadcasted_iota(jnp.int32, (rows, rows), 0) == lax.broadcasted_iota(jnp.int32, (rows, rows), 1)
    for step in range(iters):
        first_step = step == 0
        last_step = step == iters - 1
        resp_prev, avail_prev = resp_s, avail_s
        resp_new, avail_new = (resp_out, avail_out) if last_step else (resp_s, avail_s)
        pk = pack.at[step]
        pk[0:1, :] = fcol[...].T[0:1, :]
        pk[1:2, :] = scol[...].T[0:1, :]
        for k, dst in enumerate((buf_f.at[step], buf_s.at[step])):
            src = pk.at[pl.ds(k, 1)]
            pltpu.make_async_copy(src, dst.at[pl.ds(c, 1)], recv_t.at[step, k, c]).start()
            for i, p in enumerate(cpeers):
                cp = pltpu.make_async_remote_copy(
                    src_ref=src, dst_ref=dst.at[pl.ds(c, 1)], send_sem=send_t.at[step, k, i],
                    recv_sem=recv_t.at[step, k, c], device_id={"col": p}, device_id_type=MESH)
                cp.start()
                copies.append(cp)
        for k, dst in enumerate((buf_f.at[step], buf_s.at[step])):
            for s in range(n_col):
                pltpu.make_async_copy(pk.at[pl.ds(0, 1)], dst.at[pl.ds(s, 1)], recv_t.at[step, k, s]).wait()
        firsts = buf_f[step]
        seconds = buf_s[step]
        first = jnp.max(firsts, axis=0, keepdims=True)
        at_top = firsts == first
        repeats = jnp.sum(at_top.astype(jnp.float32), axis=0, keepdims=True)
        others = jnp.max(jnp.where(at_top, -jnp.inf, firsts), axis=0, keepdims=True)
        second = jnp.where(repeats > 1.0, first, jnp.maximum(jnp.max(seconds, axis=0, keepdims=True), others))
        fcol[...] = jnp.broadcast_to(first, (128, rows)).T
        scol[...] = jnp.broadcast_to(second, (128, rows)).T

        zp = zpart.at[step]
        b1 = buf1.at[step]
        half = cols // 2
        for h in range(2):
            hc = pl.ds(h * half, half)
            s = sim_s[:, hc]
            summed = s if first_step else avail_prev[:, hc] + s
            f = fcol[:, 0:1]
            sc = scol[:, 0:1]
            fresh = s - jnp.where(summed == f, sc, f)
            if first_step:
                resp = (1.0 - DAMPING) * fresh
            else:
                resp = DAMPING * resp_prev[:, hc] + (1.0 - DAMPING) * fresh
            resp_new[:, hc] = resp
            zp[:, hc] = jnp.sum(jnp.maximum(resp, 0.0), axis=0, keepdims=True)
            h_start = col_start + h * half

            @pl.when(jnp.logical_and(row_start < h_start + half, h_start < row_start + rows))
            def _():
                row_ids = row_start + lax.broadcasted_iota(jnp.int32, (rows, half), 0)
                col_ids = h_start + lax.broadcasted_iota(jnp.int32, (rows, half), 1)
                rh = resp_new[:, hc]
                zp[:, hc] = jnp.sum(jnp.where(row_ids == col_ids, rh, jnp.maximum(rh, 0.0)), axis=0, keepdims=True)

            src_h = zp.at[:, hc]
            dst_h = b1.at[pl.ds(z, 1), hc]
            pltpu.make_async_copy(src_h, dst_h, recv_z.at[step, h, z]).start()
            for i, p in enumerate(zpeers):
                cp = pltpu.make_async_remote_copy(
                    src_ref=src_h, dst_ref=dst_h, send_sem=send_z.at[step, h, i],
                    recv_sem=recv_z.at[step, h, z], device_id={"row": p}, device_id_type=MESH)
                cp.start()
                copies.append(cp)
        for h in range(2):
            hc = pl.ds(h * half, half)
            for s in range(inner):
                pltpu.make_async_copy(zp.at[:, hc], b1.at[pl.ds(s, 1), hc], recv_z.at[step, h, s]).wait()
        zs = zsum.at[step]
        zs[...] = jnp.sum(b1[...], axis=0, keepdims=True)
        b2 = buf2.at[step]
        pltpu.make_async_copy(zs, b2.at[pl.ds(y, 1)], recv_y.at[step, y]).start()
        for i, p in enumerate(ypeers):
            cp = pltpu.make_async_remote_copy(
                src_ref=zs, dst_ref=b2.at[pl.ds(y, 1)], send_sem=send_y.at[step, i],
                recv_sem=recv_y.at[step, y], device_id={"row": p}, device_id_type=MESH)
            cp.start()
            copies.append(cp)
        for s in range(outer):
            pltpu.make_async_copy(zs, b2.at[pl.ds(s, 1)], recv_y.at[step, s]).wait()
        colsum = jnp.sum(b2[...], axis=0, keepdims=True)

        cq[...] = colsum
        renew = jnp.minimum(colsum - jnp.maximum(resp_new[...], 0.0), 0.0)
        if first_step:
            avail_new[...] = (1.0 - DAMPING) * renew
        else:
            avail_new[...] = DAMPING * avail_prev[...] + (1.0 - DAMPING) * renew

        @pl.when(has_diag)
        def _():
            rb_ = resp_new[:, band]
            e = eye()
            positive = jnp.where(e, rb_, jnp.maximum(rb_, 0.0))
            renew_b = cq[:, band] - positive
            renew_b = jnp.where(e, renew_b, jnp.minimum(renew_b, 0.0))
            if first_step:
                avail_new[:, band] = (1.0 - DAMPING) * renew_b
            else:
                avail_new[:, band] = DAMPING * avail_prev[:, band] + (1.0 - DAMPING) * renew_b

        if not last_step:
            record_top(0, avail_new[...] + sim_s[...])
    for cp in copies:
        cp.wait_send()
    for j, dev in enumerate(targets):
        @pl.when(differs(dev))
        def _():
            row_copies[j].wait_send()


def propagate(chunk, pref_row, n_row, n_col, inner, iters, cid):
    mol, width = chunk.shape
    rows, cols = mol * n_col, mol * n_row
    outer = n_row // inner
    f32 = jnp.float32
    return pl.pallas_call(
        functools.partial(ap_kernel, n_row, n_col, inner, rows, iters),
        out_shape=(pltpu.VMEM((rows, cols), f32), pltpu.VMEM((rows, cols), f32)),
        in_specs=[VMEM] * 2,
        out_specs=(VMEM, VMEM),
        scratch_shapes=[
            pltpu.VMEM((n_row, mol, width), chunk.dtype),
            pltpu.VMEM((n_col, mol, width), chunk.dtype),
            pltpu.VMEM((rows, 128), f32),
            pltpu.VMEM((rows, cols), f32),
            pltpu.VMEM((rows, cols), f32),
            pltpu.VMEM((rows, cols), f32),
            pltpu.VMEM((rows, 128), f32),
            pltpu.VMEM((rows, 128), f32),
            pltpu.VMEM((1, cols), f32),
            pltpu.VMEM((iters, 2, rows), f32),
            pltpu.VMEM((iters, n_col, rows), f32),
            pltpu.VMEM((iters, n_col, rows), f32),
            pltpu.VMEM((iters, 1, cols), f32),
            pltpu.VMEM((iters, inner, cols), f32),
            pltpu.VMEM((iters, 1, cols), f32),
            pltpu.VMEM((iters, outer, cols), f32),
            pltpu.SemaphoreType.DMA((inner - 1,)),
            pltpu.SemaphoreType.DMA((inner, outer - 1)),
            pltpu.SemaphoreType.DMA((n_col // 2,)),
            pltpu.SemaphoreType.DMA((n_col // 2,)),
            pltpu.SemaphoreType.DMA((inner,)),
            pltpu.SemaphoreType.DMA((outer, inner)),
            pltpu.SemaphoreType.DMA((n_col,)),
            pltpu.SemaphoreType.DMA((iters, 2, n_col - 1)),
            pltpu.SemaphoreType.DMA((iters, 2, n_col)),
            pltpu.SemaphoreType.DMA((iters, 2, inner - 1)),
            pltpu.SemaphoreType.DMA((iters, outer - 1)),
            pltpu.SemaphoreType.DMA((iters, 2, inner)),
            pltpu.SemaphoreType.DMA((iters, outer)),
        ],
        compiler_params=pltpu.CompilerParams(
            collective_id=cid, has_side_effects=True, vmem_limit_bytes=32 * 1024 * 1024),
    )(chunk, pref_row)


def local(embedding, preference):
    rows_n = lax.axis_size("row")
    cols_n = lax.axis_size("col")
    row_idx = lax.axis_index("row")
    col_idx = lax.axis_index("col")
    mol = embedding.shape[2]
    width = embedding.shape[3]
    row_count = mol * cols_n
    col_count = mol * rows_n
    resp, avail = propagate(embedding.reshape(mol, width), preference, rows_n, cols_n, INNER, ITERS, 0)
    return (resp, avail)


def solution(mesh):
    placed = (P("col", "row", None, None), P("row"))
    return jax.shard_map(
        local,
        mesh=mesh,
        in_specs=placed,
        out_specs=(P("row", "col"), P("row", "col")),
        check_vma=False,
    )
```

```python
import functools

import jax
import jax.numpy as jnp
from jax import lax
from jax.experimental import pallas as pl
from jax.experimental.pallas import tpu as pltpu
from jax.sharding import PartitionSpec as P

ITERS = 2


DAMPING = 0.5

INNER = 8

MESH = pl.DeviceIdType.MESH
VMEM = pl.BlockSpec(memory_space=pltpu.VMEM)


def ap_kernel(n_row, n_col, inner, chunk, iters, chunk_ref, prefr_ref, resp_out, avail_out,
              colb3, rowb3, prefc, sim_s, resp_s, avail_s, fcol, scol, cq, pack, buf_f, buf_s, zpart, buf1,
              zsum, buf2, e_send_z, e_send_y, e_send_r, e_send_f, e_recv_c, e_recv_b, e_recv_r,
              send_t, recv_t, send_z, send_y, recv_z, recv_y):
    rows, cols = sim_s.shape
    r = lax.axis_index("row")
    c = lax.axis_index("col")
    outer = n_row // inner
    y = r // inner
    z = r % inner
    cpeers = [lax.rem(c + d, n_col) for d in range(1, n_col)]
    zpeers = [y * inner + lax.rem(z + d, inner) for d in range(1, inner)]
    ypeers = [lax.rem(y + d, outer) * inner + z for d in range(1, outer)]
    g = c * n_row + r
    target_row = g // n_col
    my_slot = g % n_col
    parity = c % 2
    sibling = c + 1 - 2 * parity
    targets = [(target_row, 2 * x + my_slot % 2) for x in range(n_col // 2)]
    sources = []
    for t in range(n_col // 2):
        gs = r * n_col + 2 * t + parity
        sources.append((gs % n_row, gs // n_row))

    def differs(dev):
        return jnp.logical_or(dev[0] != r, dev[1] != c)

    barrier = pltpu.get_barrier_semaphore()
    for p in cpeers:
        pl.semaphore_signal(barrier, inc=1, device_id={"col": p}, device_id_type=MESH)
    for p in zpeers + ypeers:
        pl.semaphore_signal(barrier, inc=1, device_id={"row": p}, device_id_type=MESH)
    for dev in targets + sources:
        @pl.when(differs(dev))
        def _():
            pl.semaphore_signal(barrier, inc=1, device_id=dev, device_id_type=MESH)
    self_in = jnp.logical_and(target_row == r, my_slot % 2 == parity).astype(jnp.int32)
    pl.semaphore_wait(barrier, (n_col - 1) + (inner - 1) + (outer - 1) + 2 * (n_col // 2 - self_in))

    copies = []
    pltpu.make_async_copy(chunk_ref, colb3.at[r], e_recv_c.at[z]).start()
    for i, p in enumerate(zpeers):
        cp = pltpu.make_async_remote_copy(
            src_ref=chunk_ref, dst_ref=colb3.at[r], send_sem=e_send_z.at[i],
            recv_sem=e_recv_c.at[z], device_id={"row": p}, device_id_type=MESH)
        cp.start()
        copies.append(cp)
    row_copies = []
    for j, dev in enumerate(targets):
        cp = pltpu.make_async_remote_copy(
            src_ref=chunk_ref, dst_ref=rowb3.at[my_slot], send_sem=e_send_r.at[j],
            recv_sem=e_recv_r.at[my_slot], device_id=dev, device_id_type=MESH)
        row_copies.append(cp)

        @pl.when(differs(dev))
        def _():
            cp.start()

        @pl.when(jnp.logical_not(differs(dev)))
        def _():
            pltpu.make_async_copy(chunk_ref, rowb3.at[my_slot], e_recv_r.at[my_slot]).start()

    prefc[...] = jnp.broadcast_to(prefr_ref[...].reshape(1, rows), (128, rows)).T
    for d in range(inner):
        zs = lax.rem(z + d, inner)
        slot = colb3.at[y * inner + zs]
        pltpu.make_async_copy(chunk_ref, slot, e_recv_c.at[zs]).wait()
        for i, p in enumerate(ypeers):
            cp = pltpu.make_async_remote_copy(
                src_ref=slot, dst_ref=slot, send_sem=e_send_y.at[d, i],
                recv_sem=e_recv_b.at[y, zs], device_id={"row": p}, device_id_type=MESH)
            cp.start()
            copies.append(cp)
    for t in range(n_col // 2):
        s = 2 * t + parity
        pltpu.make_async_copy(chunk_ref, rowb3.at[s], e_recv_r.at[s]).wait()
        cp = pltpu.make_async_remote_copy(
            src_ref=rowb3.at[s], dst_ref=rowb3.at[s], send_sem=e_send_f.at[t],
            recv_sem=e_recv_r.at[s], device_id={"col": sibling}, device_id_type=MESH)
        cp.start()
        copies.append(cp)
    for t in range(n_col // 2):
        s = 2 * t + 1 - parity
        pltpu.make_async_copy(chunk_ref, rowb3.at[s], e_recv_r.at[s]).wait()
    mol = chunk_ref.shape[0]
    row_start = r * rows
    col_start = c * cols
    colb_ref = colb3
    rowb_ref = rowb3


    def record_top(i0, summed):
        first = jnp.max(summed, axis=1, keepdims=True)
        hits = summed == first
        repeats = jnp.sum(hits.astype(jnp.float32), axis=1, keepdims=True)
        others = jnp.max(jnp.where(hits, -jnp.inf, summed), axis=1, keepdims=True)
        second = jnp.where(repeats > 1.0, first, others)
        fcol[pl.ds(i0, chunk), :] = jnp.broadcast_to(first, (chunk, 128))
        scol[pl.ds(i0, chunk), :] = jnp.broadcast_to(second, (chunk, 128))

    rowb_all = rowb_ref[...].reshape(rows, -1)
    xr = rowb_all.astype(jnp.float32)
    rq_s = fcol
    rq_s[...] = jnp.broadcast_to(jnp.sum(xr * xr, axis=1, keepdims=True), (rows, 128))
    blk = inner * mol
    block_firsts, block_seconds = [], []
    for d in range(outer):
        yo = lax.rem(y + d, outer)
        if d > 0:
            for s in range(inner):
                other = colb3.at[yo * inner + s]
                pltpu.make_async_copy(other, other, e_recv_b.at[yo, s]).wait()
        xb = colb_ref[pl.ds(yo * inner, inner)].reshape(blk, -1)
        xc = xb.astype(jnp.float32)
        qc = jnp.sum(xc * xc, axis=1, keepdims=True)
        cols_at = pl.ds(pl.multiple_of(yo * blk, blk), blk)
        cq[:, cols_at] = jnp.broadcast_to(qc, (blk, 128)).T[0:1, :]
        cross = lax.dot_general(
            rowb_all, xb, (((1,), (1,)), ((), ())), preferred_element_type=jnp.float32)
        sim_s[:, cols_at] = 2.0 * cross - rq_s[:, 0:1] - cq[:, cols_at]
        block_start = col_start + yo * blk

        @pl.when(jnp.logical_and(row_start < block_start + blk, block_start < row_start + rows))
        def _():
            row_ids = row_start + lax.broadcasted_iota(jnp.int32, (rows, blk), 0)
            col_ids = block_start + lax.broadcasted_iota(jnp.int32, (rows, blk), 1)
            sim_s[:, cols_at] = jnp.where(row_ids == col_ids, prefc[:, 0:1], sim_s[:, cols_at])

        summed = sim_s[:, cols_at]
        first = jnp.max(summed, axis=1, keepdims=True)
        hits = summed == first
        repeats = jnp.sum(hits.astype(jnp.float32), axis=1, keepdims=True)
        others = jnp.max(jnp.where(hits, -jnp.inf, summed), axis=1, keepdims=True)
        block_firsts.append(first)
        block_seconds.append(jnp.where(repeats > 1.0, first, others))

    first = functools.reduce(jnp.maximum, block_firsts)
    repeats = functools.reduce(jnp.add, [(f == first).astype(jnp.float32) for f in block_firsts])
    others = functools.reduce(jnp.maximum, [jnp.where(f == first, -jnp.inf, f) for f in block_firsts])
    second = jnp.where(repeats > 1.0, first, jnp.maximum(functools.reduce(jnp.maximum, block_seconds), others))
    fcol[...] = jnp.broadcast_to(first, (rows, 128))
    scol[...] = jnp.broadcast_to(second, (rows, 128))

    has_diag = row_start // cols == c
    band = pl.ds(pl.multiple_of(row_start % cols, rows), rows)

    def eye():
        return lax.broadcasted_iota(jnp.int32, (rows, rows), 0) == lax.broadcasted_iota(jnp.int32, (rows, rows), 1)
    for step in range(iters):
        first_step = step == 0
        last_step = step == iters - 1
        resp_prev, avail_prev = resp_s, avail_s
        resp_new, avail_new = (resp_out, avail_out) if last_step else (resp_s, avail_s)
        pk = pack.at[step]
        pk[0:1, :] = fcol[...].T[0:1, :]
        pk[1:2, :] = scol[...].T[0:1, :]
        for k, dst in enumerate((buf_f.at[step], buf_s.at[step])):
            src = pk.at[pl.ds(k, 1)]
            pltpu.make_async_copy(src, dst.at[pl.ds(c, 1)], recv_t.at[step, k, c]).start()
            for i, p in enumerate(cpeers):
                cp = pltpu.make_async_remote_copy(
                    src_ref=src, dst_ref=dst.at[pl.ds(c, 1)], send_sem=send_t.at[step, k, i],
                    recv_sem=recv_t.at[step, k, c], device_id={"col": p}, device_id_type=MESH)
                cp.start()
                copies.append(cp)
        for k, dst in enumerate((buf_f.at[step], buf_s.at[step])):
            for s in range(n_col):
                pltpu.make_async_copy(pk.at[pl.ds(0, 1)], dst.at[pl.ds(s, 1)], recv_t.at[step, k, s]).wait()
        firsts = buf_f[step]
        seconds = buf_s[step]
        first = jnp.max(firsts, axis=0, keepdims=True)
        at_top = firsts == first
        repeats = jnp.sum(at_top.astype(jnp.float32), axis=0, keepdims=True)
        others = jnp.max(jnp.where(at_top, -jnp.inf, firsts), axis=0, keepdims=True)
        second = jnp.where(repeats > 1.0, first, jnp.maximum(jnp.max(seconds, axis=0, keepdims=True), others))
        fcol[...] = jnp.broadcast_to(first, (128, rows)).T
        scol[...] = jnp.broadcast_to(second, (128, rows)).T

        s = sim_s[...]
        summed = s if first_step else avail_prev[...] + s
        f = fcol[:, 0:1]
        sc = scol[:, 0:1]
        fresh = s - jnp.where(summed == f, sc, f)
        if first_step:
            resp = (1.0 - DAMPING) * fresh
        else:
            resp = DAMPING * resp_prev[...] + (1.0 - DAMPING) * fresh
        resp_new[...] = resp
        zp = zpart.at[step]
        zp[...] = jnp.sum(jnp.maximum(resp, 0.0), axis=0, keepdims=True)

        @pl.when(has_diag)
        def _():
            rb_ = resp_new[:, band]
            zp[:, band] = jnp.sum(jnp.where(eye(), rb_, jnp.maximum(rb_, 0.0)), axis=0, keepdims=True)

        b1 = buf1.at[step]
        pltpu.make_async_copy(zp, b1.at[pl.ds(z, 1)], recv_z.at[step, z]).start()
        for i, p in enumerate(zpeers):
            cp = pltpu.make_async_remote_copy(
                src_ref=zp, dst_ref=b1.at[pl.ds(z, 1)], send_sem=send_z.at[step, i],
                recv_sem=recv_z.at[step, z], device_id={"row": p}, device_id_type=MESH)
            cp.start()
            copies.append(cp)
        for s in range(inner):
            pltpu.make_async_copy(zp, b1.at[pl.ds(s, 1)], recv_z.at[step, s]).wait()
        zs = zsum.at[step]
        zs[...] = jnp.sum(b1[...], axis=0, keepdims=True)
        b2 = buf2.at[step]
        pltpu.make_async_copy(zs, b2.at[pl.ds(y, 1)], recv_y.at[step, y]).start()
        for i, p in enumerate(ypeers):
            cp = pltpu.make_async_remote_copy(
                src_ref=zs, dst_ref=b2.at[pl.ds(y, 1)], send_sem=send_y.at[step, i],
                recv_sem=recv_y.at[step, y], device_id={"row": p}, device_id_type=MESH)
            cp.start()
            copies.append(cp)
        for s in range(outer):
            pltpu.make_async_copy(zs, b2.at[pl.ds(s, 1)], recv_y.at[step, s]).wait()
        colsum = jnp.sum(b2[...], axis=0, keepdims=True)

        cq[...] = colsum
        if not last_step:
            b_firsts, b_seconds = [], []
            for b in range(cols // blk):
                bc = pl.ds(b * blk, blk)
                rb_ = resp_new[:, bc]
                renew = jnp.minimum(cq[:, bc] - jnp.maximum(rb_, 0.0), 0.0)
                if first_step:
                    avail_new[:, bc] = (1.0 - DAMPING) * renew
                else:
                    avail_new[:, bc] = DAMPING * avail_prev[:, bc] + (1.0 - DAMPING) * renew
                b_start = col_start + b * blk

                @pl.when(jnp.logical_and(row_start < b_start + blk, b_start < row_start + rows))
                def _():
                    row_ids = row_start + lax.broadcasted_iota(jnp.int32, (rows, blk), 0)
                    col_ids = b_start + lax.broadcasted_iota(jnp.int32, (rows, blk), 1)
                    diag = row_ids == col_ids
                    rd = resp_new[:, bc]
                    renew_b = cq[:, bc] - jnp.where(diag, rd, jnp.maximum(rd, 0.0))
                    renew_b = jnp.where(diag, renew_b, jnp.minimum(renew_b, 0.0))
                    if first_step:
                        avail_new[:, bc] = (1.0 - DAMPING) * renew_b
                    else:
                        avail_new[:, bc] = DAMPING * avail_prev[:, bc] + (1.0 - DAMPING) * renew_b

                summed = avail_new[:, bc] + sim_s[:, bc]
                bf = jnp.max(summed, axis=1, keepdims=True)
                hits = summed == bf
                reps = jnp.sum(hits.astype(jnp.float32), axis=1, keepdims=True)
                oth = jnp.max(jnp.where(hits, -jnp.inf, summed), axis=1, keepdims=True)
                b_firsts.append(bf)
                b_seconds.append(jnp.where(reps > 1.0, bf, oth))
            fm = functools.reduce(jnp.maximum, b_firsts)
            reps = functools.reduce(jnp.add, [(v == fm).astype(jnp.float32) for v in b_firsts])
            oth = functools.reduce(jnp.maximum, [jnp.where(v == fm, -jnp.inf, v) for v in b_firsts])
            sm = jnp.where(reps > 1.0, fm, jnp.maximum(functools.reduce(jnp.maximum, b_seconds), oth))
            fcol[...] = jnp.broadcast_to(fm, (rows, 128))
            scol[...] = jnp.broadcast_to(sm, (rows, 128))
            continue
        renew = jnp.minimum(colsum - jnp.maximum(resp_new[...], 0.0), 0.0)
        if first_step:
            avail_new[...] = (1.0 - DAMPING) * renew
        else:
            avail_new[...] = DAMPING * avail_prev[...] + (1.0 - DAMPING) * renew

        @pl.when(has_diag)
        def _():
            rb_ = resp_new[:, band]
            e = eye()
            positive = jnp.where(e, rb_, jnp.maximum(rb_, 0.0))
            renew_b = cq[:, band] - positive
            renew_b = jnp.where(e, renew_b, jnp.minimum(renew_b, 0.0))
            if first_step:
                avail_new[:, band] = (1.0 - DAMPING) * renew_b
            else:
                avail_new[:, band] = DAMPING * avail_prev[:, band] + (1.0 - DAMPING) * renew_b

        if not last_step:
            record_top(0, avail_new[...] + sim_s[...])
    for cp in copies:
        cp.wait_send()
    for j, dev in enumerate(targets):
        @pl.when(differs(dev))
        def _():
            row_copies[j].wait_send()


def propagate(chunk, pref_row, n_row, n_col, inner, iters, cid):
    mol, width = chunk.shape
    rows, cols = mol * n_col, mol * n_row
    outer = n_row // inner
    f32 = jnp.float32
    return pl.pallas_call(
        functools.partial(ap_kernel, n_row, n_col, inner, rows, iters),
        out_shape=(pltpu.VMEM((rows, cols), f32), pltpu.VMEM((rows, cols), f32)),
        in_specs=[VMEM] * 2,
        out_specs=(VMEM, VMEM),
        scratch_shapes=[
            pltpu.VMEM((n_row, mol, width), chunk.dtype),
            pltpu.VMEM((n_col, mol, width), chunk.dtype),
            pltpu.VMEM((rows, 128), f32),
            pltpu.VMEM((rows, cols), f32),
            pltpu.VMEM((rows, cols), f32),
            pltpu.VMEM((rows, cols), f32),
            pltpu.VMEM((rows, 128), f32),
            pltpu.VMEM((rows, 128), f32),
            pltpu.VMEM((1, cols), f32),
            pltpu.VMEM((iters, 2, rows), f32),
            pltpu.VMEM((iters, n_col, rows), f32),
            pltpu.VMEM((iters, n_col, rows), f32),
            pltpu.VMEM((iters, 1, cols), f32),
            pltpu.VMEM((iters, inner, cols), f32),
            pltpu.VMEM((iters, 1, cols), f32),
            pltpu.VMEM((iters, outer, cols), f32),
            pltpu.SemaphoreType.DMA((inner - 1,)),
            pltpu.SemaphoreType.DMA((inner, outer - 1)),
            pltpu.SemaphoreType.DMA((n_col // 2,)),
            pltpu.SemaphoreType.DMA((n_col // 2,)),
            pltpu.SemaphoreType.DMA((inner,)),
            pltpu.SemaphoreType.DMA((outer, inner)),
            pltpu.SemaphoreType.DMA((n_col,)),
            pltpu.SemaphoreType.DMA((iters, 2, n_col - 1)),
            pltpu.SemaphoreType.DMA((iters, 2, n_col)),
            pltpu.SemaphoreType.DMA((iters, inner - 1)),
            pltpu.SemaphoreType.DMA((iters, outer - 1)),
            pltpu.SemaphoreType.DMA((iters, inner)),
            pltpu.SemaphoreType.DMA((iters, outer)),
        ],
        compiler_params=pltpu.CompilerParams(
            collective_id=cid, has_side_effects=True, vmem_limit_bytes=32 * 1024 * 1024),
    )(chunk, pref_row)


def local(embedding, preference):
    rows_n = lax.axis_size("row")
    cols_n = lax.axis_size("col")
    row_idx = lax.axis_index("row")
    col_idx = lax.axis_index("col")
    mol = embedding.shape[2]
    width = embedding.shape[3]
    row_count = mol * cols_n
    col_count = mol * rows_n
    resp, avail = propagate(embedding.reshape(mol, width), preference, rows_n, cols_n, INNER, ITERS, 0)
    return (resp, avail)


def solution(mesh):
    placed = (P("col", "row", None, None), P("row"))
    return jax.shard_map(
        local,
        mesh=mesh,
        in_specs=placed,
        out_specs=(P("row", "col"), P("row", "col")),
        check_vma=False,
    )
```

```python
import functools

import jax
import jax.numpy as jnp
from jax import lax
from jax.experimental import pallas as pl
from jax.experimental.pallas import tpu as pltpu
from jax.sharding import PartitionSpec as P

ITERS = 2


DAMPING = 0.5

INNER = 8

MESH = pl.DeviceIdType.MESH
VMEM = pl.BlockSpec(memory_space=pltpu.VMEM)


def ap_kernel(n_row, n_col, inner, chunk, iters, chunk_ref, prefr_ref, resp_out, avail_out,
              colb3, rowb3, prefc, sim_s, resp_s, avail_s, fcol, scol, cq, pack, buf_f, buf_s, zpart, buf1,
              zsum, buf2, e_send_z, e_send_y, e_send_r, e_send_f, e_recv_c, e_recv_b, e_recv_r,
              send_t, recv_t, send_z, send_y, recv_z, recv_y):
    rows, cols = sim_s.shape
    r = lax.axis_index("row")
    c = lax.axis_index("col")
    outer = n_row // inner
    y = r // inner
    z = r % inner
    cpeers = [lax.rem(c + d, n_col) for d in range(1, n_col)]
    zpeers = [y * inner + lax.rem(z + d, inner) for d in range(1, inner)]
    ypeers = [lax.rem(y + d, outer) * inner + z for d in range(1, outer)]
    g = c * n_row + r
    target_row = g // n_col
    my_slot = g % n_col
    parity = c % 2
    sibling = c + 1 - 2 * parity
    targets = [(target_row, 2 * x + my_slot % 2) for x in range(n_col // 2)]
    sources = []
    for t in range(n_col // 2):
        gs = r * n_col + 2 * t + parity
        sources.append((gs % n_row, gs // n_row))

    def differs(dev):
        return jnp.logical_or(dev[0] != r, dev[1] != c)

    barrier = pltpu.get_barrier_semaphore()
    for p in cpeers:
        pl.semaphore_signal(barrier, inc=1, device_id={"col": p}, device_id_type=MESH)
    for p in zpeers + ypeers:
        pl.semaphore_signal(barrier, inc=1, device_id={"row": p}, device_id_type=MESH)
    for dev in targets + sources:
        @pl.when(differs(dev))
        def _():
            pl.semaphore_signal(barrier, inc=1, device_id=dev, device_id_type=MESH)
    self_in = jnp.logical_and(target_row == r, my_slot % 2 == parity).astype(jnp.int32)
    pltpu.make_async_copy(chunk_ref, colb3.at[r], e_recv_c.at[z]).start()
    prefc[...] = jnp.broadcast_to(prefr_ref[...].reshape(1, rows), (128, rows)).T
    pl.semaphore_wait(barrier, (n_col - 1) + (inner - 1) + (outer - 1) + 2 * (n_col // 2 - self_in))

    copies = []
    for i, p in enumerate(zpeers):
        cp = pltpu.make_async_remote_copy(
            src_ref=chunk_ref, dst_ref=colb3.at[r], send_sem=e_send_z.at[i],
            recv_sem=e_recv_c.at[z], device_id={"row": p}, device_id_type=MESH)
        cp.start()
        copies.append(cp)
    row_copies = []
    for j, dev in enumerate(targets):
        cp = pltpu.make_async_remote_copy(
            src_ref=chunk_ref, dst_ref=rowb3.at[my_slot], send_sem=e_send_r.at[j],
            recv_sem=e_recv_r.at[my_slot], device_id=dev, device_id_type=MESH)
        row_copies.append(cp)

        @pl.when(differs(dev))
        def _():
            cp.start()

        @pl.when(jnp.logical_not(differs(dev)))
        def _():
            pltpu.make_async_copy(chunk_ref, rowb3.at[my_slot], e_recv_r.at[my_slot]).start()

    for d in range(inner):
        zs = lax.rem(z + d, inner)
        slot = colb3.at[y * inner + zs]
        pltpu.make_async_copy(chunk_ref, slot, e_recv_c.at[zs]).wait()
        for i, p in enumerate(ypeers):
            cp = pltpu.make_async_remote_copy(
                src_ref=slot, dst_ref=slot, send_sem=e_send_y.at[d, i],
                recv_sem=e_recv_b.at[y, zs], device_id={"row": p}, device_id_type=MESH)
            cp.start()
            copies.append(cp)
    for t in range(n_col // 2):
        s = 2 * t + parity
        pltpu.make_async_copy(chunk_ref, rowb3.at[s], e_recv_r.at[s]).wait()
        cp = pltpu.make_async_remote_copy(
            src_ref=rowb3.at[s], dst_ref=rowb3.at[s], send_sem=e_send_f.at[t],
            recv_sem=e_recv_r.at[s], device_id={"col": sibling}, device_id_type=MESH)
        cp.start()
        copies.append(cp)
    for t in range(n_col // 2):
        s = 2 * t + 1 - parity
        pltpu.make_async_copy(chunk_ref, rowb3.at[s], e_recv_r.at[s]).wait()
    mol = chunk_ref.shape[0]
    row_start = r * rows
    col_start = c * cols
    colb_ref = colb3
    rowb_ref = rowb3


    def record_top(i0, summed):
        first = jnp.max(summed, axis=1, keepdims=True)
        hits = summed == first
        repeats = jnp.sum(hits.astype(jnp.float32), axis=1, keepdims=True)
        others = jnp.max(jnp.where(hits, -jnp.inf, summed), axis=1, keepdims=True)
        second = jnp.where(repeats > 1.0, first, others)
        fcol[pl.ds(i0, chunk), :] = jnp.broadcast_to(first, (chunk, 128))
        scol[pl.ds(i0, chunk), :] = jnp.broadcast_to(second, (chunk, 128))

    rowb_all = rowb_ref[...].reshape(rows, -1)
    xr = rowb_all.astype(jnp.float32)
    rq_s = fcol
    rq_s[...] = jnp.broadcast_to(jnp.sum(xr * xr, axis=1, keepdims=True), (rows, 128))
    blk = inner * mol
    block_firsts, block_seconds = [], []
    for d in range(outer):
        yo = lax.rem(y + d, outer)
        if d > 0:
            for s in range(inner):
                other = colb3.at[yo * inner + s]
                pltpu.make_async_copy(other, other, e_recv_b.at[yo, s]).wait()
        xb = colb_ref[pl.ds(yo * inner, inner)].reshape(blk, -1)
        xc = xb.astype(jnp.float32)
        qc = jnp.sum(xc * xc, axis=1, keepdims=True)
        cols_at = pl.ds(pl.multiple_of(yo * blk, blk), blk)
        cq[:, cols_at] = jnp.broadcast_to(qc, (blk, 128)).T[0:1, :]
        cross = lax.dot_general(
            rowb_all, xb, (((1,), (1,)), ((), ())), preferred_element_type=jnp.float32)
        sim_s[:, cols_at] = 2.0 * cross - rq_s[:, 0:1] - cq[:, cols_at]
        block_start = col_start + yo * blk

        @pl.when(jnp.logical_and(row_start < block_start + blk, block_start < row_start + rows))
        def _():
            row_ids = row_start + lax.broadcasted_iota(jnp.int32, (rows, blk), 0)
            col_ids = block_start + lax.broadcasted_iota(jnp.int32, (rows, blk), 1)
            sim_s[:, cols_at] = jnp.where(row_ids == col_ids, prefc[:, 0:1], sim_s[:, cols_at])

        summed = sim_s[:, cols_at]
        first = jnp.max(summed, axis=1, keepdims=True)
        hits = summed == first
        repeats = jnp.sum(hits.astype(jnp.float32), axis=1, keepdims=True)
        others = jnp.max(jnp.where(hits, -jnp.inf, summed), axis=1, keepdims=True)
        block_firsts.append(first)
        block_seconds.append(jnp.where(repeats > 1.0, first, others))

    first = functools.reduce(jnp.maximum, block_firsts)
    repeats = functools.reduce(jnp.add, [(f == first).astype(jnp.float32) for f in block_firsts])
    others = functools.reduce(jnp.maximum, [jnp.where(f == first, -jnp.inf, f) for f in block_firsts])
    second = jnp.where(repeats > 1.0, first, jnp.maximum(functools.reduce(jnp.maximum, block_seconds), others))
    fcol[...] = jnp.broadcast_to(first, (rows, 128))
    scol[...] = jnp.broadcast_to(second, (rows, 128))

    has_diag = row_start // cols == c
    band = pl.ds(pl.multiple_of(row_start % cols, rows), rows)

    def eye():
        return lax.broadcasted_iota(jnp.int32, (rows, rows), 0) == lax.broadcasted_iota(jnp.int32, (rows, rows), 1)
    for step in range(iters):
        first_step = step == 0
        last_step = step == iters - 1
        resp_prev, avail_prev = resp_s, avail_s
        resp_new, avail_new = (resp_out, avail_out) if last_step else (resp_s, avail_s)
        pk = pack.at[step]
        pk[0:1, :] = fcol[...].T[0:1, :]
        pk[1:2, :] = scol[...].T[0:1, :]
        for k, dst in enumerate((buf_f.at[step], buf_s.at[step])):
            src = pk.at[pl.ds(k, 1)]
            pltpu.make_async_copy(src, dst.at[pl.ds(c, 1)], recv_t.at[step, k, c]).start()
            for i, p in enumerate(cpeers):
                cp = pltpu.make_async_remote_copy(
                    src_ref=src, dst_ref=dst.at[pl.ds(c, 1)], send_sem=send_t.at[step, k, i],
                    recv_sem=recv_t.at[step, k, c], device_id={"col": p}, device_id_type=MESH)
                cp.start()
                copies.append(cp)
        for k, dst in enumerate((buf_f.at[step], buf_s.at[step])):
            for s in range(n_col):
                pltpu.make_async_copy(pk.at[pl.ds(0, 1)], dst.at[pl.ds(s, 1)], recv_t.at[step, k, s]).wait()
        firsts = buf_f[step]
        seconds = buf_s[step]
        first = jnp.max(firsts, axis=0, keepdims=True)
        at_top = firsts == first
        repeats = jnp.sum(at_top.astype(jnp.float32), axis=0, keepdims=True)
        others = jnp.max(jnp.where(at_top, -jnp.inf, firsts), axis=0, keepdims=True)
        second = jnp.where(repeats > 1.0, first, jnp.maximum(jnp.max(seconds, axis=0, keepdims=True), others))
        fcol[...] = jnp.broadcast_to(first, (128, rows)).T
        scol[...] = jnp.broadcast_to(second, (128, rows)).T

        s = sim_s[...]
        summed = s if first_step else avail_prev[...] + s
        f = fcol[:, 0:1]
        sc = scol[:, 0:1]
        fresh = s - jnp.where(summed == f, sc, f)
        if first_step:
            resp = (1.0 - DAMPING) * fresh
        else:
            resp = DAMPING * resp_prev[...] + (1.0 - DAMPING) * fresh
        resp_new[...] = resp
        zp = zpart.at[step]
        zp[...] = jnp.sum(jnp.maximum(resp, 0.0), axis=0, keepdims=True)

        @pl.when(has_diag)
        def _():
            rb_ = resp_new[:, band]
            zp[:, band] = jnp.sum(jnp.where(eye(), rb_, jnp.maximum(rb_, 0.0)), axis=0, keepdims=True)

        b1 = buf1.at[step]
        pltpu.make_async_copy(zp, b1.at[pl.ds(z, 1)], recv_z.at[step, z]).start()
        for i, p in enumerate(zpeers):
            cp = pltpu.make_async_remote_copy(
                src_ref=zp, dst_ref=b1.at[pl.ds(z, 1)], send_sem=send_z.at[step, i],
                recv_sem=recv_z.at[step, z], device_id={"row": p}, device_id_type=MESH)
            cp.start()
            copies.append(cp)
        for s in range(inner):
            pltpu.make_async_copy(zp, b1.at[pl.ds(s, 1)], recv_z.at[step, s]).wait()
        zs = zsum.at[step]
        zs[...] = jnp.sum(b1[...], axis=0, keepdims=True)
        b2 = buf2.at[step]
        pltpu.make_async_copy(zs, b2.at[pl.ds(y, 1)], recv_y.at[step, y]).start()
        for i, p in enumerate(ypeers):
            cp = pltpu.make_async_remote_copy(
                src_ref=zs, dst_ref=b2.at[pl.ds(y, 1)], send_sem=send_y.at[step, i],
                recv_sem=recv_y.at[step, y], device_id={"row": p}, device_id_type=MESH)
            cp.start()
            copies.append(cp)
        for s in range(outer):
            pltpu.make_async_copy(zs, b2.at[pl.ds(s, 1)], recv_y.at[step, s]).wait()
        colsum = jnp.sum(b2[...], axis=0, keepdims=True)

        cq[...] = colsum
        renew = jnp.minimum(colsum - jnp.maximum(resp_new[...], 0.0), 0.0)
        if first_step:
            avail_new[...] = (1.0 - DAMPING) * renew
        else:
            avail_new[...] = DAMPING * avail_prev[...] + (1.0 - DAMPING) * renew

        @pl.when(has_diag)
        def _():
            rb_ = resp_new[:, band]
            e = eye()
            positive = jnp.where(e, rb_, jnp.maximum(rb_, 0.0))
            renew_b = cq[:, band] - positive
            renew_b = jnp.where(e, renew_b, jnp.minimum(renew_b, 0.0))
            if first_step:
                avail_new[:, band] = (1.0 - DAMPING) * renew_b
            else:
                avail_new[:, band] = DAMPING * avail_prev[:, band] + (1.0 - DAMPING) * renew_b

        if not last_step:
            record_top(0, avail_new[...] + sim_s[...])
    for cp in copies:
        cp.wait_send()
    for j, dev in enumerate(targets):
        @pl.when(differs(dev))
        def _():
            row_copies[j].wait_send()


def propagate(chunk, pref_row, n_row, n_col, inner, iters, cid):
    mol, width = chunk.shape
    rows, cols = mol * n_col, mol * n_row
    outer = n_row // inner
    f32 = jnp.float32
    return pl.pallas_call(
        functools.partial(ap_kernel, n_row, n_col, inner, rows, iters),
        out_shape=(pltpu.VMEM((rows, cols), f32), pltpu.VMEM((rows, cols), f32)),
        in_specs=[VMEM] * 2,
        out_specs=(VMEM, VMEM),
        scratch_shapes=[
            pltpu.VMEM((n_row, mol, width), chunk.dtype),
            pltpu.VMEM((n_col, mol, width), chunk.dtype),
            pltpu.VMEM((rows, 128), f32),
            pltpu.VMEM((rows, cols), f32),
            pltpu.VMEM((rows, cols), f32),
            pltpu.VMEM((rows, cols), f32),
            pltpu.VMEM((rows, 128), f32),
            pltpu.VMEM((rows, 128), f32),
            pltpu.VMEM((1, cols), f32),
            pltpu.VMEM((iters, 2, rows), f32),
            pltpu.VMEM((iters, n_col, rows), f32),
            pltpu.VMEM((iters, n_col, rows), f32),
            pltpu.VMEM((iters, 1, cols), f32),
            pltpu.VMEM((iters, inner, cols), f32),
            pltpu.VMEM((iters, 1, cols), f32),
            pltpu.VMEM((iters, outer, cols), f32),
            pltpu.SemaphoreType.DMA((inner - 1,)),
            pltpu.SemaphoreType.DMA((inner, outer - 1)),
            pltpu.SemaphoreType.DMA((n_col // 2,)),
            pltpu.SemaphoreType.DMA((n_col // 2,)),
            pltpu.SemaphoreType.DMA((inner,)),
            pltpu.SemaphoreType.DMA((outer, inner)),
            pltpu.SemaphoreType.DMA((n_col,)),
            pltpu.SemaphoreType.DMA((iters, 2, n_col - 1)),
            pltpu.SemaphoreType.DMA((iters, 2, n_col)),
            pltpu.SemaphoreType.DMA((iters, inner - 1)),
            pltpu.SemaphoreType.DMA((iters, outer - 1)),
            pltpu.SemaphoreType.DMA((iters, inner)),
            pltpu.SemaphoreType.DMA((iters, outer)),
        ],
        compiler_params=pltpu.CompilerParams(
            collective_id=cid, has_side_effects=True, vmem_limit_bytes=32 * 1024 * 1024),
    )(chunk, pref_row)


def local(embedding, preference):
    rows_n = lax.axis_size("row")
    cols_n = lax.axis_size("col")
    row_idx = lax.axis_index("row")
    col_idx = lax.axis_index("col")
    mol = embedding.shape[2]
    width = embedding.shape[3]
    row_count = mol * cols_n
    col_count = mol * rows_n
    resp, avail = propagate(embedding.reshape(mol, width), preference, rows_n, cols_n, INNER, ITERS, 0)
    return (resp, avail)


def solution(mesh):
    placed = (P("col", "row", None, None), P("row"))
    return jax.shard_map(
        local,
        mesh=mesh,
        in_specs=placed,
        out_specs=(P("row", "col"), P("row", "col")),
        check_vma=False,
    )
```
